32 devices in a mesh: section: 2 (over x), dp: 4 (over z), row: 2 (over y), col: 2 (over core).
Axes of the slice: x: 2, y: 2, z: 4, core: 2. Of those that a mesh axis runs over, the one named last changes fastest.
Arguments:
- latents_in: bfloat16 [4096, 384], P(('dp', 'row'), 'col'), may hold values from -4 to 4
- labels: int32 [16], P(('dp', 'row')), may hold values from 0 to 999
- timesteps: int32 [16], P(('dp', 'row')), may hold values from 0 to 999
- out_grad: bfloat16 [4096, 384], P(('dp', 'row'), 'col'), may hold values from -6 to 6
- label_table: bfloat16 [1000, 384], replicated, may hold values from -6 to 6
- time_table: bfloat16 [1000, 384], replicated, may hold values from -6 to 6
- ada_w: bfloat16 [2, 384, 6, 384], P('section', None, None, 'col'), may hold values from -0.3125 to 0.3125
- ada_b: float32 [2, 6, 384], P('section', None, 'col'), may hold values from -1.5 to 1.5
- qkv_w: bfloat16 [2, 384, 3, 384], P('section', 'col', None, 'row'), may hold values from -0.3125 to 0.3125
- qkv_b: float32 [2, 3, 384], P('section', None, 'row'), may hold values from -1.5 to 1.5
- proj_w: bfloat16 [2, 384, 384], P('section', 'row', 'col'), may hold values from -2.5 to 2.5
- proj_b: float32 [2, 384], P('section', 'col'), may hold values from -1.5 to 1.5
- fc1_w: bfloat16 [2, 384, 1536], P('section', 'col', 'row'), may hold values from -0.3125 to 0.3125
- fc1_b: float32 [2, 1536], P('section', 'row'), may hold values from -1.5 to 1.5
- fc2_w: bfloat16 [2, 1536, 384], P('section', 'row', 'col'), may hold values from -0.15625 to 0.15625
- fc2_b: float32 [2, 384], P('section', 'col'), may hold values from -1.5 to 1.5
Outputs:
- block_outs: bfloat16 [2, 4096, 384], P('section', ('dp', 'row'), 'col')
- input_grads: float32 [2, 4096, 384], P('section', ('dp', 'row'), 'col')
- cond_grad: float32 [16, 384], P(('dp', 'row'))
- label_table_grad: float32 [1000, 384], replicated
- time_table_grad: float32 [1000, 384], replicated
- ada_w_grad: float32 [2, 384, 6, 384], P('section', None, None, 'col')
- ada_b_grad: float32 [2, 6, 384], P('section', None, 'col')
- qkv_w_grad: float32 [2, 384, 3, 384], P('section', 'col', None, 'row')
- qkv_b_grad: float32 [2, 3, 384], P('section', None, 'row')
- proj_w_grad: float32 [2, 384, 384], P('section', 'row', 'col')
- proj_b_grad: float32 [2, 384], P('section', 'col')
- fc1_w_grad: float32 [2, 384, 1536], P('section', 'col', 'row')
- fc1_b_grad: float32 [2, 1536], P('section', 'row')
- fc2_w_grad: float32 [2, 1536, 384], P('section', 'row', 'col')
- fc2_b_grad: float32 [2, 384], P('section', 'col')
The draws below stay inside these ranges and needn't reach their ends.
All inputs are finite; a program needn't handle non-finite values.
Results may differ from the reference program's by a relative error of at most 0.035.
The reference program's roundings to bfloat16 on the way count: a program that leaves them out, or rounds other values in their place, can miss the bound.
Values may be sent and summed in bfloat16 or wider, within the bound.
A program may use at most 128 MiB of HBM per device.

```python
import jax
import jax.numpy as jnp
from jax import lax

D = 384
HEADS = 6
HD = 64
FF = 1536
SEQ = 256
CLASSES = 1000
STEPS = 1000
LATENTS = 16
TOKENS = 4096


def draw_latents_in(key, part):
    base = jax.random.truncated_normal(key, -4.0, 4.0, (TOKENS, D), jnp.float32)
    return base.astype(jnp.bfloat16)


def plant(drawn, rng, low, largest):
    extent = drawn.shape
    index_at = [jax.random.randint(jax.random.fold_in(rng, axis), (), 0, extent[axis]) for axis in range(len(extent))]
    drawn = drawn.at[tuple(index_at)].set(low)
    longest = extent.index(max(extent))
    index_at[longest] = (index_at[longest] + 1) % extent[longest]
    return drawn.at[tuple(index_at)].set(largest)


def levels(key, dims, pieces, smallest, top_value):
    factor_of, own = 1.0, jax.random.fold_in(key, 6)
    for dim, blocks in pieces:
        heights = jnp.exp(jax.random.uniform(jax.random.fold_in(own, dim), (blocks,), jnp.float32, smallest / len(pieces), top_value / len(pieces)))
        factor_of = factor_of * jnp.repeat(heights, dims[dim] // blocks).reshape([-1 if axis == dim else 1 for axis in range(len(dims))])
    return factor_of


def bell_draw(key, dims, scale, limit, cuts=(), dtype=jnp.bfloat16):
    values = jax.random.normal(key, dims, jnp.float32) * scale
    if len(cuts) > 0:
        values = levels(key, dims, cuts, -0.22, 0.18) * values
    return jnp.clip(values, min=-limit, max=limit).astype(dtype)


def setup_inputs(seed: int = 0) -> dict:
    seeds = jax.random.split(jax.random.key(seed), 17)
    latents_in = draw_latents_in(jax.random.fold_in(seeds[16], 71), 0)
    labels = plant(jax.random.randint(seeds[1], (LATENTS,), 0, CLASSES), jax.random.fold_in(seeds[1], 1), 0, CLASSES - 1).astype(jnp.int32)
    timesteps = plant(jax.random.randint(seeds[2], (LATENTS,), 0, STEPS), jax.random.fold_in(seeds[2], 1), 0, STEPS - 1).astype(jnp.int32)
    out_grad = bell_draw(seeds[3], (TOKENS, D), 1.0, 6.0, ((0, 8), (1, 2)))
    label_table = bell_draw(seeds[4], (CLASSES, D), 1.0, 6.0)
    time_table = bell_draw(seeds[5], (STEPS, D), 1.0, 6.0)
    ada_w = bell_draw(seeds[6], (2, D, 6, D), D ** -0.5, 0.3125, ((0, 2), (3, 2)))
    ada_b = bell_draw(seeds[7], (2, 6, D), 0.3, 1.5, ((0, 2), (2, 2)), jnp.float32)
    qkv_w = bell_draw(seeds[8], (2, D, 3, D), D ** -0.5, 0.3125, ((0, 2), (1, 2), (3, 2)))
    qkv_b = bell_draw(seeds[9], (2, 3, D), 0.3, 1.5, ((0, 2), (2, 2)), jnp.float32)
    proj_w = bell_draw(seeds[10], (2, D, D), (4 * D // SEQ) ** -0.5, 2.5, ((0, 2), (1, 2), (2, 2)))
    proj_b = bell_draw(seeds[11], (2, D), 0.3, 1.5, ((0, 2), (1, 2)), jnp.float32)
    fc1_w = bell_draw(seeds[12], (2, D, FF), D ** -0.5, 0.3125, ((0, 2), (1, 2), (2, 2)))
    fc1_b = bell_draw(seeds[13], (2, FF), 0.3, 1.5, ((0, 2), (1, 2)), jnp.float32)
    fc2_w = bell_draw(seeds[14], (2, FF, D), FF ** -0.5, 0.15625, ((0, 2), (1, 2), (2, 2)))
    fc2_b = bell_draw(seeds[15], (2, D), 0.3, 1.5, ((0, 2), (1, 2)), jnp.float32)
    return dict(latents_in=latents_in, labels=labels, timesteps=timesteps, out_grad=out_grad, label_table=label_table, time_table=time_table, ada_w=ada_w, ada_b=ada_b, qkv_w=qkv_w, qkv_b=qkv_b, proj_w=proj_w, proj_b=proj_b, fc1_w=fc1_w, fc1_b=fc1_b, fc2_w=fc2_w, fc2_b=fc2_b)


EPS = 1e-06

def rounded(value):
    return lax.optimization_barrier(value.astype(jnp.bfloat16))

def matmul(left_arr, right_arr):
    return jnp.dot(left_arr, right_arr, preferred_element_type=jnp.float32)

def norm_rows(stream):
    mean_val = lax.optimization_barrier(jnp.mean(stream, axis=-1, keepdims=True))
    variance = lax.optimization_barrier(jnp.mean(jnp.square(stream - mean_val), axis=-1, keepdims=True))
    inv_std = lax.rsqrt(variance + EPS)
    return ((stream - mean_val) * inv_std, inv_std)

def norm_back(grad_norm, normed, inv_std):
    return inv_std * (grad_norm - lax.optimization_barrier(jnp.mean(grad_norm, axis=-1, keepdims=True)) - normed * lax.optimization_barrier(jnp.mean(grad_norm * normed, axis=-1, keepdims=True)))

def gelu_back(pre_act, grad_act):
    return jax.vjp(lambda value: jax.nn.gelu(value, approximate=True), pre_act)[1](grad_act)[0]

def block_forward(stream, modul, params):
    w_qkv, b_qkv, w_proj, b_proj, w_up, b_up, w_down, b_down = params
    scale = 1.0 / HD ** 0.5
    normed1, inv1 = norm_rows(stream)
    hidden1 = (normed1 * (1.0 + modul[1]) + modul[0]).astype(jnp.bfloat16)
    packed = rounded(matmul(hidden1, w_qkv.reshape(D, 3 * D)) + b_qkv.reshape(3 * D))
    parts = packed.reshape(SEQ, 3, HEADS, HD).astype(jnp.float32)
    queries, keys_part, values = (parts[:, 0], parts[:, 1], parts[:, 2])
    scores = jnp.einsum('qhd,khd->hqk', queries, keys_part) * scale
    log_total = jax.nn.logsumexp(scores, axis=-1)
    prob_low = rounded(jnp.exp(scores - log_total[..., None])).astype(jnp.float32)
    attended = jnp.einsum('hqk,khd->qhd', prob_low, values).astype(jnp.bfloat16).reshape(SEQ, D)
    branch_a = matmul(attended, w_proj) + b_proj
    middle = stream + modul[2] * branch_a
    normed2, inv2 = norm_rows(middle)
    hidden2 = (normed2 * (1.0 + modul[4]) + modul[3]).astype(jnp.bfloat16)
    pre_act = matmul(hidden2, w_up) + b_up
    activ = jax.nn.gelu(pre_act, approximate=True).astype(jnp.bfloat16)
    branch_f = matmul(activ, w_down) + b_down
    result = middle + modul[5] * branch_f
    saved = (normed1, inv1, hidden1, packed, log_total, attended, branch_a, normed2, inv2, hidden2, pre_act, activ, branch_f)
    return (result, saved)

def block_backward(grad_out, modul, params, saved):
    w_qkv, b_qkv, w_proj, b_proj, w_up, b_up, w_down, b_down = params
    normed1, inv1, hidden1, packed, log_total, attended, branch_a, normed2, inv2, hidden2, pre_act, activ, branch_f = saved
    scale = 1.0 / HD ** 0.5
    d_gate2 = lax.optimization_barrier(jnp.sum(grad_out * branch_f, axis=0))
    grad_f = (grad_out * modul[5]).astype(jnp.bfloat16)
    g_down = matmul(activ.T, grad_f)
    g_bdown = lax.optimization_barrier(jnp.sum(grad_f.astype(jnp.float32), axis=0))
    grad_act = matmul(grad_f, w_down.T)
    grad_pre = gelu_back(pre_act, grad_act).astype(jnp.bfloat16)
    g_up = matmul(hidden2.T, grad_pre)
    g_bup = lax.optimization_barrier(jnp.sum(grad_pre.astype(jnp.float32), axis=0))
    grad_h2 = matmul(grad_pre, w_up.T)
    d_scale2 = lax.optimization_barrier(jnp.sum(grad_h2 * normed2, axis=0))
    d_shift2 = lax.optimization_barrier(jnp.sum(grad_h2, axis=0))
    grad_mid = grad_out + norm_back(grad_h2 * (1.0 + modul[4]), normed2, inv2)
    d_gate1 = lax.optimization_barrier(jnp.sum(grad_mid * branch_a, axis=0))
    grad_a = (grad_mid * modul[2]).astype(jnp.bfloat16)
    g_proj = matmul(attended.T, grad_a)
    g_bproj = lax.optimization_barrier(jnp.sum(grad_a.astype(jnp.float32), axis=0))
    grad_att = rounded(matmul(grad_a, w_proj.T)).astype(jnp.float32).reshape(SEQ, HEADS, HD)
    parts = packed.reshape(SEQ, 3, HEADS, HD).astype(jnp.float32)
    queries, keys_part, values = (parts[:, 0], parts[:, 1], parts[:, 2])
    scores = jnp.einsum('qhd,khd->hqk', queries, keys_part) * scale
    prob_full = jnp.exp(scores - log_total[..., None])
    prob_low = rounded(prob_full).astype(jnp.float32)
    grad_values = jnp.einsum('hqk,qhd->khd', prob_low, grad_att)
    grad_prob = jnp.einsum('qhd,khd->hqk', grad_att, values)
    delta = lax.optimization_barrier(jnp.sum(prob_full * grad_prob, axis=-1, keepdims=True))
    grad_scores = rounded(prob_full * (grad_prob - delta) * scale).astype(jnp.float32)
    grad_queries = jnp.einsum('hqk,khd->qhd', grad_scores, keys_part)
    grad_keys = jnp.einsum('hqk,qhd->khd', grad_scores, queries)
    grad_packed = jnp.stack([grad_queries, grad_keys, grad_values], axis=1).astype(jnp.bfloat16).reshape(SEQ, 3 * D)
    g_qkv = matmul(hidden1.T, grad_packed).reshape(D, 3, D)
    g_bqkv = lax.optimization_barrier(jnp.sum(grad_packed.astype(jnp.float32), axis=0)).reshape(3, D)
    grad_h1 = matmul(grad_packed, w_qkv.reshape(D, 3 * D).T)
    d_scale1 = lax.optimization_barrier(jnp.sum(grad_h1 * normed1, axis=0))
    d_shift1 = lax.optimization_barrier(jnp.sum(grad_h1, axis=0))
    grad_in = grad_mid + norm_back(grad_h1 * (1.0 + modul[1]), normed1, inv1)
    d_mod = jnp.stack([d_shift1, d_scale1, d_gate1, d_shift2, d_scale2, d_gate2])
    return (grad_in, (g_qkv, g_bqkv, g_proj, g_bproj, g_up, g_bup, g_down, g_bdown), d_mod)

def reference(latents_in, labels, timesteps, out_grad, label_table, time_table, ada_w, ada_b, qkv_w, qkv_b, proj_w, proj_b, fc1_w, fc1_b, fc2_w, fc2_b):
    stacks = (qkv_w, qkv_b, proj_w, proj_b, fc1_w, fc1_b, fc2_w, fc2_b)
    params = [tuple((arr[section_index] for arr in stacks)) for section_index in range(2)]
    ada_flat = [ada_w[section_index].reshape(D, 6 * D) for section_index in range(2)]
    zero_blocks = tuple((tuple((jnp.zeros(arr.shape[1:], jnp.float32) for arr in stacks)) for section_index in range(2)))
    zero_ada = tuple((jnp.zeros((D, 6 * D), jnp.float32) for section_index in range(2)))
    zero_adab = tuple((jnp.zeros((6, D), jnp.float32) for section_index in range(2)))
    carry_init = (zero_blocks, zero_ada, zero_adab, jnp.zeros((CLASSES, D), jnp.float32), jnp.zeros((STEPS, D), jnp.float32))

    def per_latent(carry, item):
        block_grads, ada_grads, adab_grads, label_grad, time_grad = carry
        tokens_in, cotangent, label_id, step_id = item
        cond = label_table[label_id].astype(jnp.float32) + time_table[step_id].astype(jnp.float32)
        silu_low = jax.nn.silu(cond).astype(jnp.bfloat16)
        moduls = [(matmul(silu_low[None, :], ada_flat[section_index])[0] + ada_b[section_index].reshape(6 * D)).reshape(6, D) for section_index in range(2)]
        first_out, first_saved = block_forward(tokens_in.astype(jnp.float32), moduls[0], params[0])
        first_low = rounded(first_out)
        second_out, second_saved = block_forward(first_low.astype(jnp.float32), moduls[1], params[1])
        second_low = second_out.astype(jnp.bfloat16)
        grad_second, grads_second, dmod_second = block_backward(cotangent.astype(jnp.float32), moduls[1], params[1], second_saved)
        grad_first, grads_first, dmod_first = block_backward(grad_second, moduls[0], params[0], first_saved)
        dmods = [dmod_first, dmod_second]
        new_grads = [grads_first, grads_second]
        cond_pull = jnp.zeros((D,), jnp.float32)
        new_ada = []
        new_adab = []
        for section_index in range(2):
            dmod_low = dmods[section_index].astype(jnp.bfloat16).reshape(1, 6 * D)
            new_ada.append(ada_grads[section_index] + matmul(silu_low[:, None], dmod_low))
            new_adab.append(adab_grads[section_index] + dmods[section_index])
            cond_pull = cond_pull + matmul(dmod_low, ada_flat[section_index].T)[0]
        cond_grad = jax.vjp(jax.nn.silu, cond)[1](cond_pull)[0]
        label_grad = label_grad.at[label_id].add(cond_grad)
        time_grad = time_grad.at[step_id].add(cond_grad)
        block_grads = tuple((tuple((left_arr + right_arr for left_arr, right_arr in zip(block_grads[section_index], new_grads[section_index]))) for section_index in range(2)))
        new_carry = (block_grads, tuple(new_ada), tuple(new_adab), label_grad, time_grad)
        return (new_carry, (first_low, second_low, grad_first, grad_second, cond_grad))
    items = (latents_in.reshape(LATENTS, SEQ, D), out_grad.reshape(LATENTS, SEQ, D), labels, timesteps)
    final, outputs = lax.scan(per_latent, carry_init, items)
    block_grads, ada_grads, adab_grads, label_grad, time_grad = final
    first_lows, second_lows, grad_firsts, grad_seconds, cond_grads = outputs
    block_outs = jnp.stack([first_lows.reshape(TOKENS, D), second_lows.reshape(TOKENS, D)])
    input_grads = jnp.stack([grad_firsts.reshape(TOKENS, D), grad_seconds.reshape(TOKENS, D)])
    ada_w_grad = jnp.stack([ada_grads[0].reshape(D, 6, D), ada_grads[1].reshape(D, 6, D)])
    ada_b_grad = jnp.stack([adab_grads[0], adab_grads[1]])
    stacked = [jnp.stack([block_grads[0][index_leaf], block_grads[1][index_leaf]]) for index_leaf in range(8)]
    return (block_outs, input_grads, cond_grads, label_grad, time_grad, ada_w_grad, ada_b_grad, stacked[0], stacked[1], stacked[2], stacked[3], stacked[4], stacked[5], stacked[6], stacked[7])
```

```python
import functools
import math

import jax
import jax.numpy as jnp
from jax import lax
from jax.experimental import pallas as pl
from jax.experimental.pallas import tpu as pltpu
from jax.sharding import PartitionSpec as P

D = 384
HALF = D // 2
HD = 64
FF = 1536
FFH = FF // 2
SEQ = 256
EPS = 1e-06
SCALE = 1.0 / math.sqrt(HD)
SOFT = SCALE * math.log2(math.e)
MESH = pl.DeviceIdType.MESH
F32 = jnp.float32
BF16 = jnp.bfloat16

ROWS_A, ROWS_B, ROWS_T = 4 * HALF, 5 * HALF, 6 * HALF
GROWS = ROWS_T + 16
CHUNKS = ((0, 192), (192, 192), (384, 192), (576, 192), (768, 192), (960, 208))
READY_DOWN, READY_UP = 2, 4
PIECES = 6
STRIP = HALF // 2


def dot(a, b):
    return jnp.dot(a, b, preferred_element_type=F32)


def dot_nt(a, b):
    return lax.dot_general(a, b, (((1,), (1,)), ((), ())), preferred_element_type=F32)


def dot_tn(a, b):
    return lax.dot_general(a, b, (((0,), (0,)), ((), ())), preferred_element_type=F32)


def norm_rows(v):
    mean_val = jnp.mean(v, axis=-1, keepdims=True)
    cen = v - mean_val
    inv = lax.rsqrt(jnp.mean(cen * cen, axis=-1, keepdims=True) + EPS)
    return cen * inv, inv


def norm_back(g, normed, inv):
    return inv * (
        g
        - jnp.mean(g, axis=-1, keepdims=True)
        - normed * jnp.mean(g * normed, axis=-1, keepdims=True)
    )


C0 = math.sqrt(2.0 / math.pi)
C1 = 0.044715 * C0


def gelu_and_slope(v):
    u = v * v
    p = 0.5 + 0.5 * jnp.tanh(v * (C0 + C1 * u))
    act = v * p
    return act, p + act * (1.0 - p) * (2.0 * C0 + (6.0 * C1) * u)


def col_sum(v):
    return jnp.sum(v.astype(F32), axis=0, keepdims=True)


def flipped(index, step):
    return index + step * (1 - 2 * lax.rem(index // step, 2))


def align(index, size):
    return pl.multiple_of(index * size, size)


class Wires:
    def __init__(self, send_sem, recv_sem):
        self.send_sem, self.recv_sem = send_sem, recv_sem
        self.number, self.started = {}, []

    def index(self, name):
        return self.number.setdefault(name, len(self.number))

    def copy(self, name, src, dst, where):
        k = self.index(name)
        return pltpu.make_async_remote_copy(
            src_ref=src,
            dst_ref=dst,
            send_sem=self.send_sem.at[k],
            recv_sem=self.recv_sem.at[k],
            device_id=where,
            device_id_type=MESH,
        )

    def send(self, name, src, dst, where):
        self.copy(name, src, dst, where).start()
        self.started.append((lambda: self.copy(name, src, dst, where), None))

    def send_if(self, cond, make):
        pl.when(cond)(lambda: make().start())
        self.started.append((make, cond))

    def arrived(self, name, dst, where):
        self.copy(name, dst, dst, where).wait_recv()

    def finish(self):
        for make, cond in self.started:

            def wait(make=make):
                make().wait_send()

            if cond is None:
                wait()
            else:
                pl.when(cond)(wait)


def main_kernel(
    bits, dp,
    lat, labels, times, cot, ltab, ttab, ada, adab, qkv, qb, proj, pb, fc1, b1, fc2, b2,
    res, block_out, input_grad, cond_grad, dm16, silu16, adab_sum, g3, ids,
    xr, cr, modbuf, mod, ball, sh, wa, wb, wp, w1, w2, xf, gof, x2, g2, obuf, gbuf,
    normed1, normed2, branch_a, branch_f, hidden1, hidden2, packed, prob, attended, act, slope,
    grad_mid, gatt, gpack, outt, gint, gp, rc, t1, own1, rr, t2, zz, dmod, dm, pull, table, condb, silub, biasg,
    send_sem, recv_sem, local_sem,
):
    r, c, z = lax.axis_index("row"), lax.axis_index("col"), lax.axis_index("dp")
    sec = lax.axis_index("section")
    h = lax.rem(z, 2)
    to_col, to_row, to_sec = {"col": 1 - c}, {"row": 1 - r}, {"section": 1 - sec}
    to_dp = [{"dp": flipped(z, 1 << j)} for j in range(bits)]
    middle_at = dp // 2
    left = jnp.where(z < middle_at, 1, 0)
    outer = jnp.logical_or(z == 0, z == dp - 1)
    inner = jnp.logical_or(z == middle_at - 1, z == middle_at)
    to_in = {"dp": z + 2 * left - 1}
    to_out = {"dp": jnp.where(outer, dp - 1 - z, z + 1 - 2 * left)}
    not_outer, not_inner = jnp.logical_not(outer), jnp.logical_not(inner)
    first, second = sec == 0, sec == 1

    barrier = pltpu.get_barrier_semaphore()
    greeted = [to_col, to_row, to_sec, *to_dp, to_in, to_out]
    for where in greeted:
        pl.semaphore_signal(barrier, inc=1, device_id=where, device_id_type=MESH)

    sh[0, :, :HALF] = qkv[0]
    sh[0, :, HALF:] = qkv[1]
    sh[1, :, :HALF] = qkv[2]
    sh[1, :, HALF:] = proj[...]
    own_bias = 2 * r + c
    ball[own_bias] = jnp.zeros((8, D), F32)
    ball[own_bias, 0:1, :HALF] = qb[0]
    ball[own_bias, 0:1, HALF:] = qb[1]
    ball[own_bias, 1:2, :HALF] = qb[2]
    ball[own_bias, 1:2, HALF:] = pb[...]
    ball[own_bias, 2:3, :] = b1[:, :D]
    ball[own_bias, 3:4, :] = b1[:, D:]
    ball[own_bias, 4:5, :HALF] = b2[...]

    pl.semaphore_wait(barrier, len(greeted))
    wires = Wires(send_sem, recv_sem)

    def source(i, at, size):
        rows = pl.ds(at, size)
        if i < 2:
            return sh.at[i, rows]
        lanes = pl.ds((i % 2) * D, D)
        return (fc1 if i < 4 else fc2).at[rows, lanes]

    def place(i, pr, pc, at, size):
        rows = pl.ds(pl.multiple_of(pc * HALF + at, 16), size)
        if i < 2:
            return (wa, wb)[i].at[pr, rows]
        lanes = pl.ds(pl.multiple_of(pr * FFH + (i % 2) * D, 128), D)
        return (w1 if i < 4 else w2).at[rows, lanes]

    def strip(half):
        return pl.multiple_of(half * STRIP, 16)

    for i in range(PIECES):
        wires.send(("y", i), source(i, strip(h), STRIP), place(i, r, c, strip(h), STRIP), to_row)
        if i == 0:
            own_lanes = pl.ds(align(c, SEQ), SEQ)
            their_lanes = pl.ds(align(1 - c, SEQ), SEQ)
            wires.send("x", lat.at[:, their_lanes], xr.at[c], to_col)
            wires.send("own0", source(0, 0, HALF), place(0, r, c, 0, HALF), to_col)
            wires.send("bias col", ball.at[own_bias], ball.at[own_bias], to_col)
            wires.send("bias row", ball.at[own_bias], ball.at[own_bias], to_row)
    wires.send("cot", cot.at[:, their_lanes], cr.at[c], to_col)
    for i in range(1, PIECES):
        wires.send(("own", i), source(i, 0, HALF), place(i, r, c, 0, HALF), to_col)
    local = []
    for i in range(PIECES):
        copy = pltpu.make_async_copy(source(i, 0, HALF), place(i, r, c, 0, HALF), local_sem.at[i])
        copy.start()
        local.append(copy)

    def hot(ids_ref, table_ref):
        wide = (2, table_ref.shape[0])
        wanted = jnp.where(lax.broadcasted_iota(jnp.int32, wide, 0) == 0, ids_ref[0], ids_ref[1])
        return dot(jnp.where(lax.broadcasted_iota(jnp.int32, wide, 1) == wanted, 1.0, 0.0).astype(BF16), table_ref[...])

    cond = hot(labels, ltab) + hot(times, ttab)
    condb[...] = cond
    silu_low = (cond / (1.0 + jnp.exp(-cond))).astype(BF16)
    silub[...] = silu_low.astype(F32)
    modbuf[0:2] = jnp.zeros((2, 8, HALF), F32)
    for i in range(6):
        part = dot_nt(silu_low, ada[i]) + adab[i]
        for latent in range(2):
            modbuf[latent, i : i + 1, :] = part[latent : latent + 1, :]
    wires.send("mod", modbuf.at[1 - c], modbuf.at[2 + c], to_col)
    modbuf[2 + c] = modbuf[c]

    def y_step(i):
        wires.arrived(("y", i), place(i, 1 - r, c, strip(h), STRIP), to_row)
        here = place(i, 1 - r, c, strip(h), STRIP)
        wires.copy(("z", i), here, here, to_dp[0]).start()
        wires.copy(("fy", i), here, here, to_col).start()

    def z_step(i):
        here = place(i, 1 - r, c, strip(1 - h), STRIP)
        wires.arrived(("z", i), here, to_dp[0])
        wires.copy(("fz", i), here, here, to_col).start()

    def ready(i):
        wires.arrived("own0" if i == 0 else ("own", i), place(i, r, 1 - c, 0, HALF), to_col)
        wires.arrived(("fy", i), place(i, 1 - r, 1 - c, strip(h), STRIP), to_col)
        wires.arrived(("fz", i), place(i, 1 - r, 1 - c, strip(1 - h), STRIP), to_col)

    order = [("y", 0), ("y", 1), ("z", 0), ("y", 2), ("z", 1), ("y", 3), ("z", 2), ("y", 4), ("z", 3), ("y", 5), ("z", 4), ("z", 5)]

    def do(steps):
        for kind, i in steps:
            (y_step if kind == "y" else z_step)(i)

    xr[c] = lat[:, own_lanes]
    cr[c] = cot[:, own_lanes]
    for copy in local:
        copy.wait()
    wires.arrived("x", xr.at[1 - c], to_col)
    wires.arrived("mod", modbuf.at[2 + 1 - c], to_col)
    for half in range(2):
        mod[:, half * HALF : (half + 1) * HALF] = modbuf[2 + half]
    wires.arrived("bias col", ball.at[2 * r + 1 - c], to_col)
    wires.arrived("bias row", ball.at[2 * (1 - r) + c], to_row)
    wires.arrived("cot", cr.at[1 - c], to_col)
    do(order[:3])

    @pl.when(first)
    def _():
        xf[...] = jnp.concatenate([xr[0].astype(F32).T, xr[1].astype(F32).T], axis=1)

    @pl.when(second)
    def _():
        gof[...] = jnp.concatenate([cr[0].astype(F32).T, cr[1].astype(F32).T], axis=1)

    do(order[3:5])

    @pl.when(second)
    def _():
        do(order[5:])
        for i in range(PIECES):
            ready(i)
        for part in range(2):
            rows = pl.ds(part * 128, 128)
            wires.arrived(("fwd", part), x2.at[rows], to_sec)
        xf[...] = x2[...].astype(F32)


    def on_first(steps, items):
        @pl.when(first)
        def _():
            do(steps)
            for i in items:
                ready(i)

    m = [mod[i : i + 1, :] for i in range(6)]
    n1, inv1 = norm_rows(xf[...])
    normed1[...] = n1
    hidden1[...] = (n1 * (1.0 + m[1]) + m[0]).astype(BF16)

    on_first([], [0])
    hid = hidden1[...]
    for q in range(2):
        bias = ball[2 * q + c, 0:1, :]
        packed[:, q * D : (q + 1) * D] = (dot(hid, wa[q]) + bias).astype(BF16)
    on_first(order[5:6], [1])
    for q in range(2):
        bias = ball[2 * q + c, 1:2, :HALF]
        at = 2 * D + q * HALF
        packed[:, at : at + HALF] = (dot(hid, wb[q, :, :HALF]) + bias).astype(BF16)
        for half in range(2):
            wp[q * HALF : (q + 1) * HALF, half * HALF : (half + 1) * HALF] = wb[q, half * HALF : (half + 1) * HALF, HALF:]

    def qkv_of(head):
        q, j = head // 3, head % 3
        at = q * D + j * HD
        vat = 2 * D + head * HD
        return packed[:, at : at + HD], packed[:, at + HALF : at + HALF + HD], packed[:, vat : vat + HD]

    later = {0: order[6:7], 1: order[7:8], 2: order[8:9], 3: order[9:10], 4: order[10:11]}
    heads = []
    for head in range(6):
        q, k, v = qkv_of(head)
        s = dot_nt(q, k)
        e = jnp.exp2((s - jnp.max(s, axis=-1, keepdims=True)) * SOFT)
        p = e * (1.0 / jnp.sum(e, axis=-1, keepdims=True))
        prob[head] = p
        attended[:, head * HD : (head + 1) * HD] = dot(p.astype(BF16), v).astype(BF16)
        if head in later:
            on_first(later[head], [])
    ba = dot(attended[...], wp[...]) + jnp.concatenate([ball[2 * r, 1:2, HALF:], ball[2 * r + 1, 1:2, HALF:]], axis=1)
    branch_a[...] = ba
    middle = xf[...] + m[2] * ba
    n2, inv2 = norm_rows(middle)
    normed2[...] = n2
    hidden2[...] = (n2 * (1.0 + m[4]) + m[3]).astype(BF16)
    on_first(order[11:], [2, 3])
    for q in range(2):
        bias = jnp.concatenate([ball[2 * q + c, 2:3, :], ball[2 * q + c, 3:4, :]], axis=1)
        lanes = slice(q * FFH, (q + 1) * FFH)
        a, sl = gelu_and_slope(dot(hidden2[...], w1[:, lanes]) + bias)
        act[:, lanes] = a.astype(BF16)
        slope[:, lanes] = sl
    on_first([], [4, 5])
    down_bias = jnp.concatenate([ball[2 * r, 4:5, :HALF], ball[2 * r + 1, 4:5, :HALF]], axis=1)
    for part in range(2):
        rows = slice(part * 128, (part + 1) * 128)
        bf = dot_nt(act[rows, :], w2[...]) + down_bias
        branch_f[rows, :] = bf
        obuf[rows, :] = (middle[rows, :] + m[5] * bf).astype(BF16)

        @pl.when(first)
        def _():
            there = pl.ds(part * 128, 128)
            wires.copy(("fwd", part), obuf.at[there], x2.at[there], to_sec).start()

    outt[...] = obuf[...].astype(F32).T.astype(BF16)
    own_feats = pl.ds(align(c, HALF), HALF)
    their_feats = pl.ds(align(1 - c, HALF), HALF)
    wires.send("out", outt.at[their_feats], block_out.at[:, own_lanes], to_col)
    block_out[:, own_lanes] = outt[own_feats, :]

    @pl.when(first)
    def _():
        for part in range(2):
            wires.arrived(("bwd", part), g2.at[pl.ds(part * 128, 128)], to_sec)
        gof[...] = g2[...].astype(F32)

    def col_names(k):
        at, size = CHUNKS[k]
        return pl.ds(at, size)

    def send_col(k):
        rows = col_names(k)
        wires.send(("c0", k), gp.at[1 - r, 1 - c, rows], rc.at[1 - r, rows], to_col)
        wires.send(("c1", k), gp.at[r, 1 - c, rows], rc.at[r, rows], to_col)

    def total(a, b):
        return (a.astype(F32) + b.astype(F32)).astype(BF16)

    def from_col(k):
        rows = col_names(k)
        wires.arrived(("c0", k), rc.at[1 - r, rows], to_col)
        t1[rows, :] = total(gp[1 - r, c, rows, :], rc[1 - r, rows, :])
        wires.send(("r", k), t1.at[rows], rr.at[rows], to_row)
        wires.arrived(("c1", k), rc.at[r, rows], to_col)
        own1[rows, :] = total(gp[r, c, rows, :], rc[r, rows, :])

    slot = jnp.where(inner, 1, 0)
    zname = {0: "zi", 1: "zm"}

    def send_in(k, cond):
        rows = col_names(k)
        for kind in range(2):
            say = jnp.logical_and(cond, inner if kind else not_inner)

            def make(kind=kind):
                return wires.copy((zname[kind], k), t2.at[rows], zz.at[kind, rows], to_in)

            wires.send_if(say, make)

    def from_row(k):
        rows = col_names(k)
        wires.arrived(("r", k), rr.at[rows], to_row)
        t2[rows, :] = total(own1[rows, :], rr[rows, :])
        send_in(k, outer)

    def fold(k):
        rows = col_names(k)

        @pl.when(not_outer)
        def _():
            wires.arrived(("zi", k), zz.at[0, rows], to_out)
            t2[rows, :] = total(t2[rows, :], zz[0, rows, :])

        send_in(k, not_outer)

    def finish(k):
        rows = col_names(k)

        @pl.when(inner)
        def _():
            wires.arrived(("zm", k), zz.at[1, rows], to_in)
            res[rows, :] = total(t2[rows, :], zz[1, rows, :])

        @pl.when(not_inner)
        def _():
            wires.arrived(("zo", k), res.at[rows], to_in)

        wires.send_if(not_outer, lambda: wires.copy(("zo", k), res.at[rows], res.at[rows], to_out))

    grad_out = gof[...]
    grad_f = (grad_out * m[5]).astype(BF16)
    ga = dot(grad_f, w2[...])
    grad_pre = (ga * slope[...]).astype(BF16)
    gd = dot_tn(grad_f, act[...]).astype(BF16)
    for q in range(2):
        for half in range(2):
            for k in range(2):
                at = q * FFH + k * D
                gp[q, half, k * HALF : (k + 1) * HALF, :] = gd[half * HALF : (half + 1) * HALF, at : at + D]
    for k in range(READY_DOWN):
        send_col(k)
    gu = dot_tn(hidden2[...], grad_pre).astype(BF16)
    for q in range(2):
        for half in range(2):
            for k in range(2):
                at = q * FFH + k * D
                gp[q, half, (2 + k) * HALF : (3 + k) * HALF, :] = gu[half * HALF : (half + 1) * HALF, at : at + D]
    for k in range(READY_DOWN, READY_UP):
        send_col(k)
    dmod[5:6, :] = col_sum(grad_out * branch_f[...])
    biasg[0:1, :D] = col_sum(grad_f)
    biasg[1:2, :] = col_sum(grad_pre)
    grad_h2 = dot_nt(grad_pre, w1[...])
    for k in range(READY_DOWN):
        from_col(k)
    n2 = normed2[...]
    dmod[4:5, :] = col_sum(grad_h2 * n2)
    dmod[3:4, :] = col_sum(grad_h2)
    gm = grad_out + norm_back(grad_h2 * (1.0 + m[4]), n2, inv2)
    grad_mid[...] = gm
    grad_a = (gm * m[2]).astype(BF16)
    dmod[2:3, :] = col_sum(gm * branch_a[...])
    biasg[2:3, :D] = col_sum(grad_a)
    gatt[...] = dot_nt(grad_a, wp[...]).astype(BF16)
    for k in range(READY_DOWN, READY_UP):
        from_col(k)
    gproj = dot_tn(attended[...], grad_a).astype(BF16)
    for q in range(2):
        for half in range(2):
            gp[q, half, ROWS_B:ROWS_T, HALF:] = gproj[q * HALF : (q + 1) * HALF, half * HALF : (half + 1) * HALF]
    for head in range(6):
        q, k, v = qkv_of(head)
        p = prob[head]
        g = gatt[:, head * HD : (head + 1) * HD]
        grad_prob = dot_nt(g, v)
        delta = jnp.sum(p * grad_prob, axis=-1, keepdims=True)
        gs = (p * (grad_prob - delta) * SCALE).astype(BF16)
        at = (head // 3) * D + (head % 3) * HD
        vat = 2 * D + head * HD
        gpack[:, at : at + HD] = dot(gs, k).astype(BF16)
        gpack[:, at + HALF : at + HALF + HD] = dot_tn(gs, q).astype(BF16)
        gpack[:, vat : vat + HD] = dot_tn(p.astype(BF16), g).astype(BF16)
    n1 = normed1[...]
    grad_h1 = dot_nt(gpack[:, :D], wa[0]) + dot_nt(gpack[:, D : 2 * D], wa[1])
    grad_h1 += dot_nt(gpack[:, 2 * D : 2 * D + HALF], wb[0, :, :HALF])
    grad_h1 += dot_nt(gpack[:, 2 * D + HALF :], wb[1, :, :HALF])
    gi = grad_mid[...] + norm_back(grad_h1 * (1.0 + m[1]), n1, inv1)
    gbuf[...] = gi.astype(BF16)

    @pl.when(second)
    def _():
        for part in range(2):
            there = pl.ds(part * 128, 128)
            wires.copy(("bwd", part), gbuf.at[there], g2.at[there], to_sec).start()

    gq = dot_tn(hidden1[...], gpack[...]).astype(BF16)
    for q in range(2):
        for half in range(2):
            rows = slice(half * HALF, (half + 1) * HALF)
            gp[q, half, ROWS_A:ROWS_B, :] = gq[rows, q * D : (q + 1) * D]
            gp[q, half, ROWS_B:ROWS_T, :HALF] = gq[rows, 2 * D + q * HALF : 2 * D + (q + 1) * HALF]
    bq = col_sum(gpack[...])
    zero = jnp.zeros((1, HALF), F32)
    for q in range(2):
        for half in range(2):
            feats = slice(half * HALF, (half + 1) * HALF)
            tail = [
                bq[:, q * D : (q + 1) * D],
                jnp.concatenate([bq[:, 2 * D + q * HALF : 2 * D + (q + 1) * HALF], biasg[2:3, feats]], axis=1),
                biasg[1:2, q * FFH : q * FFH + D],
                biasg[1:2, q * FFH + D : (q + 1) * FFH],
                jnp.concatenate([biasg[0:1, feats], zero], axis=1),
                jnp.zeros((11, D), F32),
            ]
            gp[q, half, ROWS_T:GROWS, :] = jnp.concatenate(tail, axis=0).astype(BF16)
    for k in range(READY_UP, len(CHUNKS)):
        send_col(k)
    dmod[1:2, :] = col_sum(grad_h1 * n1)
    dmod[0:1, :] = col_sum(grad_h1)
    for half in range(2):
        dm[2 + half, 0:6, :] = dmod[0:6, half * HALF : (half + 1) * HALF]
        dm[2 + half, 6:8, :] = jnp.zeros((2, HALF), F32)
    wires.send("dm", dm.at[2 + 1 - c], dm.at[c], to_col)
    gint[...] = gi.T
    wires.send("gin", gint.at[their_feats], input_grad.at[:, own_lanes], to_col)
    input_grad[:, own_lanes] = gint[own_feats, :]

    me = 2 * z + r
    own = 2

    def pull_part():
        wires.arrived("dm", dm.at[1 - c], to_col)
        dm[c] = dm[2 + c]
        part = jnp.zeros((2, D), F32)
        for i in range(6):
            low = jnp.concatenate([dm[0, i : i + 1, :], dm[1, i : i + 1, :]], axis=0).astype(BF16)
            part += dot(low, ada[i])
        pull[0] = jnp.concatenate([part, jnp.zeros((6, D), F32)], axis=0)
        wires.send("p0", pull.at[0], pull.at[1], to_col)

    def pull_section():
        wires.arrived("p0", pull.at[1], to_col)
        pull[2] = pull[0] + pull[1]
        wires.send("p1", pull.at[2], pull.at[3], to_sec)

    def fill_table():
        wires.arrived("p1", pull.at[3], to_sec)
        v = condb[...]
        sig = 1.0 / (1.0 + jnp.exp(-v))
        grad = (pull[2, 0:2, :] + pull[3, 0:2, :]) * (sig * (1.0 + v * (1.0 - sig)))
        cond_grad[...] = grad

        def ids_of(ref):
            wanted = jnp.where(lax.broadcasted_iota(jnp.int32, (2, D), 0) == 0, ref[0], ref[1])
            return wanted.astype(F32)

        table[me, 0:8, :] = jnp.concatenate([grad, silub[...], ids_of(labels), ids_of(times)], axis=0)
        table[me, 8:16, :] = jnp.concatenate([dm[0], dm[1]], axis=1)

    def share_table(j):
        size = 1 << j
        block = pl.ds((me // size) * size, size)
        if j > 0:
            low = size // 2
            other = pl.ds(flipped(me // low, 1) * low, low)
            wires.arrived(("t", j - 1), table.at[other], to_row if j == 1 else to_dp[j - 2])
        if j <= bits:
            wires.send(("t", j), table.at[block], table.at[block], to_row if j == 0 else to_dp[j - 1])

    def spread_table():
        places = table.shape[0]
        rows8 = [table[i, 0:8, :] for i in range(places)]
        grads = jnp.concatenate([v[0:2] for v in rows8], axis=0)
        silus = jnp.concatenate([v[2:4] for v in rows8], axis=0)
        high = grads.astype(BF16)
        rest = grads - high.astype(F32)
        mid = rest.astype(BF16)
        g3[...] = jnp.concatenate([high.astype(F32), mid.astype(F32), rest - mid.astype(F32)], axis=0).astype(BF16)
        silu16[...] = silus.astype(BF16)
        for which in range(2):
            ids[which] = jnp.concatenate([v[4 + 2 * which : 6 + 2 * which] for v in rows8], axis=0)
        summed = jnp.zeros((8, D), F32)
        for i in range(places):
            summed += table[i, 8:16, :]
        for i in range(6):
            adab_sum[i] = summed[i : i + 1, :HALF] + summed[i : i + 1, HALF:]
            parts = []
            for p in range(places):
                row = table[p, 8 + i : 9 + i, :]
                parts += [row[:, :HALF], row[:, HALF:]]
            dm16[i] = jnp.concatenate(parts, axis=0).astype(BF16)

    small = [pull_part, pull_section, fill_table]
    small += [functools.partial(share_table, j) for j in range(bits + 2)] + [spread_table]
    count = len(CHUNKS)
    late = count - READY_UP
    for tick in range(max(count + 4, len(small))):
        if tick < late:
            from_col(READY_UP + tick)
        for lag, step in ((0, from_row), (2, fold), (4, finish)):
            if 0 <= tick - lag < count:
                step(tick - lag)
        if tick < len(small):
            small[tick]()
    wires.arrived("out", block_out.at[:, their_lanes], to_col)
    wires.arrived("gin", input_grad.at[:, their_lanes], to_col)
    wires.finish()
    for i in range(PIECES):
        near = place(i, 1 - r, c, strip(h), STRIP)
        far = place(i, 1 - r, c, strip(1 - h), STRIP)
        wires.copy(("z", i), near, near, to_dp[0]).wait_send()
        wires.copy(("fy", i), near, near, to_col).wait_send()
        wires.copy(("fz", i), far, far, to_col).wait_send()

    @pl.when(first)
    def _():
        for part in range(2):
            there = pl.ds(part * 128, 128)
            wires.copy(("fwd", part), obuf.at[there], x2.at[there], to_sec).wait_send()

    @pl.when(second)
    def _():
        for part in range(2):
            there = pl.ds(part * 128, 128)
            wires.copy(("bwd", part), gbuf.at[there], g2.at[there], to_sec).wait_send()


def last_kernel(
    res, block_in, grad_in, cond_in, dm16, silu16, adab_in, g3, ids,
    block_out, input_grad, cond_out, g_label, g_time, g_ada, g_adab, g_qkv, g_qb, g_proj, g_pb, g_fc1, g_b1, g_fc2, g_b2,
):
    count = g3.shape[0] // 3
    for which, out in ((0, g_label), (1, g_time)):
        one = ids[which][:, :1]
        wide = (count, out.shape[0])
        hot = jnp.where(lax.broadcasted_iota(jnp.int32, wide, 1).astype(F32) == one, 1.0, 0.0).astype(BF16)
        out[...] = dot_tn(jnp.concatenate([hot, hot, hot], axis=0), g3[...])
    for i in range(6):
        g_ada[i] = dot_tn(dm16[i], silu16[...])
    block_out[...] = block_in[...]
    input_grad[...] = grad_in[...]
    cond_out[...] = cond_in[...]
    g_adab[...] = adab_in[...]
    for k in range(2):
        g_fc2[:, k * D : (k + 1) * D] = res[k * HALF : (k + 1) * HALF, :].astype(F32)
        g_fc1[:, k * D : (k + 1) * D] = res[(2 + k) * HALF : (3 + k) * HALF, :].astype(F32)
    low = res[ROWS_A:ROWS_B, :].astype(F32)
    g_qkv[0] = low[:, :HALF]
    g_qkv[1] = low[:, HALF:]
    low = res[ROWS_B:ROWS_T, :].astype(F32)
    g_qkv[2] = low[:, :HALF]
    g_proj[...] = low[:, HALF:]
    tail = res[ROWS_T:GROWS, :].astype(F32)
    g_qb[0] = tail[0:1, :HALF]
    g_qb[1] = tail[0:1, HALF:]
    g_qb[2] = tail[1:2, :HALF]
    g_pb[...] = tail[1:2, HALF:]
    g_b1[:, :D] = tail[2:3, :]
    g_b1[:, D:] = tail[3:4, :]
    g_b2[...] = tail[4:5, :HALF]


def on_device(
    latents_in, labels, timesteps, out_grad, label_table, time_table, ada_w, ada_b,
    qkv_w, qkv_b, proj_w, proj_b, fc1_w, fc1_b, fc2_w, fc2_b,
):
    own = latents_in.shape[0] // SEQ
    dp = lax.axis_size("dp")
    places = dp * lax.axis_size("row")
    bits = dp.bit_length() - 1
    latents = places * own
    vmem, smem = pl.BlockSpec(memory_space=pltpu.VMEM), pl.BlockSpec(memory_space=pltpu.SMEM)
    args = (
        latents_in.T,
        labels,
        timesteps,
        out_grad.T,
        label_table,
        time_table,
        jnp.transpose(ada_w[0], (1, 2, 0)),
        jnp.transpose(ada_b, (1, 0, 2)),
        jnp.transpose(qkv_w[0], (1, 0, 2)),
        jnp.transpose(qkv_b, (1, 0, 2)),
        proj_w[0],
        proj_b,
        fc1_w[0],
        fc1_b,
        fc2_w[0].T,
        fc2_b,
    )
    outs = [
        ((GROWS, D), BF16),
        ((HALF, own * SEQ), BF16),
        ((HALF, own * SEQ), F32),
        ((own, D), F32),
        ((6, latents, HALF), BF16),
        ((latents, D), BF16),
        ((6, 1, HALF), F32),
        ((3 * latents, D), BF16),
        ((2, latents, D), F32),
    ]
    scratch = [
        ((2, HALF, SEQ), BF16),
        ((2, HALF, SEQ), BF16),
        ((4, 8, HALF), F32),
        ((8, D), F32),
        ((4, 8, D), F32),
        ((2, HALF, D), BF16),
        ((2, D, D), BF16),
        ((2, D, D), BF16),
        ((D, D), BF16),
        ((D, FF), BF16),
        ((D, FF), BF16),
        ((SEQ, D), F32),
        ((SEQ, D), F32),
        ((SEQ, D), BF16),
        ((SEQ, D), BF16),
        ((SEQ, D), BF16),
        ((SEQ, D), BF16),
        ((SEQ, D), F32),
        ((SEQ, D), F32),
        ((SEQ, D), F32),
        ((SEQ, D), F32),
        ((SEQ, D), BF16),
        ((SEQ, D), BF16),
        ((SEQ, 3 * D), BF16),
        ((6, SEQ, SEQ), F32),
        ((SEQ, D), BF16),
        ((SEQ, FF), BF16),
        ((SEQ, FF), F32),
        ((SEQ, D), F32),
        ((SEQ, D), BF16),
        ((SEQ, 3 * D), BF16),
        ((D, SEQ), BF16),
        ((D, SEQ), F32),
        ((2, 2, GROWS, D), BF16),
        ((2, GROWS, D), BF16),
        ((GROWS, D), BF16),
        ((GROWS, D), BF16),
        ((GROWS, D), BF16),
        ((GROWS, D), BF16),
        ((2, GROWS, D), BF16),
        ((8, D), F32),
        ((4, 8, HALF), F32),
        ((4, 8, D), F32),
        ((places, 16, D), F32),
        ((own, D), F32),
        ((own, D), F32),
        ((8, FF), F32),
    ]
    wires = 4 * PIECES + 8 + 8 * len(CHUNKS) + 12 + bits
    made = pl.pallas_call(
        functools.partial(main_kernel, bits, dp),
        out_shape=[jax.ShapeDtypeStruct(s, d) for s, d in outs],
        in_specs=[smem if i in (1, 2) else vmem for i in range(len(args))],
        out_specs=[vmem] * len(outs),
        scratch_shapes=[pltpu.VMEM(s, d) for s, d in scratch]
        + [pltpu.SemaphoreType.DMA((wires,)), pltpu.SemaphoreType.DMA((wires,)), pltpu.SemaphoreType.DMA((PIECES,))],
        compiler_params=pltpu.CompilerParams(
            vmem_limit_bytes=56 * 1024 * 1024, collective_id=0, has_side_effects=True
        ),
    )(*args)
    ends = [
        ((HALF, own * SEQ), BF16),
        ((HALF, own * SEQ), F32),
        ((own, D), F32),
        (label_table.shape, F32),
        (time_table.shape, F32),
        ((6, HALF, D), F32),
        ((6, 1, HALF), F32),
        ((3, HALF, HALF), F32),
        ((3, 1, HALF), F32),
        ((HALF, HALF), F32),
        ((1, HALF), F32),
        ((HALF, FFH), F32),
        ((1, FFH), F32),
        ((HALF, FFH), F32),
        ((1, HALF), F32),
    ]
    (
        block_outs, input_grads, cond_grad, g_label, g_time, g_ada, g_adab,
        g_qkv, g_qb, g_proj, g_pb, g_fc1, g_b1, g_fc2, g_b2,
    ) = pl.pallas_call(
        last_kernel,
        out_shape=[jax.ShapeDtypeStruct(s, d) for s, d in ends],
        in_specs=[vmem] * len(made),
        out_specs=[vmem] * len(ends),
        compiler_params=pltpu.CompilerParams(vmem_limit_bytes=40 * 1024 * 1024),
    )(*made)
    return (
        block_outs.T[None],
        input_grads.T[None],
        cond_grad,
        g_label,
        g_time,
        jnp.transpose(g_ada, (2, 0, 1))[None],
        jnp.transpose(g_adab, (1, 0, 2)),
        jnp.transpose(g_qkv, (1, 0, 2))[None],
        jnp.transpose(g_qb, (1, 0, 2)),
        g_proj[None],
        g_pb,
        g_fc1[None],
        g_b1,
        g_fc2.T[None],
        g_b2,
    )


def solution(mesh):
    return jax.shard_map(
        on_device,
        mesh=mesh,
        in_specs=(
            P(("dp", "row"), "col"),
            P(("dp", "row")),
            P(("dp", "row")),
            P(("dp", "row"), "col"),
            P(),
            P(),
            P("section", None, None, "col"),
            P("section", None, "col"),
            P("section", "col", None, "row"),
            P("section", None, "row"),
            P("section", "row", "col"),
            P("section", "col"),
            P("section", "col", "row"),
            P("section", "row"),
            P("section", "row", "col"),
            P("section", "col"),
        ),
        out_specs=(
            P("section", ("dp", "row"), "col"),
            P("section", ("dp", "row"), "col"),
            P(("dp", "row"), None),
            P(),
            P(),
            P("section", None, None, "col"),
            P("section", None, "col"),
            P("section", "col", None, "row"),
            P("section", None, "row"),
            P("section", "row", "col"),
            P("section", "col"),
            P("section", "col", "row"),
            P("section", "row"),
            P("section", "row", "col"),
            P("section", "col"),
        ),
        check_vma=False,
    )
```

```python
import functools
import math

import jax
import jax.numpy as jnp
from jax import lax
from jax.experimental import pallas as pl
from jax.experimental.pallas import tpu as pltpu
from jax.sharding import PartitionSpec as P

D = 384
HALF = D // 2
HD = 64
FF = 1536
FFH = FF // 2
SEQ = 256
EPS = 1e-06
SCALE = 1.0 / math.sqrt(HD)
SOFT = SCALE * math.log2(math.e)
MESH = pl.DeviceIdType.MESH
F32 = jnp.float32
BF16 = jnp.bfloat16

ROWS_A, ROWS_B, ROWS_T = 4 * HALF, 5 * HALF, 6 * HALF
GROWS = ROWS_T + 16
GROUPS = (
    ((0, 96), (96, 96)),
    ((192, 96), (288, 96)),
    ((384, 96), (480, 96)),
    ((576, 96), (672, 96)),
    ((768, 96), (864, 96)),
    ((960, 96), (1056, 64), (1120, 48)),
)
CHUNKS = tuple(chunk for group in GROUPS for chunk in group)
PIECES = 6
RELAYED = 5
STRIP = HALF // 2
STRIPS = {i: ((0, STRIP),) if i < 4 else ((0, STRIP // 2), (STRIP // 2, STRIP // 2)) for i in range(RELAYED)}
PARTS = 4
PART = SEQ // PARTS


def dot(a, b):
    return jnp.dot(a, b, preferred_element_type=F32)


def dot_nt(a, b):
    return lax.dot_general(a, b, (((1,), (1,)), ((), ())), preferred_element_type=F32)


def dot_tn(a, b):
    return lax.dot_general(a, b, (((0,), (0,)), ((), ())), preferred_element_type=F32)


def norm_rows(v):
    mean_val = jnp.mean(v, axis=-1, keepdims=True)
    cen = v - mean_val
    inv = lax.rsqrt(jnp.mean(cen * cen, axis=-1, keepdims=True) + EPS)
    return cen * inv, inv


def norm_back(g, normed, inv):
    return inv * (
        g
        - jnp.mean(g, axis=-1, keepdims=True)
        - normed * jnp.mean(g * normed, axis=-1, keepdims=True)
    )


C0 = math.sqrt(2.0 / math.pi)
C1 = 0.044715 * C0


def gelu_and_slope(v):
    u = v * v
    p = 0.5 + 0.5 * jnp.tanh(v * (C0 + C1 * u))
    act = v * p
    return act, p + act * (1.0 - p) * (2.0 * C0 + (6.0 * C1) * u)


def col_sum(v):
    return jnp.sum(v.astype(F32), axis=0, keepdims=True)


def flipped(index, step):
    return index + step * (1 - 2 * lax.rem(index // step, 2))


def align(index, size):
    return pl.multiple_of(index * size, size)


class Wires:
    def __init__(self, send_sem, recv_sem):
        self.send_sem, self.recv_sem = send_sem, recv_sem
        self.number, self.started = {}, []

    def index(self, name):
        return self.number.setdefault(name, len(self.number))

    def copy(self, name, src, dst, where):
        k = self.index(name)
        return pltpu.make_async_remote_copy(
            src_ref=src,
            dst_ref=dst,
            send_sem=self.send_sem.at[k],
            recv_sem=self.recv_sem.at[k],
            device_id=where,
            device_id_type=MESH,
        )

    def send(self, name, src, dst, where):
        self.copy(name, src, dst, where).start()
        self.started.append((lambda: self.copy(name, src, dst, where), None))

    def send_if(self, cond, make):
        pl.when(cond)(lambda: make().start())
        self.started.append((make, cond))

    def arrived(self, name, dst, where):
        self.copy(name, dst, dst, where).wait_recv()

    def finish(self):
        for make, cond in self.started:

            def wait(make=make):
                make().wait_send()

            if cond is None:
                wait()
            else:
                pl.when(cond)(wait)


def main_kernel(
    bits, dp,
    lat, labels_in, times_in, cot, ltab_in, ttab_in, ada_in, adab_in, qkv_in, qb_in, proj_in, pb_in, fc1, b1_in, fc2, b2_in,
    res, block_out, input_grad, cond_grad, dm16, silu16, adab_sum, g3, ids,
    labels, times, adab, qkv, qb, proj, pb, b1, b2, ltab, ttab, ada, xr, cr, modbuf, mod, ball, sh, wa, wb, wp, w1, w2, xf, gof, x2, g2, obuf, gbuf,
    normed1, inv1, normed2, branch_a, branch_f, hidden1, hidden2, pqk, pv, prob, attended, act, slope,
    gf, gpre, gra, gatt, gqk, gv, outt, gint, gp, rc, t1, own1, rr, t2, zz, dmod, dm, pull, early, late, condb, biasg,
    send_sem, recv_sem, local_sem,
):
    r, c, z = lax.axis_index("row"), lax.axis_index("col"), lax.axis_index("dp")
    sec = lax.axis_index("section")
    h = lax.rem(z, 2)
    to_col, to_row, to_sec = {"col": 1 - c}, {"row": 1 - r}, {"section": 1 - sec}
    to_dp = [{"dp": flipped(z, 1 << j)} for j in range(bits)]
    middle_at = dp // 2
    left = jnp.where(z < middle_at, 1, 0)
    outer = jnp.logical_or(z == 0, z == dp - 1)
    inner = jnp.logical_or(z == middle_at - 1, z == middle_at)
    to_in = {"dp": z + 2 * left - 1}
    to_out = {"dp": jnp.where(outer, dp - 1 - z, z + 1 - 2 * left)}
    not_outer, not_inner = jnp.logical_not(outer), jnp.logical_not(inner)
    first, second = sec == 0, sec == 1

    barrier = pltpu.get_barrier_semaphore()
    me = 2 * z + r
    places = early.shape[0]
    others = [lax.rem(me + step, places) for step in range(1, places)]
    homes = [{"dp": other // 2, "row": lax.rem(other, 2)} for other in others]
    greeted = [to_col, to_sec, *homes]
    for where in greeted:
        pl.semaphore_signal(barrier, inc=1, device_id=where, device_id_type=MESH)

    def place(i, pr, pc, at, size):
        rows = pl.ds(pl.multiple_of(pc * HALF + at, 16), size)
        if i < 2:
            return (wa, wb)[i].at[pr, rows]
        return (w1 if i < 4 else w2).at[pr, rows, pl.ds((i % 2) * D, D)]

    own_lanes = pl.ds(align(c, SEQ), SEQ)
    their_lanes = pl.ds(align(1 - c, SEQ), SEQ)
    own_rows = pl.ds(align(c, HALF), HALF)
    local = []

    def bring(src, dst):
        copy = pltpu.make_async_copy(src, dst, local_sem.at[len(local)])
        copy.start()
        local.append(copy)

    for src, dst in (
        (qkv_in, qkv), (proj_in, proj), (qb_in, qb), (pb_in, pb), (b1_in, b1), (b2_in, b2),
        (labels_in, labels), (times_in, times), (adab_in, adab), (ltab_in, ltab), (ttab_in, ttab),
    ):
        bring(src, dst)
    bring(ada_in, ada)
    bring(lat.at[:, own_lanes], xr.at[c])
    bring(cot.at[:, own_lanes], cr.at[c])
    bring(fc1, w1.at[r, own_rows])
    bring(fc2, w2.at[r, own_rows])

    for copy in local[:6]:
        copy.wait()
    sh[0, :, :HALF] = qkv[0]
    sh[0, :, HALF:] = qkv[1]
    sh[1, :, :HALF] = qkv[2]
    sh[1, :, HALF:] = proj[...]
    own_bias = 2 * r + c
    ball[own_bias] = jnp.zeros((8, D), F32)
    ball[own_bias, 0:1, :HALF] = qb[0]
    ball[own_bias, 0:1, HALF:] = qb[1]
    ball[own_bias, 1:2, :HALF] = qb[2]
    ball[own_bias, 1:2, HALF:] = pb[...]
    ball[own_bias, 2:3, :] = b1[:, :D]
    ball[own_bias, 3:4, :] = b1[:, D:]
    ball[own_bias, 4:5, :HALF] = b2[...]

    pl.semaphore_wait(barrier, len(greeted))
    wires = Wires(send_sem, recv_sem)

    def source(i, at, size):
        rows = pl.ds(at, size)
        if i < 2:
            return sh.at[i, rows]
        return (fc1 if i < 4 else fc2).at[rows, pl.ds((i % 2) * D, D)]

    def strip(half, at):
        return pl.multiple_of(half * STRIP + at, 16)

    for i in range(RELAYED):
        for s, (at, size) in enumerate(STRIPS[i]):
            here = strip(h, at)
            wires.send(("y", i, s), source(i, here, size), place(i, r, c, here, size), to_row)
        if i == 0:
            wires.send("x", lat.at[:, their_lanes], xr.at[c], to_col)
            wires.send("bias col", ball.at[own_bias], ball.at[own_bias], to_col)
            for k in range(2):
                wires.send(("own", k), source(k, 0, HALF), place(k, r, c, 0, HALF), to_col)
            wires.send("bias row", ball.at[own_bias], ball.at[own_bias], to_row)
    for s in range(2):
        wires.send(("y", RELAYED, s), source(RELAYED, s * STRIP, STRIP), place(RELAYED, r, c, s * STRIP, STRIP), to_row)
    for k in range(2, PIECES):
        wires.send(("own", k), source(k, 0, HALF), place(k, r, c, 0, HALF), to_col)
    wires.send("cot", cot.at[:, their_lanes], cr.at[c], to_col)
    wa[r, own_rows] = sh[0]
    wb[r, own_rows] = sh[1]
    for copy in local[6:]:
        copy.wait()

    def hot(ids_ref, table_ref):
        wide = (2, table_ref.shape[0])
        wanted = jnp.where(lax.broadcasted_iota(jnp.int32, wide, 0) == 0, ids_ref[0], ids_ref[1])
        return dot(jnp.where(lax.broadcasted_iota(jnp.int32, wide, 1) == wanted, 1.0, 0.0).astype(BF16), table_ref[...])

    cond = hot(labels, ltab) + hot(times, ttab)
    condb[...] = cond
    silu_low = (cond / (1.0 + jnp.exp(-cond))).astype(BF16)
    modbuf[0:2] = jnp.zeros((2, 8, HALF), F32)
    for i in range(6):
        part = dot_nt(silu_low, ada[i]) + adab[i]
        for latent in range(2):
            modbuf[latent, i : i + 1, :] = part[latent : latent + 1, :]
    wires.send("mod", modbuf.at[1 - c], modbuf.at[2 + c], to_col)
    modbuf[2 + c] = modbuf[c]

    def y_step(i, s=0):
        if i < RELAYED:
            at, size = STRIPS[i][s]
            here = place(i, 1 - r, c, strip(h, at), size)
        else:
            here = place(i, 1 - r, c, s * STRIP, STRIP)
        wires.arrived(("y", i, s), here, to_row)
        if i < RELAYED:
            wires.copy(("z", i, s), here, here, to_dp[0]).start()
        wires.copy(("fy", i, s), here, here, to_col).start()

    def z_step(i, s=0):
        at, size = STRIPS[i][s]
        here = place(i, 1 - r, c, strip(1 - h, at), size)
        wires.arrived(("z", i, s), here, to_dp[0])
        wires.copy(("fz", i, s), here, here, to_col).start()

    def ready_own(i):
        wires.arrived(("own", i), place(i, r, 1 - c, 0, HALF), to_col)

    def ready_other(i):
        if i < RELAYED:
            for s, (at, size) in enumerate(STRIPS[i]):
                wires.arrived(("fy", i, s), place(i, 1 - r, 1 - c, strip(h, at), size), to_col)
                wires.arrived(("fz", i, s), place(i, 1 - r, 1 - c, strip(1 - h, at), size), to_col)
        else:
            for s in range(2):
                wires.arrived(("fy", i, s), place(i, 1 - r, 1 - c, s * STRIP, STRIP), to_col)

    def on_first(*steps):
        @pl.when(first)
        def _():
            for step, *args in steps:
                step(*args)

    def ids_of(ref):
        wanted = jnp.where(lax.broadcasted_iota(jnp.int32, (2, D), 0) == 0, ref[0], ref[1])
        return wanted.astype(F32)

    def share(name, table):
        for step, home in enumerate(homes):
            wires.copy((name, step), table.at[me], table.at[me], home).start()

    def shared(name, table, wait):
        for step in range(places - 1):
            other = lax.rem(me + places - 1 - step, places)
            copy = wires.copy((name, step), table.at[other], table.at[other], homes[step])
            copy.wait_recv() if wait else copy.wait_send()

    def spread_early():
        shared("s", early, True)
        rows = [early[i] for i in range(places)]
        silu16[...] = jnp.concatenate([v[0:2] for v in rows], axis=0).astype(BF16)
        for which in range(2):
            ids[which] = jnp.concatenate([v[2 + 2 * which : 4 + 2 * which] for v in rows], axis=0)

    early[me] = jnp.concatenate([silu_low.astype(F32), ids_of(labels), ids_of(times), jnp.zeros((2, D), F32)], axis=0)

    wires.arrived("x", xr.at[1 - c], to_col)
    wires.arrived("bias col", ball.at[2 * r + 1 - c], to_col)
    for k in range(2):
        ready_own(k)

    @pl.when(first)
    def _():
        xf[...] = jnp.concatenate([xr[0].astype(F32).T, xr[1].astype(F32).T], axis=1)

    wires.arrived("mod", modbuf.at[2 + 1 - c], to_col)
    for half in range(2):
        mod[:, half * HALF : (half + 1) * HALF] = modbuf[2 + half]
    wires.arrived("bias row", ball.at[2 * (1 - r) + c], to_row)

    @pl.when(second)
    def _():
        wires.arrived("cot", cr.at[1 - c], to_col)
        gof[...] = jnp.concatenate([cr[0].astype(F32).T, cr[1].astype(F32).T], axis=1)
        for kind, i, s in (
            (y_step, 0, 0), (y_step, 1, 0), (y_step, 2, 0), (z_step, 0, 0), (y_step, 3, 0), (z_step, 1, 0),
            (y_step, 4, 0), (y_step, 4, 1), (z_step, 2, 0), (z_step, 3, 0), (y_step, 5, 0), (z_step, 4, 0),
            (z_step, 4, 1), (y_step, 5, 1),
        ):
            kind(i, s)
        for i in range(PIECES):
            ready_other(i)
        share("s", early)
        spread_early()

    m = [mod[i : i + 1, :] for i in range(6)]
    for part in range(PARTS):
        rows = slice(part * PART, (part + 1) * PART)

        @pl.when(second)
        def _():
            wires.arrived(("fwd", part), x2.at[pl.ds(part * PART, PART)], to_sec)
            xf[rows, :] = x2[rows, :].astype(F32)

        n1, inv1[rows, :] = norm_rows(xf[rows, :])
        normed1[rows, :] = n1
        hidden1[rows, :] = (n1 * (1.0 + m[1]) + m[0]).astype(BF16)

    def query_key(q):
        pqk[q] = (dot(hidden1[...], wa[q]) + ball[2 * q + c, 0:1, :]).astype(BF16)

    def value(q):
        pv[q] = (dot(hidden1[...], wb[q, :, :HALF]) + ball[2 * q + c, 1:2, :HALF]).astype(BF16)

    def parts_of(q, j):
        return pqk[q, :, j * HD : (j + 1) * HD], pqk[q, :, HALF + j * HD : HALF + (j + 1) * HD], pv[q, :, j * HD : (j + 1) * HD]

    def attend(q, j):
        query, key, val = parts_of(q, j)
        s = dot_nt(query, key)
        e = jnp.exp2((s - jnp.max(s, axis=-1, keepdims=True)) * SOFT)
        p = e * (1.0 / jnp.sum(e, axis=-1, keepdims=True))
        prob[3 * q + j] = p
        attended[q, :, j * HD : (j + 1) * HD] = dot(p.astype(BF16), val).astype(BF16)

    query_key(r)
    value(r)
    on_first((y_step, 0))
    attend(r, 0)
    attend(r, 1)
    on_first((y_step, 1))
    attend(r, 2)
    on_first((y_step, 2), (z_step, 0), (ready_other, 0))
    query_key(1 - r)
    on_first((y_step, 3), (z_step, 1), (ready_other, 1))
    value(1 - r)
    for q in range(2):
        for half in range(2):
            wp[q * HALF : (q + 1) * HALF, half * HALF : (half + 1) * HALF] = wb[q, half * HALF : (half + 1) * HALF, HALF:]
    on_first((y_step, 4, 0))
    attend(1 - r, 0)
    on_first((y_step, 4, 1))
    attend(1 - r, 1)
    on_first((z_step, 2))
    attend(1 - r, 2)
    ba = dot(attended[0], wp[:HALF]) + dot(attended[1], wp[HALF:])
    ba += jnp.concatenate([ball[2 * r, 1:2, HALF:], ball[2 * r + 1, 1:2, HALF:]], axis=1)
    branch_a[...] = ba
    middle = xf[...] + m[2] * ba
    n2, inv2 = norm_rows(middle)
    xf[...] = middle
    normed2[...] = n2
    hidden2[...] = (n2 * (1.0 + m[4]) + m[3]).astype(BF16)

    def up(q):
        bias = jnp.concatenate([ball[2 * q + c, 2:3, :], ball[2 * q + c, 3:4, :]], axis=1)
        a, sl = gelu_and_slope(dot(hidden2[...], w1[q]) + bias)
        act[q] = a.astype(BF16)
        slope[q] = sl

    on_first((z_step, 3), (z_step, 4, 0))
    for k in range(2, PIECES):
        ready_own(k)
    up(r)
    on_first((z_step, 4, 1), (y_step, 5, 0), (ready_other, 2), (ready_other, 3))
    up(1 - r)
    on_first((y_step, 5, 1))
    down_bias = jnp.concatenate([ball[2 * r, 4:5, :HALF], ball[2 * r + 1, 4:5, :HALF]], axis=1)
    branch_f[...] = dot_nt(act[r], w2[r]) + down_bias
    on_first((ready_other, 4), (ready_other, 5))
    for part in range(2):
        rows = slice(part * 128, (part + 1) * 128)
        bf = branch_f[rows, :] + dot_nt(act[1 - r, rows, :], w2[1 - r])
        branch_f[rows, :] = bf
        obuf[rows, :] = (xf[rows, :] + m[5] * bf).astype(BF16)

        @pl.when(first)
        def _():
            for sub in range(2):
                there = pl.ds((2 * part + sub) * PART, PART)
                wires.copy(("fwd", 2 * part + sub), obuf.at[there], x2.at[there], to_sec).start()

    their_feats = pl.ds(align(1 - c, HALF), HALF)

    def send_out():
        outt[...] = obuf[...].astype(F32).T.astype(BF16)
        wires.copy("out", outt.at[their_feats], block_out.at[:, own_lanes], to_col).start()
        block_out[:, own_lanes] = outt[own_rows, :]

    pl.when(first)(send_out)

    @pl.when(first)
    def _():
        share("s", early)
        spread_early()
        wires.arrived("cot", cr.at[1 - c], to_col)
        for part in range(PARTS):
            wires.arrived(("bwd", part), g2.at[pl.ds(part * PART, PART)], to_sec)
            rows = slice(part * PART, (part + 1) * PART)
            gof[rows, :] = g2[rows, :].astype(F32)

    def send_col(g):
        at = GROUPS[g][0][0]
        rows = pl.ds(at, GROUPS[g][-1][0] + GROUPS[g][-1][1] - at)
        wires.copy(("c0", g), gp.at[1 - r, 1 - c, rows], rc.at[1 - r, rows], to_col).start()
        wires.copy(("c1", g), gp.at[r, 1 - c, rows], rc.at[r, rows], to_col).start()

    def total(a, b):
        return (a.astype(F32) + b.astype(F32)).astype(BF16)

    def from_col(g):
        at = GROUPS[g][0][0]
        rows = pl.ds(at, GROUPS[g][-1][0] + GROUPS[g][-1][1] - at)
        wires.arrived(("c0", g), rc.at[1 - r, rows], to_col)
        for at, size in GROUPS[g]:
            chunk = pl.ds(at, size)
            t1[chunk, :] = total(gp[1 - r, c, chunk, :], rc[1 - r, chunk, :])
            wires.copy(("r", at), t1.at[chunk], rr.at[chunk], to_row).start()
        wires.arrived(("c1", g), rc.at[r, rows], to_col)
        own1[rows, :] = total(gp[r, c, rows, :], rc[r, rows, :])

    zname = {0: "zi", 1: "zm"}

    def send_in(k, cond):
        rows = pl.ds(*CHUNKS[k])
        for kind in range(2):
            say = jnp.logical_and(cond, inner if kind else not_inner)

            def make(kind=kind):
                return wires.copy((zname[kind], k), t2.at[rows], zz.at[kind, rows], to_in)

            wires.send_if(say, make)

    def from_row(k):
        rows = pl.ds(*CHUNKS[k])
        wires.arrived(("r", CHUNKS[k][0]), rr.at[rows], to_row)
        t2[rows, :] = total(own1[rows, :], rr[rows, :])
        send_in(k, outer)

    def fold(k):
        rows = pl.ds(*CHUNKS[k])

        @pl.when(not_outer)
        def _():
            wires.arrived(("zi", k), zz.at[0, rows], to_out)
            t2[rows, :] = total(t2[rows, :], zz[0, rows, :])

        send_in(k, not_outer)

    def send_back(k, cond):
        rows = pl.ds(*CHUNKS[k])
        wires.send_if(cond, lambda: wires.copy(("zo", k), res.at[rows], res.at[rows], to_out))

    def finish(k):
        rows = pl.ds(*CHUNKS[k])

        @pl.when(inner)
        def _():
            wires.arrived(("zm", k), zz.at[1, rows], to_in)
            res[rows, :] = total(t2[rows, :], zz[1, rows, :])

        send_back(k, jnp.logical_and(inner, not_outer))

    def last(k):
        rows = pl.ds(*CHUNKS[k])

        @pl.when(not_inner)
        def _():
            wires.arrived(("zo", k), res.at[rows], to_in)

        send_back(k, jnp.logical_and(not_inner, not_outer))

    def rows_of(half):
        return slice(half * HALF, (half + 1) * HALF)

    def weight_down():
        back = gf[...].astype(F32).T.astype(BF16)
        for k in range(2):
            for q in range(2):
                grad = dot(back, act[q, :, k * D : (k + 1) * D]).astype(BF16)
                for half in range(2):
                    gp[q, half, rows_of(k), :] = grad[rows_of(half), :]
            send_col(k)

    def weight_up():
        back = hidden2[...].astype(F32).T.astype(BF16)
        for k in range(2):
            for q in range(2):
                grad = dot(back, gpre[q, :, k * D : (k + 1) * D]).astype(BF16)
                for half in range(2):
                    gp[q, half, rows_of(2 + k), :] = grad[rows_of(half), :]
            send_col(2 + k)

    def weight_proj():
        for q in range(2):
            grad = dot_tn(attended[q], gra[...]).astype(BF16)
            for half in range(2):
                gp[q, half, ROWS_B:ROWS_T, HALF:] = grad[:, rows_of(half)]

    def sums_down():
        dmod[5:6, :] = col_sum(gof[...] * branch_f[...])
        biasg[0:1, :D] = col_sum(gf[...])
        for q in range(2):
            biasg[1:2, q * FFH : (q + 1) * FFH] = col_sum(gpre[q])

    gf[...] = (gof[...] * m[5]).astype(BF16)
    pl.when(first)(weight_down)
    for q in range(2):
        gpre[q] = (dot(gf[...], w2[q]) * slope[q]).astype(BF16)

    @pl.when(first)
    def _():
        from_col(0)
        from_col(1)
        weight_up()

    grad_h2 = dot_nt(gpre[0], w1[0]) + dot_nt(gpre[1], w1[1])
    n2 = normed2[...]
    gm = gof[...] + norm_back(grad_h2 * (1.0 + m[4]), n2, inv2)
    gra[...] = (gm * m[2]).astype(BF16)
    gatt[...] = dot_nt(gra[...], wp[...]).astype(BF16)
    dmod[4:5, :] = col_sum(grad_h2 * n2)
    dmod[3:4, :] = col_sum(grad_h2)
    dmod[2:3, :] = col_sum(gm * branch_a[...])
    biasg[2:3, :D] = col_sum(gra[...])

    @pl.when(first)
    def _():
        from_col(2)
        from_col(3)

    for head in range(6):
        q, j = head // 3, head % 3
        query, key, val = parts_of(q, j)
        p = prob[head]
        g = gatt[:, head * HD : (head + 1) * HD]
        grad_prob = dot_nt(g, val)
        delta = jnp.sum(p * grad_prob, axis=-1, keepdims=True)
        gs = (p * (grad_prob - delta) * SCALE).astype(BF16)
        gqk[q, :, j * HD : (j + 1) * HD] = dot(gs, key).astype(BF16)
        gqk[q, :, HALF + j * HD : HALF + (j + 1) * HD] = dot_tn(gs, query).astype(BF16)
        gv[q, :, j * HD : (j + 1) * HD] = dot_tn(p.astype(BF16), g).astype(BF16)
    n1 = normed1[...]
    grad_h1 = dot_nt(gqk[0], wa[0]) + dot_nt(gqk[1], wa[1])
    grad_h1 += dot_nt(gv[0], wb[0, :, :HALF]) + dot_nt(gv[1], wb[1, :, :HALF])
    gi = gm + norm_back(grad_h1 * (1.0 + m[1]), n1, inv1[...])
    gbuf[...] = gi.astype(BF16)

    @pl.when(second)
    def _():
        for part in range(PARTS):
            there = pl.ds(part * PART, PART)
            wires.copy(("bwd", part), gbuf.at[there], g2.at[there], to_sec).start()
        weight_down()
        weight_up()

    weight_proj()
    back = hidden1[...].astype(F32).T.astype(BF16)
    for q in range(2):
        grad = dot(back, gqk[q]).astype(BF16)
        for half in range(2):
            gp[q, half, ROWS_A:ROWS_B, :] = grad[rows_of(half), :]
    send_col(4)
    for q in range(2):
        grad = dot(back, gv[q]).astype(BF16)
        for half in range(2):
            gp[q, half, ROWS_B:ROWS_T, :HALF] = grad[rows_of(half), :]

    @pl.when(second)
    def _():
        from_col(0)
        from_col(1)

    sums_down()
    zero = jnp.zeros((1, HALF), F32)
    for q in range(2):
        bqk, bv = col_sum(gqk[q]), col_sum(gv[q])
        for half in range(2):
            tail = [
                bqk,
                jnp.concatenate([bv, biasg[2:3, rows_of(half)]], axis=1),
                biasg[1:2, q * FFH : q * FFH + D],
                biasg[1:2, q * FFH + D : (q + 1) * FFH],
                jnp.concatenate([biasg[0:1, rows_of(half)], zero], axis=1),
                jnp.zeros((11, D), F32),
            ]
            gp[q, half, ROWS_T:GROWS, :] = jnp.concatenate(tail, axis=0).astype(BF16)
    send_col(5)

    @pl.when(second)
    def _():
        from_col(2)
        from_col(3)

    dmod[1:2, :] = col_sum(grad_h1 * n1)
    dmod[0:1, :] = col_sum(grad_h1)
    for half in range(2):
        dm[2 + half, 0:6, :] = dmod[0:6, rows_of(half)]
        dm[2 + half, 6:8, :] = jnp.zeros((2, HALF), F32)
    wires.send("dm", dm.at[2 + 1 - c], dm.at[c], to_col)
    gint[...] = gi.T
    wires.send("gin", gint.at[their_feats], input_grad.at[:, own_lanes], to_col)
    input_grad[:, own_lanes] = gint[own_rows, :]
    pl.when(second)(send_out)

    def pull_part():
        wires.arrived("dm", dm.at[1 - c], to_col)
        dm[c] = dm[2 + c]
        part = jnp.zeros((2, D), F32)
        for i in range(6):
            low = jnp.concatenate([dm[0, i : i + 1, :], dm[1, i : i + 1, :]], axis=0).astype(BF16)
            part += dot(low, ada[i])
        pull[0] = jnp.concatenate([part, jnp.zeros((6, D), F32)], axis=0)
        wires.send("p0", pull.at[0], pull.at[1], to_col)

    def pull_section():
        wires.arrived("p0", pull.at[1], to_col)
        pull[2] = pull[0] + pull[1]
        wires.send("p1", pull.at[2], pull.at[3], to_sec)

    def fill_table():
        wires.arrived("p1", pull.at[3], to_sec)
        v = condb[...]
        sig = 1.0 / (1.0 + jnp.exp(-v))
        grad = (pull[2, 0:2, :] + pull[3, 0:2, :]) * (sig * (1.0 + v * (1.0 - sig)))
        cond_grad[...] = grad

        mods = jnp.concatenate([dm[0, 0:6, :], dm[1, 0:6, :]], axis=1)
        late[me] = jnp.concatenate([grad, mods], axis=0)
        share("t", late)

    def spread_late():
        shared("t", late, True)
        rows = [late[i] for i in range(places)]
        grads = jnp.concatenate([v[0:2] for v in rows], axis=0)
        high = grads.astype(BF16)
        rest = grads - high.astype(F32)
        mid = rest.astype(BF16)
        g3[...] = jnp.concatenate([high.astype(F32), mid.astype(F32), rest - mid.astype(F32)], axis=0).astype(BF16)
        summed = functools.reduce(lambda v, w: v + w, rows)
        for i in range(6):
            adab_sum[i] = summed[2 + i : 3 + i, :HALF] + summed[2 + i : 3 + i, HALF:]
            parts = []
            for v in rows:
                parts += [v[2 + i : 3 + i, :HALF], v[2 + i : 3 + i, HALF:]]
            dm16[i] = jnp.concatenate(parts, axis=0).astype(BF16)

    small = [pull_part, pull_section, fill_table]
    count = len(CHUNKS)
    for tick in range(max(count + 6, 2 * len(small))):
        if tick < 2:
            from_col(4 + tick)
        for lag, step in ((0, from_row), (3, fold), (6, finish)):
            if 0 <= tick - lag < count:
                step(tick - lag)
        if tick % 2 == 1 and tick // 2 < len(small):
            small[tick // 2]()
    spread_late()
    for k in range(count):
        last(k)
    wires.arrived("out", block_out.at[:, their_lanes], to_col)
    wires.arrived("gin", input_grad.at[:, their_lanes], to_col)
    wires.finish()
    shared("s", early, False)
    shared("t", late, False)
    wires.copy("out", outt.at[their_feats], block_out.at[:, own_lanes], to_col).wait_send()
    for g, group in enumerate(GROUPS):
        rows = pl.ds(group[0][0], group[-1][0] + group[-1][1] - group[0][0])
        wires.copy(("c0", g), gp.at[1 - r, 1 - c, rows], rc.at[1 - r, rows], to_col).wait_send()
        wires.copy(("c1", g), gp.at[r, 1 - c, rows], rc.at[r, rows], to_col).wait_send()
        for at, size in group:
            chunk = pl.ds(at, size)
            wires.copy(("r", at), t1.at[chunk], rr.at[chunk], to_row).wait_send()
    for i in range(RELAYED):
        for s, (at, size) in enumerate(STRIPS[i]):
            near = place(i, 1 - r, c, strip(h, at), size)
            far = place(i, 1 - r, c, strip(1 - h, at), size)
            wires.copy(("z", i, s), near, near, to_dp[0]).wait_send()
            wires.copy(("fy", i, s), near, near, to_col).wait_send()
            wires.copy(("fz", i, s), far, far, to_col).wait_send()
    for s in range(2):
        near = place(RELAYED, 1 - r, c, s * STRIP, STRIP)
        wires.copy(("fy", RELAYED, s), near, near, to_col).wait_send()
    for name, src, dst, which in (("fwd", obuf, x2, first), ("bwd", gbuf, g2, second)):

        @pl.when(which)
        def _():
            for part in range(PARTS):
                there = pl.ds(part * PART, PART)
                wires.copy((name, part), src.at[there], dst.at[there], to_sec).wait_send()


def last_kernel(
    res, block_in, grad_in, cond_in, dm16, silu16, adab_in, g3, ids,
    block_out, input_grad, label_out, time_out, ada_out, qkv_out, proj_out, fc1_out, fc2_out,
    cond_out, g_adab, g_qb, g_pb, g_b1, g_b2,
    g_label, g_time, g_ada, g_qkv, g_proj, g_fc1, g_fc2, sem,
):
    copies = []

    def move(src, dst):
        copy = pltpu.make_async_copy(src, dst, sem.at[len(copies)])
        copy.start()
        copies.append(copy)

    move(block_in, block_out)
    move(grad_in, input_grad)
    count = g3.shape[0] // 3
    for which, held, out in ((0, g_label, label_out), (1, g_time, time_out)):
        one = ids[which][:, :1]
        wide = (count, out.shape[0])
        hot = jnp.where(lax.broadcasted_iota(jnp.int32, wide, 1).astype(F32) == one, 1.0, 0.0).astype(BF16)
        held[...] = dot_tn(jnp.concatenate([hot, hot, hot], axis=0), g3[...])
        move(held, out)
    for i in range(6):
        g_ada[i] = dot_tn(dm16[i], silu16[...])
    move(g_ada, ada_out)
    for k in range(2):
        g_fc2[:, k * D : (k + 1) * D] = res[k * HALF : (k + 1) * HALF, :].astype(F32)
        g_fc1[:, k * D : (k + 1) * D] = res[(2 + k) * HALF : (3 + k) * HALF, :].astype(F32)
    move(g_fc2, fc2_out)
    move(g_fc1, fc1_out)
    low = res[ROWS_A:ROWS_B, :].astype(F32)
    g_qkv[0] = low[:, :HALF]
    g_qkv[1] = low[:, HALF:]
    low = res[ROWS_B:ROWS_T, :].astype(F32)
    g_qkv[2] = low[:, :HALF]
    g_proj[...] = low[:, HALF:]
    move(g_qkv, qkv_out)
    move(g_proj, proj_out)
    cond_out[...] = cond_in[...]
    g_adab[...] = adab_in[...]
    tail = res[ROWS_T:GROWS, :].astype(F32)
    g_qb[0] = tail[0:1, :HALF]
    g_qb[1] = tail[0:1, HALF:]
    g_qb[2] = tail[1:2, :HALF]
    g_pb[...] = tail[1:2, HALF:]
    g_b1[:, :D] = tail[2:3, :]
    g_b1[:, D:] = tail[3:4, :]
    g_b2[...] = tail[4:5, :HALF]
    for copy in copies:
        copy.wait()


def on_device(
    latents_in, labels, timesteps, out_grad, label_table, time_table, ada_w, ada_b,
    qkv_w, qkv_b, proj_w, proj_b, fc1_w, fc1_b, fc2_w, fc2_b,
):
    own = latents_in.shape[0] // SEQ
    dp = lax.axis_size("dp")
    places = dp * lax.axis_size("row")
    bits = dp.bit_length() - 1
    latents = places * own
    vmem, hbm = pl.BlockSpec(memory_space=pltpu.VMEM), pl.BlockSpec(memory_space=pltpu.HBM)
    args = (
        latents_in.T,
        labels,
        timesteps,
        out_grad.T,
        label_table,
        time_table,
        jnp.transpose(ada_w[0], (1, 2, 0)),
        jnp.transpose(ada_b, (1, 0, 2)),
        jnp.transpose(qkv_w[0], (1, 0, 2)),
        jnp.transpose(qkv_b, (1, 0, 2)),
        proj_w[0],
        proj_b,
        fc1_w[0],
        fc1_b,
        fc2_w[0].T,
        fc2_b,
    )
    outs = [
        ((GROWS, D), BF16),
        ((HALF, own * SEQ), BF16),
        ((HALF, own * SEQ), F32),
        ((own, D), F32),
        ((6, latents, HALF), BF16),
        ((latents, D), BF16),
        ((6, 1, HALF), F32),
        ((3 * latents, D), BF16),
        ((2, latents, D), F32),
    ]
    scratch = [
        ((6, 1, HALF), F32),
        ((3, HALF, HALF), BF16),
        ((3, 1, HALF), F32),
        ((HALF, HALF), BF16),
        ((1, HALF), F32),
        ((1, FFH), F32),
        ((1, HALF), F32),
        (label_table.shape, BF16),
        (time_table.shape, BF16),
        ((6, HALF, D), BF16),
        ((2, HALF, SEQ), BF16),
        ((2, HALF, SEQ), BF16),
        ((4, 8, HALF), F32),
        ((8, D), F32),
        ((4, 8, D), F32),
        ((2, HALF, D), BF16),
        ((2, D, D), BF16),
        ((2, D, D), BF16),
        ((D, D), BF16),
        ((2, D, FFH), BF16),
        ((2, D, FFH), BF16),
        ((SEQ, D), F32),
        ((SEQ, D), F32),
        ((SEQ, D), BF16),
        ((SEQ, D), BF16),
        ((SEQ, D), BF16),
        ((SEQ, D), BF16),
        ((SEQ, D), F32),
        ((SEQ, 1), F32),
        ((SEQ, D), F32),
        ((SEQ, D), F32),
        ((SEQ, D), F32),
        ((SEQ, D), BF16),
        ((SEQ, D), BF16),
        ((2, SEQ, D), BF16),
        ((2, SEQ, HALF), BF16),
        ((6, SEQ, SEQ), F32),
        ((2, SEQ, HALF), BF16),
        ((2, SEQ, FFH), BF16),
        ((2, SEQ, FFH), F32),
        ((SEQ, D), BF16),
        ((2, SEQ, FFH), BF16),
        ((SEQ, D), BF16),
        ((SEQ, D), BF16),
        ((2, SEQ, D), BF16),
        ((2, SEQ, HALF), BF16),
        ((D, SEQ), BF16),
        ((D, SEQ), F32),
        ((2, 2, GROWS, D), BF16),
        ((2, GROWS, D), BF16),
        ((GROWS, D), BF16),
        ((GROWS, D), BF16),
        ((GROWS, D), BF16),
        ((GROWS, D), BF16),
        ((2, GROWS, D), BF16),
        ((8, D), F32),
        ((4, 8, HALF), F32),
        ((4, 8, D), F32),
        ((places, 8, D), F32),
        ((places, 8, D), F32),
        ((own, D), F32),
        ((8, FF), F32),
    ]
    wires = 64 + 2 * len(GROUPS) + 4 * len(CHUNKS) + 2 * places
    made = pl.pallas_call(
        functools.partial(main_kernel, bits, dp),
        out_shape=[jax.ShapeDtypeStruct(s, d) for s, d in outs],
        in_specs=[hbm] * len(args),
        out_specs=[vmem] * len(outs),
        scratch_shapes=[pltpu.SMEM((own,), jnp.int32)] * 2
        + [pltpu.VMEM(s, d) for s, d in scratch]
        + [pltpu.SemaphoreType.DMA((wires,)), pltpu.SemaphoreType.DMA((wires,)), pltpu.SemaphoreType.DMA((16,))],
        compiler_params=pltpu.CompilerParams(
            vmem_limit_bytes=46 * 1024 * 1024, collective_id=0, has_side_effects=True
        ),
    )(*[pltpu.with_memory_space_constraint(a, pltpu.HBM) for a in args])
    big = [
        ((HALF, own * SEQ), BF16),
        ((HALF, own * SEQ), F32),
        (label_table.shape, F32),
        (time_table.shape, F32),
        ((6, HALF, D), F32),
        ((3, HALF, HALF), F32),
        ((HALF, HALF), F32),
        ((HALF, FFH), F32),
        ((HALF, FFH), F32),
    ]
    little = [
        ((own, D), F32),
        ((6, 1, HALF), F32),
        ((3, 1, HALF), F32),
        ((1, HALF), F32),
        ((1, FFH), F32),
        ((1, HALF), F32),
    ]
    (
        block_outs, input_grads, g_label, g_time, g_ada, g_qkv, g_proj, g_fc1, g_fc2,
        cond_grad, g_adab, g_qb, g_pb, g_b1, g_b2,
    ) = pl.pallas_call(
        last_kernel,
        out_shape=[jax.ShapeDtypeStruct(s, d) for s, d in big + little],
        in_specs=[vmem] * len(made),
        out_specs=[hbm] * len(big) + [vmem] * len(little),
        scratch_shapes=[pltpu.VMEM(s, d) for s, d in big[2:]] + [pltpu.SemaphoreType.DMA((len(big),))],
        compiler_params=pltpu.CompilerParams(vmem_limit_bytes=46 * 1024 * 1024),
    )(*made)
    return (
        block_outs.T[None],
        input_grads.T[None],
        cond_grad,
        g_label,
        g_time,
        jnp.transpose(g_ada, (2, 0, 1))[None],
        jnp.transpose(g_adab, (1, 0, 2)),
        jnp.transpose(g_qkv, (1, 0, 2))[None],
        jnp.transpose(g_qb, (1, 0, 2)),
        g_proj[None],
        g_pb,
        g_fc1[None],
        g_b1,
        g_fc2.T[None],
        g_b2,
    )


def solution(mesh):
    return jax.shard_map(
        on_device,
        mesh=mesh,
        in_specs=(
            P(("dp", "row"), "col"),
            P(("dp", "row")),
            P(("dp", "row")),
            P(("dp", "row"), "col"),
            P(),
            P(),
            P("section", None, None, "col"),
            P("section", None, "col"),
            P("section", "col", None, "row"),
            P("section", None, "row"),
            P("section", "row", "col"),
            P("section", "col"),
            P("section", "col", "row"),
            P("section", "row"),
            P("section", "row", "col"),
            P("section", "col"),
        ),
        out_specs=(
            P("section", ("dp", "row"), "col"),
            P("section", ("dp", "row"), "col"),
            P(("dp", "row"), None),
            P(),
            P(),
            P("section", None, None, "col"),
            P("section", None, "col"),
            P("section", "col", None, "row"),
            P("section", None, "row"),
            P("section", "row", "col"),
            P("section", "col"),
            P("section", "col", "row"),
            P("section", "row"),
            P("section", "row", "col"),
            P("section", "col"),
        ),
        check_vma=False,
    )
```

```python
import functools
import math

import jax
import jax.numpy as jnp
from jax import lax
from jax.experimental import pallas as pl
from jax.experimental.pallas import tpu as pltpu
from jax.sharding import PartitionSpec as P

D = 384
HALF = D // 2
HD = 64
FF = 1536
FFH = FF // 2
SEQ = 256
EPS = 1e-06
SCALE = 1.0 / math.sqrt(HD)
SOFT = SCALE * math.log2(math.e)
MESH = pl.DeviceIdType.MESH
F32 = jnp.float32
BF16 = jnp.bfloat16

ROWS_A, ROWS_B, ROWS_T = 4 * HALF, 5 * HALF, 6 * HALF
GROWS = ROWS_T + 16
GROUPS = (
    ((0, 96), (96, 96)),
    ((192, 96), (288, 96)),
    ((384, 96), (480, 96)),
    ((576, 96), (672, 96)),
    ((768, 64), (832, 64), (896, 64)),
    ((960, 64), (1024, 48), (1072, 48), (1120, 32), (1152, 16)),
)
CHUNKS = tuple(chunk for group in GROUPS for chunk in group)
PIECES = 6
RELAYED = 5
STRIP = HALF // 2
STRIPS = {i: ((0, STRIP),) if i < 4 else ((0, STRIP // 2), (STRIP // 2, STRIP // 2)) for i in range(RELAYED)}
PARTS = 4
PART = SEQ // PARTS


def dot(a, b):
    return jnp.dot(a, b, preferred_element_type=F32)


def dot_nt(a, b):
    return lax.dot_general(a, b, (((1,), (1,)), ((), ())), preferred_element_type=F32)


def dot_tn(a, b):
    return lax.dot_general(a, b, (((0,), (0,)), ((), ())), preferred_element_type=F32)


def norm_rows(v):
    mean_val = jnp.mean(v, axis=-1, keepdims=True)
    cen = v - mean_val
    inv = lax.rsqrt(jnp.mean(cen * cen, axis=-1, keepdims=True) + EPS)
    return cen * inv, inv


def norm_back(g, normed, inv):
    return inv * (
        g
        - jnp.mean(g, axis=-1, keepdims=True)
        - normed * jnp.mean(g * normed, axis=-1, keepdims=True)
    )


C0 = math.sqrt(2.0 / math.pi)
C1 = 0.044715 * C0


def gelu_and_slope(v):
    u = v * v
    p = 0.5 + 0.5 * jnp.tanh(v * (C0 + C1 * u))
    act = v * p
    return act, p + act * (1.0 - p) * (2.0 * C0 + (6.0 * C1) * u)


def col_sum(v):
    return jnp.sum(v.astype(F32), axis=0, keepdims=True)


def flipped(index, step):
    return index + step * (1 - 2 * lax.rem(index // step, 2))


def align(index, size):
    return pl.multiple_of(index * size, size)


class Wires:
    def __init__(self, send_sem, recv_sem):
        self.send_sem, self.recv_sem = send_sem, recv_sem
        self.number, self.started = {}, []

    def index(self, name):
        return self.number.setdefault(name, len(self.number))

    def copy(self, name, src, dst, where):
        k = self.index(name)
        return pltpu.make_async_remote_copy(
            src_ref=src,
            dst_ref=dst,
            send_sem=self.send_sem.at[k],
            recv_sem=self.recv_sem.at[k],
            device_id=where,
            device_id_type=MESH,
        )

    def send(self, name, src, dst, where):
        self.copy(name, src, dst, where).start()
        self.started.append((lambda: self.copy(name, src, dst, where), None))

    def send_if(self, cond, make):
        pl.when(cond)(lambda: make().start())
        self.started.append((make, cond))

    def arrived(self, name, dst, where):
        self.copy(name, dst, dst, where).wait_recv()

    def finish(self):
        for make, cond in self.started:

            def wait(make=make):
                make().wait_send()

            if cond is None:
                wait()
            else:
                pl.when(cond)(wait)


def main_kernel(
    bits, dp,
    lat, labels_in, times_in, cot, ltab_in, ttab_in, ada_in, adab_in, qkv_in, qb_in, proj_in, pb_in, fc1, b1_in, fc2, b2_in,
    res, block_out, input_grad, cond_grad, dm16, silu16, adab_sum, g3, ids,
    labels, times, adab, qkv, qb, proj, pb, b1, b2, ltab, ttab, ada, xr, cr, modbuf, mod, ball, sh, wa, wb, wp, w1, w2, xf, gof, x2, g2, obuf, gbuf,
    normed1, inv1, inv2, normed2, gh1, gh2, gm, gin, branch_a, branch_f, hidden1, hidden2, pqk, pv, prob, attended, act, slope,
    gf, gpre, gra, gatt, gqk, gv, outt, gint, gp, rc, t1, own1, rr, t2, zz, dmod, dm, pull, early, late, condb, biasg,
    send_sem, recv_sem, local_sem,
):
    r, c, z = lax.axis_index("row"), lax.axis_index("col"), lax.axis_index("dp")
    sec = lax.axis_index("section")
    h = lax.rem(z, 2)
    to_col, to_row, to_sec = {"col": 1 - c}, {"row": 1 - r}, {"section": 1 - sec}
    to_dp = [{"dp": flipped(z, 1 << j)} for j in range(bits)]
    middle_at = dp // 2
    left = jnp.where(z < middle_at, 1, 0)
    outer = jnp.logical_or(z == 0, z == dp - 1)
    inner = jnp.logical_or(z == middle_at - 1, z == middle_at)
    to_in = {"dp": z + 2 * left - 1}
    to_out = {"dp": jnp.where(outer, dp - 1 - z, z + 1 - 2 * left)}
    not_outer, not_inner = jnp.logical_not(outer), jnp.logical_not(inner)
    first, second = sec == 0, sec == 1

    barrier = pltpu.get_barrier_semaphore()
    me = 2 * z + r
    places = early.shape[0]
    others = [lax.rem(me + step, places) for step in range(1, places)]
    homes = [{"dp": other // 2, "row": lax.rem(other, 2)} for other in others]
    greeted = [to_col, to_sec, *homes]
    for where in greeted:
        pl.semaphore_signal(barrier, inc=1, device_id=where, device_id_type=MESH)

    def place(i, pr, pc, at, size):
        rows = pl.ds(pl.multiple_of(pc * HALF + at, 16), size)
        if i < 2:
            return (wa, wb)[i].at[pr, rows]
        return (w1 if i < 4 else w2).at[pr, rows, pl.ds((i % 2) * D, D)]

    own_lanes = pl.ds(align(c, SEQ), SEQ)
    their_lanes = pl.ds(align(1 - c, SEQ), SEQ)
    own_rows = pl.ds(align(c, HALF), HALF)
    local = []

    def bring(src, dst):
        copy = pltpu.make_async_copy(src, dst, local_sem.at[len(local)])
        copy.start()
        local.append(copy)

    for src, dst in (
        (qkv_in, qkv), (proj_in, proj), (qb_in, qb), (pb_in, pb), (b1_in, b1), (b2_in, b2),
        (labels_in, labels), (times_in, times), (adab_in, adab), (ltab_in, ltab), (ttab_in, ttab),
    ):
        bring(src, dst)
    bring(ada_in, ada)
    bring(lat.at[:, own_lanes], xr.at[c])
    bring(cot.at[:, own_lanes], cr.at[c])
    bring(fc1, w1.at[r, own_rows])
    bring(fc2, w2.at[r, own_rows])

    for copy in local[:6]:
        copy.wait()
    sh[0, :, :HALF] = qkv[0]
    sh[0, :, HALF:] = qkv[1]
    sh[1, :, :HALF] = qkv[2]
    sh[1, :, HALF:] = proj[...]
    own_bias = 2 * r + c
    ball[own_bias] = jnp.zeros((8, D), F32)
    ball[own_bias, 0:1, :HALF] = qb[0]
    ball[own_bias, 0:1, HALF:] = qb[1]
    ball[own_bias, 1:2, :HALF] = qb[2]
    ball[own_bias, 1:2, HALF:] = pb[...]
    ball[own_bias, 2:3, :] = b1[:, :D]
    ball[own_bias, 3:4, :] = b1[:, D:]
    ball[own_bias, 4:5, :HALF] = b2[...]

    pl.semaphore_wait(barrier, len(greeted))
    wires = Wires(send_sem, recv_sem)

    def source(i, at, size):
        rows = pl.ds(at, size)
        if i < 2:
            return sh.at[i, rows]
        return (fc1 if i < 4 else fc2).at[rows, pl.ds((i % 2) * D, D)]

    def strip(half, at):
        return pl.multiple_of(half * STRIP + at, 16)

    for i in range(RELAYED):
        for s, (at, size) in enumerate(STRIPS[i]):
            here = strip(h, at)
            wires.send(("y", i, s), source(i, here, size), place(i, r, c, here, size), to_row)
        if i == 0:
            wires.send("x", lat.at[:, their_lanes], xr.at[c], to_col)
            wires.send("bias col", ball.at[own_bias], ball.at[own_bias], to_col)
            for k in range(2):
                wires.send(("own", k), source(k, 0, HALF), place(k, r, c, 0, HALF), to_col)
            wires.send("bias row", ball.at[own_bias], ball.at[own_bias], to_row)
    for s in range(2):
        wires.send(("y", RELAYED, s), source(RELAYED, s * STRIP, STRIP), place(RELAYED, r, c, s * STRIP, STRIP), to_row)
    for k in range(2, PIECES):
        wires.send(("own", k), source(k, 0, HALF), place(k, r, c, 0, HALF), to_col)
    wires.send("cot", cot.at[:, their_lanes], cr.at[c], to_col)
    wa[r, own_rows] = sh[0]
    wb[r, own_rows] = sh[1]
    for copy in local[6:]:
        copy.wait()

    def hot(ids_ref, table_ref):
        wide = (2, table_ref.shape[0])
        wanted = jnp.where(lax.broadcasted_iota(jnp.int32, wide, 0) == 0, ids_ref[0], ids_ref[1])
        return dot(jnp.where(lax.broadcasted_iota(jnp.int32, wide, 1) == wanted, 1.0, 0.0).astype(BF16), table_ref[...])

    cond = hot(labels, ltab) + hot(times, ttab)
    condb[...] = cond
    silu_low = (cond / (1.0 + jnp.exp(-cond))).astype(BF16)
    modbuf[0:2] = jnp.zeros((2, 8, HALF), F32)
    for i in range(6):
        part = dot_nt(silu_low, ada[i]) + adab[i]
        for latent in range(2):
            modbuf[latent, i : i + 1, :] = part[latent : latent + 1, :]
    wires.send("mod", modbuf.at[1 - c], modbuf.at[2 + c], to_col)
    modbuf[2 + c] = modbuf[c]

    def y_step(i, s=0):
        if i < RELAYED:
            at, size = STRIPS[i][s]
            here = place(i, 1 - r, c, strip(h, at), size)
        else:
            here = place(i, 1 - r, c, s * STRIP, STRIP)
        wires.arrived(("y", i, s), here, to_row)
        if i < RELAYED:
            wires.copy(("z", i, s), here, here, to_dp[0]).start()
        wires.copy(("fy", i, s), here, here, to_col).start()

    def z_step(i, s=0):
        at, size = STRIPS[i][s]
        here = place(i, 1 - r, c, strip(1 - h, at), size)
        wires.arrived(("z", i, s), here, to_dp[0])
        wires.copy(("fz", i, s), here, here, to_col).start()

    def ready_own(i):
        wires.arrived(("own", i), place(i, r, 1 - c, 0, HALF), to_col)

    def ready_other(i):
        if i < RELAYED:
            for s, (at, size) in enumerate(STRIPS[i]):
                wires.arrived(("fy", i, s), place(i, 1 - r, 1 - c, strip(h, at), size), to_col)
                wires.arrived(("fz", i, s), place(i, 1 - r, 1 - c, strip(1 - h, at), size), to_col)
        else:
            for s in range(2):
                wires.arrived(("fy", i, s), place(i, 1 - r, 1 - c, s * STRIP, STRIP), to_col)

    def ids_of(ref):
        wanted = jnp.where(lax.broadcasted_iota(jnp.int32, (2, D), 0) == 0, ref[0], ref[1])
        return wanted.astype(F32)

    def share(name, table):
        for step, home in enumerate(homes):
            wires.copy((name, step), table.at[me], table.at[me], home).start()

    def shared(name, table, wait):
        for step in range(places - 1):
            other = lax.rem(me + places - 1 - step, places)
            copy = wires.copy((name, step), table.at[other], table.at[other], homes[step])
            copy.wait_recv() if wait else copy.wait_send()

    def spread_early():
        shared("s", early, True)
        rows = [early[i] for i in range(places)]
        silu16[...] = jnp.concatenate([v[0:2] for v in rows], axis=0).astype(BF16)
        for which in range(2):
            ids[which] = jnp.concatenate([v[2 + 2 * which : 4 + 2 * which] for v in rows], axis=0)

    early[me] = jnp.concatenate([silu_low.astype(F32), ids_of(labels), ids_of(times), jnp.zeros((2, D), F32)], axis=0)

    wires.arrived("x", xr.at[1 - c], to_col)
    wires.arrived("bias col", ball.at[2 * r + 1 - c], to_col)
    for k in range(2):
        ready_own(k)

    @pl.when(first)
    def _():
        xf[...] = jnp.concatenate([xr[0].astype(F32).T, xr[1].astype(F32).T], axis=1)

    wires.arrived("mod", modbuf.at[2 + 1 - c], to_col)
    for half in range(2):
        mod[:, half * HALF : (half + 1) * HALF] = modbuf[2 + half]
    wires.arrived("bias row", ball.at[2 * (1 - r) + c], to_row)

    @pl.when(second)
    def _():
        wires.arrived("cot", cr.at[1 - c], to_col)
        gof[...] = jnp.concatenate([cr[0].astype(F32).T, cr[1].astype(F32).T], axis=1)
        for kind, i, s in (
            (y_step, 0, 0), (y_step, 1, 0), (y_step, 2, 0), (z_step, 0, 0), (y_step, 3, 0), (z_step, 1, 0),
            (y_step, 4, 0), (y_step, 4, 1), (z_step, 2, 0), (z_step, 3, 0), (y_step, 5, 0), (z_step, 4, 0),
            (z_step, 4, 1), (y_step, 5, 1),
        ):
            kind(i, s)
        for i in range(PIECES):
            ready_other(i)
        share("s", early)
        spread_early()

    m = [mod[i : i + 1, :] for i in range(6)]

    def norm_one(part):
        rows = slice(part * PART, (part + 1) * PART)
        n1, inv1[rows, :] = norm_rows(xf[rows, :])
        normed1[rows, :] = n1
        hidden1[rows, :] = (n1 * (1.0 + m[1]) + m[0]).astype(BF16)

    def query_key(q):
        pqk[q] = (dot(hidden1[...], wa[q]) + ball[2 * q + c, 0:1, :]).astype(BF16)

    def value(q):
        pv[q] = (dot(hidden1[...], wb[q, :, :HALF]) + ball[2 * q + c, 1:2, :HALF]).astype(BF16)

    def parts_of(q, j):
        return pqk[q, :, j * HD : (j + 1) * HD], pqk[q, :, HALF + j * HD : HALF + (j + 1) * HD], pv[q, :, j * HD : (j + 1) * HD]

    def attend(q, j):
        query, key, val = parts_of(q, j)
        s = dot_nt(query, key)
        e = jnp.exp2((s - jnp.max(s, axis=-1, keepdims=True)) * SOFT)
        p = e * (1.0 / jnp.sum(e, axis=-1, keepdims=True))
        prob[3 * q + j] = p
        attended[q, :, j * HD : (j + 1) * HD] = dot(p.astype(BF16), val).astype(BF16)

    def whole_proj():
        for q in range(2):
            for half in range(2):
                rows = slice(half * HALF, (half + 1) * HALF)
                wp[q * HALF : (q + 1) * HALF, rows] = wb[q, rows, HALF:]

    def middle():
        ba = dot(attended[0], wp[:HALF]) + dot(attended[1], wp[HALF:])
        ba += jnp.concatenate([ball[2 * r, 1:2, HALF:], ball[2 * r + 1, 1:2, HALF:]], axis=1)
        branch_a[...] = ba
        mid = xf[...] + m[2] * ba
        n2, inv2[...] = norm_rows(mid)
        xf[...] = mid
        normed2[...] = n2
        hidden2[...] = (n2 * (1.0 + m[4]) + m[3]).astype(BF16)

    def up(q):
        bias = jnp.concatenate([ball[2 * q + c, 2:3, :], ball[2 * q + c, 3:4, :]], axis=1)
        a, sl = gelu_and_slope(dot(hidden2[...], w1[q]) + bias)
        act[q] = a.astype(BF16)
        slope[q] = sl

    def down_start(q):
        bias = jnp.concatenate([ball[2 * r, 4:5, :HALF], ball[2 * r + 1, 4:5, :HALF]], axis=1)
        branch_f[...] = dot_nt(act[q], w2[q]) + bias

    def down_end(q, part):
        rows = slice(part * 128, (part + 1) * 128)
        bf = branch_f[rows, :] + dot_nt(act[q, rows, :], w2[q])
        branch_f[rows, :] = bf
        obuf[rows, :] = (xf[rows, :] + m[5] * bf).astype(BF16)

    @pl.when(first)
    def _():
        for part in range(PARTS):
            norm_one(part)
        query_key(r)
        value(r)
        y_step(0)
        attend(r, 0)
        attend(r, 1)
        y_step(1)
        attend(r, 2)
        y_step(2)
        z_step(0)
        ready_other(0)
        query_key(1 - r)
        y_step(3)
        z_step(1)
        ready_other(1)
        value(1 - r)
        whole_proj()
        y_step(4, 0)
        attend(1 - r, 0)
        y_step(4, 1)
        attend(1 - r, 1)
        z_step(2)
        attend(1 - r, 2)
        middle()
        for k in range(2, PIECES):
            ready_own(k)
        up(r)
        z_step(3)
        y_step(5, 0)
        z_step(4, 0)
        ready_other(2)
        ready_other(3)
        up(1 - r)
        down_start(r)
        y_step(5, 1)
        z_step(4, 1)
        ready_other(4)
        ready_other(5)
        for part in range(2):
            down_end(1 - r, part)
            for sub in range(2):
                there = pl.ds((2 * part + sub) * PART, PART)
                wires.copy(("fwd", 2 * part + sub), obuf.at[there], x2.at[there], to_sec).start()

    @pl.when(second)
    def _():
        whole_proj()
        for k in range(2, PIECES):
            ready_own(k)
        for part in range(PARTS):
            rows = slice(part * PART, (part + 1) * PART)
            wires.arrived(("fwd", part), x2.at[pl.ds(part * PART, PART)], to_sec)
            xf[rows, :] = x2[rows, :].astype(F32)
            norm_one(part)
        for q in range(2):
            query_key(q)
            value(q)
        for head in range(6):
            attend(head // 3, head % 3)
        middle()
        for q in range(2):
            up(q)
        down_start(0)
        for part in range(2):
            down_end(1, part)

    their_feats = pl.ds(align(1 - c, HALF), HALF)

    def send_out():
        outt[...] = obuf[...].astype(F32).T.astype(BF16)
        wires.copy("out", outt.at[their_feats], block_out.at[:, own_lanes], to_col).start()
        block_out[:, own_lanes] = outt[own_rows, :]

    pl.when(first)(send_out)

    @pl.when(first)
    def _():
        share("s", early)
        spread_early()
        wires.arrived("cot", cr.at[1 - c], to_col)
        for part in range(PARTS):
            wires.arrived(("bwd", part), g2.at[pl.ds(part * PART, PART)], to_sec)
            rows = slice(part * PART, (part + 1) * PART)
            gof[rows, :] = g2[rows, :].astype(F32)

    def send_col(g):
        at = GROUPS[g][0][0]
        rows = pl.ds(at, GROUPS[g][-1][0] + GROUPS[g][-1][1] - at)
        wires.copy(("c0", g), gp.at[1 - r, 1 - c, rows], rc.at[1 - r, rows], to_col).start()
        wires.copy(("c1", g), gp.at[r, 1 - c, rows], rc.at[r, rows], to_col).start()

    def total(a, b):
        return (a.astype(F32) + b.astype(F32)).astype(BF16)

    def from_col(g):
        facing(g)
        settle(g)

    def facing(g):
        at = GROUPS[g][0][0]
        rows = pl.ds(at, GROUPS[g][-1][0] + GROUPS[g][-1][1] - at)
        wires.arrived(("c0", g), rc.at[1 - r, rows], to_col)
        for at, size in GROUPS[g]:
            chunk = pl.ds(at, size)
            t1[chunk, :] = total(gp[1 - r, c, chunk, :], rc[1 - r, chunk, :])
            wires.copy(("r", at), t1.at[chunk], rr.at[chunk], to_row).start()

    def settle(g):
        at = GROUPS[g][0][0]
        rows = pl.ds(at, GROUPS[g][-1][0] + GROUPS[g][-1][1] - at)
        wires.arrived(("c1", g), rc.at[r, rows], to_col)
        own1[rows, :] = total(gp[r, c, rows, :], rc[r, rows, :])

    zname = {0: "zi", 1: "zm"}

    def send_in(k, cond):
        rows = pl.ds(*CHUNKS[k])
        for kind in range(2):
            say = jnp.logical_and(cond, inner if kind else not_inner)

            def make(kind=kind):
                return wires.copy((zname[kind], k), t2.at[rows], zz.at[kind, rows], to_in)

            wires.send_if(say, make)

    def from_row(k):
        rows = pl.ds(*CHUNKS[k])
        wires.arrived(("r", CHUNKS[k][0]), rr.at[rows], to_row)
        t2[rows, :] = total(own1[rows, :], rr[rows, :])
        send_in(k, outer)

    def fold(k):
        rows = pl.ds(*CHUNKS[k])

        @pl.when(not_outer)
        def _():
            wires.arrived(("zi", k), zz.at[0, rows], to_out)
            t2[rows, :] = total(t2[rows, :], zz[0, rows, :])

        send_in(k, not_outer)

    def send_back(k, cond):
        rows = pl.ds(*CHUNKS[k])
        wires.send_if(cond, lambda: wires.copy(("zo", k), res.at[rows], res.at[rows], to_out))

    def finish(k):
        rows = pl.ds(*CHUNKS[k])

        @pl.when(inner)
        def _():
            wires.arrived(("zm", k), zz.at[1, rows], to_in)
            res[rows, :] = total(t2[rows, :], zz[1, rows, :])

        send_back(k, jnp.logical_and(inner, not_outer))

    def last(k):
        rows = pl.ds(*CHUNKS[k])

        @pl.when(not_inner)
        def _():
            wires.arrived(("zo", k), res.at[rows], to_in)

        send_back(k, jnp.logical_and(not_inner, not_outer))

    def rows_of(half):
        return slice(half * HALF, (half + 1) * HALF)

    def send_part(g, which):
        q = r if which else 1 - r
        at = GROUPS[g][0][0]
        rows = pl.ds(at, GROUPS[g][-1][0] + GROUPS[g][-1][1] - at)
        wires.copy(("c" + str(which), g), gp.at[q, 1 - c, rows], rc.at[q, rows], to_col).start()

    def weight_down():
        back = gf[...].astype(F32).T.astype(BF16)
        for which in range(2):
            q = r if which else 1 - r
            for k in range(2):
                grad = dot(back, act[q, :, k * D : (k + 1) * D]).astype(BF16)
                for half in range(2):
                    gp[q, half, rows_of(k), :] = grad[rows_of(half), :]
                send_part(k, which)

    def weight_up():
        back = hidden2[...].astype(F32).T.astype(BF16)
        for k in range(2):
            for q in range(2):
                grad = dot(back, gpre[q, :, k * D : (k + 1) * D]).astype(BF16)
                for half in range(2):
                    gp[q, half, rows_of(2 + k), :] = grad[rows_of(half), :]
            send_col(2 + k)

    def weight_proj():
        for q in range(2):
            grad = dot_tn(attended[q], gra[...]).astype(BF16)
            for half in range(2):
                gp[q, half, ROWS_B:ROWS_T, HALF:] = grad[:, rows_of(half)]

    def sums_down():
        dmod[5:6, :] = col_sum(gof[...] * branch_f[...])
        biasg[0:1, :D] = col_sum(gf[...])
        for q in range(2):
            biasg[1:2, q * FFH : (q + 1) * FFH] = col_sum(gpre[q])

    def grad_down():
        for q in range(2):
            gpre[q] = (dot(gf[...], w2[q]) * slope[q]).astype(BF16)

    def grad_middle():
        grad_h2 = dot_nt(gpre[0], w1[0]) + dot_nt(gpre[1], w1[1])
        gh2[...] = grad_h2
        mid = gof[...] + norm_back(grad_h2 * (1.0 + m[4]), normed2[...], inv2[...])
        gm[...] = mid
        gra[...] = (mid * m[2]).astype(BF16)
        gatt[...] = dot_nt(gra[...], wp[...]).astype(BF16)

    def sums_middle():
        dmod[4:5, :] = col_sum(gh2[...] * normed2[...])
        dmod[3:4, :] = col_sum(gh2[...])
        dmod[2:3, :] = col_sum(gm[...] * branch_a[...])
        biasg[2:3, :D] = col_sum(gra[...])

    def attend_back(head):
        q, j = head // 3, head % 3
        query, key, val = parts_of(q, j)
        p = prob[head]
        g = gatt[:, head * HD : (head + 1) * HD]
        grad_prob = dot_nt(g, val)
        delta = jnp.sum(p * grad_prob, axis=-1, keepdims=True)
        gs = (p * (grad_prob - delta) * SCALE).astype(BF16)
        gqk[q, :, j * HD : (j + 1) * HD] = dot(gs, key).astype(BF16)
        gqk[q, :, HALF + j * HD : HALF + (j + 1) * HD] = dot_tn(gs, query).astype(BF16)
        gv[q, :, j * HD : (j + 1) * HD] = dot_tn(p.astype(BF16), g).astype(BF16)

    def grad_first():
        grad_h1 = dot_nt(gqk[0], wa[0]) + dot_nt(gqk[1], wa[1])
        gh1[...] = grad_h1 + dot_nt(gv[0], wb[0, :, :HALF]) + dot_nt(gv[1], wb[1, :, :HALF])

    def grad_input(part):
        rows = slice(part * PART, (part + 1) * PART)
        gin[rows, :] = gm[rows, :] + norm_back(gh1[rows, :] * (1.0 + m[1]), normed1[rows, :], inv1[rows, :])

    @pl.when(first)
    def _():
        gf[...] = (gof[...] * m[5]).astype(BF16)
        weight_down()
        facing(0)
        facing(1)
        grad_down()
        settle(0)
        settle(1)
        weight_up()
        sums_down()
        grad_middle()
        from_col(2)
        from_col(3)
        for head in range(6):
            attend_back(head)
        grad_first()

    @pl.when(second)
    def _():
        gf[...] = (gof[...] * m[5]).astype(BF16)
        grad_down()
        grad_middle()
        for head in range(6):
            attend_back(head)
        grad_first()
        for part in range(PARTS):
            rows = slice(part * PART, (part + 1) * PART)
            grad_input(part)
            gbuf[rows, :] = gin[rows, :].astype(BF16)
            there = pl.ds(part * PART, PART)
            wires.copy(("bwd", part), gbuf.at[there], g2.at[there], to_sec).start()
        weight_down()
        weight_up()
        sums_down()

    weight_proj()
    back = hidden1[...].astype(F32).T.astype(BF16)
    for q in range(2):
        grad = dot(back, gqk[q]).astype(BF16)
        for half in range(2):
            gp[q, half, ROWS_A:ROWS_B, :] = grad[rows_of(half), :]
    send_col(4)
    for q in range(2):
        grad = dot(back, gv[q]).astype(BF16)
        for half in range(2):
            gp[q, half, ROWS_B:ROWS_T, :HALF] = grad[rows_of(half), :]

    @pl.when(second)
    def _():
        from_col(0)
        from_col(1)

    sums_middle()
    zero = jnp.zeros((1, HALF), F32)
    for q in range(2):
        bqk, bv = col_sum(gqk[q]), col_sum(gv[q])
        for half in range(2):
            tail = [
                bqk,
                jnp.concatenate([bv, biasg[2:3, rows_of(half)]], axis=1),
                biasg[1:2, q * FFH : q * FFH + D],
                biasg[1:2, q * FFH + D : (q + 1) * FFH],
                jnp.concatenate([biasg[0:1, rows_of(half)], zero], axis=1),
                jnp.zeros((11, D), F32),
            ]
            gp[q, half, ROWS_T:GROWS, :] = jnp.concatenate(tail, axis=0).astype(BF16)
    send_col(5)

    @pl.when(second)
    def _():
        from_col(2)
        from_col(3)

    dmod[1:2, :] = col_sum(gh1[...] * normed1[...])
    dmod[0:1, :] = col_sum(gh1[...])
    for half in range(2):
        dm[2 + half, 0:6, :] = dmod[0:6, rows_of(half)]
        dm[2 + half, 6:8, :] = jnp.zeros((2, HALF), F32)
    wires.send("dm", dm.at[2 + 1 - c], dm.at[c], to_col)

    @pl.when(first)
    def _():
        for part in range(PARTS):
            grad_input(part)

    gint[...] = gin[...].T
    wires.send("gin", gint.at[their_feats], input_grad.at[:, own_lanes], to_col)
    input_grad[:, own_lanes] = gint[own_rows, :]
    pl.when(second)(send_out)

    def pull_part():
        wires.arrived("dm", dm.at[1 - c], to_col)
        dm[c] = dm[2 + c]
        part = jnp.zeros((2, D), F32)
        for i in range(6):
            low = jnp.concatenate([dm[0, i : i + 1, :], dm[1, i : i + 1, :]], axis=0).astype(BF16)
            part += dot(low, ada[i])
        pull[0] = jnp.concatenate([part, jnp.zeros((6, D), F32)], axis=0)
        wires.send("p0", pull.at[0], pull.at[1], to_col)

    def pull_section():
        wires.arrived("p0", pull.at[1], to_col)
        pull[2] = pull[0] + pull[1]
        wires.send("p1", pull.at[2], pull.at[3], to_sec)

    def fill_table():
        wires.arrived("p1", pull.at[3], to_sec)
        v = condb[...]
        sig = 1.0 / (1.0 + jnp.exp(-v))
        grad = (pull[2, 0:2, :] + pull[3, 0:2, :]) * (sig * (1.0 + v * (1.0 - sig)))
        cond_grad[...] = grad

        mods = jnp.concatenate([dm[0, 0:6, :], dm[1, 0:6, :]], axis=1)
        late[me] = jnp.concatenate([grad, mods], axis=0)
        share("t", late)

    def spread_late():
        shared("t", late, True)
        rows = [late[i] for i in range(places)]
        grads = jnp.concatenate([v[0:2] for v in rows], axis=0)
        high = grads.astype(BF16)
        rest = grads - high.astype(F32)
        mid = rest.astype(BF16)
        g3[...] = jnp.concatenate([high.astype(F32), mid.astype(F32), rest - mid.astype(F32)], axis=0).astype(BF16)
        summed = functools.reduce(lambda v, w: v + w, rows)
        for i in range(6):
            adab_sum[i] = summed[2 + i : 3 + i, :HALF] + summed[2 + i : 3 + i, HALF:]
            parts = []
            for v in rows:
                parts += [v[2 + i : 3 + i, :HALF], v[2 + i : 3 + i, HALF:]]
            dm16[i] = jnp.concatenate(parts, axis=0).astype(BF16)

    small = [pull_part, pull_section, fill_table]
    count = len(CHUNKS)
    for tick in range(max(count + 6, 2 * len(small))):
        if tick < 2:
            from_col(4 + tick)
        for lag, step in ((0, from_row), (3, fold), (6, finish)):
            if 0 <= tick - lag < count:
                step(tick - lag)
        if tick % 2 == 1 and tick // 2 < len(small):
            small[tick // 2]()
    spread_late()
    for k in range(count):
        last(k)
    wires.arrived("out", block_out.at[:, their_lanes], to_col)
    wires.arrived("gin", input_grad.at[:, their_lanes], to_col)
    wires.finish()
    shared("s", early, False)
    shared("t", late, False)
    wires.copy("out", outt.at[their_feats], block_out.at[:, own_lanes], to_col).wait_send()
    for g, group in enumerate(GROUPS):
        rows = pl.ds(group[0][0], group[-1][0] + group[-1][1] - group[0][0])
        wires.copy(("c0", g), gp.at[1 - r, 1 - c, rows], rc.at[1 - r, rows], to_col).wait_send()
        wires.copy(("c1", g), gp.at[r, 1 - c, rows], rc.at[r, rows], to_col).wait_send()
        for at, size in group:
            chunk = pl.ds(at, size)
            wires.copy(("r", at), t1.at[chunk], rr.at[chunk], to_row).wait_send()
    for i in range(RELAYED):
        for s, (at, size) in enumerate(STRIPS[i]):
            near = place(i, 1 - r, c, strip(h, at), size)
            far = place(i, 1 - r, c, strip(1 - h, at), size)
            wires.copy(("z", i, s), near, near, to_dp[0]).wait_send()
            wires.copy(("fy", i, s), near, near, to_col).wait_send()
            wires.copy(("fz", i, s), far, far, to_col).wait_send()
    for s in range(2):
        near = place(RELAYED, 1 - r, c, s * STRIP, STRIP)
        wires.copy(("fy", RELAYED, s), near, near, to_col).wait_send()
    for name, src, dst, which in (("fwd", obuf, x2, first), ("bwd", gbuf, g2, second)):

        @pl.when(which)
        def _():
            for part in range(PARTS):
                there = pl.ds(part * PART, PART)
                wires.copy((name, part), src.at[there], dst.at[there], to_sec).wait_send()


def last_kernel(
    res, block_in, grad_in, cond_in, dm16, silu16, adab_in, g3, ids,
    block_out, input_grad, label_out, time_out, ada_out, qkv_out, proj_out, fc1_out, fc2_out,
    cond_out, g_adab, g_qb, g_pb, g_b1, g_b2,
    g_label, g_time, g_ada, g_qkv, g_proj, g_fc1, g_fc2, sem,
):
    copies = []

    def move(src, dst):
        copy = pltpu.make_async_copy(src, dst, sem.at[len(copies)])
        copy.start()
        copies.append(copy)

    move(block_in, block_out)
    move(grad_in, input_grad)
    count = g3.shape[0] // 3
    for which, held, out in ((0, g_label, label_out), (1, g_time, time_out)):
        one = ids[which][:, :1]
        wide = (count, out.shape[0])
        hot = jnp.where(lax.broadcasted_iota(jnp.int32, wide, 1).astype(F32) == one, 1.0, 0.0).astype(BF16)
        held[...] = dot_tn(jnp.concatenate([hot, hot, hot], axis=0), g3[...])
        move(held, out)
    for i in range(6):
        g_ada[i] = dot_tn(dm16[i], silu16[...])
    move(g_ada, ada_out)
    for k in range(2):
        g_fc2[:, k * D : (k + 1) * D] = res[k * HALF : (k + 1) * HALF, :].astype(F32)
        g_fc1[:, k * D : (k + 1) * D] = res[(2 + k) * HALF : (3 + k) * HALF, :].astype(F32)
    move(g_fc2, fc2_out)
    move(g_fc1, fc1_out)
    low = res[ROWS_A:ROWS_B, :].astype(F32)
    g_qkv[0] = low[:, :HALF]
    g_qkv[1] = low[:, HALF:]
    low = res[ROWS_B:ROWS_T, :].astype(F32)
    g_qkv[2] = low[:, :HALF]
    g_proj[...] = low[:, HALF:]
    move(g_qkv, qkv_out)
    move(g_proj, proj_out)
    cond_out[...] = cond_in[...]
    g_adab[...] = adab_in[...]
    tail = res[ROWS_T:GROWS, :].astype(F32)
    g_qb[0] = tail[0:1, :HALF]
    g_qb[1] = tail[0:1, HALF:]
    g_qb[2] = tail[1:2, :HALF]
    g_pb[...] = tail[1:2, HALF:]
    g_b1[:, :D] = tail[2:3, :]
    g_b1[:, D:] = tail[3:4, :]
    g_b2[...] = tail[4:5, :HALF]
    for copy in copies:
        copy.wait()


def on_device(
    latents_in, labels, timesteps, out_grad, label_table, time_table, ada_w, ada_b,
    qkv_w, qkv_b, proj_w, proj_b, fc1_w, fc1_b, fc2_w, fc2_b,
):
    own = latents_in.shape[0] // SEQ
    dp = lax.axis_size("dp")
    places = dp * lax.axis_size("row")
    bits = dp.bit_length() - 1
    latents = places * own
    vmem, hbm = pl.BlockSpec(memory_space=pltpu.VMEM), pl.BlockSpec(memory_space=pltpu.HBM)
    args = (
        latents_in.T,
        labels,
        timesteps,
        out_grad.T,
        label_table,
        time_table,
        jnp.transpose(ada_w[0], (1, 2, 0)),
        jnp.transpose(ada_b, (1, 0, 2)),
        jnp.transpose(qkv_w[0], (1, 0, 2)),
        jnp.transpose(qkv_b, (1, 0, 2)),
        proj_w[0],
        proj_b,
        fc1_w[0],
        fc1_b,
        fc2_w[0].T,
        fc2_b,
    )
    outs = [
        ((GROWS, D), BF16),
        ((HALF, own * SEQ), BF16),
        ((HALF, own * SEQ), F32),
        ((own, D), F32),
        ((6, latents, HALF), BF16),
        ((latents, D), BF16),
        ((6, 1, HALF), F32),
        ((3 * latents, D), BF16),
        ((2, latents, D), F32),
    ]
    scratch = [
        ((6, 1, HALF), F32),
        ((3, HALF, HALF), BF16),
        ((3, 1, HALF), F32),
        ((HALF, HALF), BF16),
        ((1, HALF), F32),
        ((1, FFH), F32),
        ((1, HALF), F32),
        (label_table.shape, BF16),
        (time_table.shape, BF16),
        ((6, HALF, D), BF16),
        ((2, HALF, SEQ), BF16),
        ((2, HALF, SEQ), BF16),
        ((4, 8, HALF), F32),
        ((8, D), F32),
        ((4, 8, D), F32),
        ((2, HALF, D), BF16),
        ((2, D, D), BF16),
        ((2, D, D), BF16),
        ((D, D), BF16),
        ((2, D, FFH), BF16),
        ((2, D, FFH), BF16),
        ((SEQ, D), F32),
        ((SEQ, D), F32),
        ((SEQ, D), BF16),
        ((SEQ, D), BF16),
        ((SEQ, D), BF16),
        ((SEQ, D), BF16),
        ((SEQ, D), F32),
        ((SEQ, 1), F32),
        ((SEQ, 1), F32),
        ((SEQ, D), F32),
        ((SEQ, D), F32),
        ((SEQ, D), F32),
        ((SEQ, D), F32),
        ((SEQ, D), F32),
        ((SEQ, D), F32),
        ((SEQ, D), F32),
        ((SEQ, D), BF16),
        ((SEQ, D), BF16),
        ((2, SEQ, D), BF16),
        ((2, SEQ, HALF), BF16),
        ((6, SEQ, SEQ), F32),
        ((2, SEQ, HALF), BF16),
        ((2, SEQ, FFH), BF16),
        ((2, SEQ, FFH), F32),
        ((SEQ, D), BF16),
        ((2, SEQ, FFH), BF16),
        ((SEQ, D), BF16),
        ((SEQ, D), BF16),
        ((2, SEQ, D), BF16),
        ((2, SEQ, HALF), BF16),
        ((D, SEQ), BF16),
        ((D, SEQ), F32),
        ((2, 2, GROWS, D), BF16),
        ((2, GROWS, D), BF16),
        ((GROWS, D), BF16),
        ((GROWS, D), BF16),
        ((GROWS, D), BF16),
        ((GROWS, D), BF16),
        ((2, GROWS, D), BF16),
        ((8, D), F32),
        ((4, 8, HALF), F32),
        ((4, 8, D), F32),
        ((places, 8, D), F32),
        ((places, 8, D), F32),
        ((own, D), F32),
        ((8, FF), F32),
    ]
    wires = 64 + 2 * len(GROUPS) + 4 * len(CHUNKS) + 2 * places
    made = pl.pallas_call(
        functools.partial(main_kernel, bits, dp),
        out_shape=[jax.ShapeDtypeStruct(s, d) for s, d in outs],
        in_specs=[hbm] * len(args),
        out_specs=[vmem] * len(outs),
        scratch_shapes=[pltpu.SMEM((own,), jnp.int32)] * 2
        + [pltpu.VMEM(s, d) for s, d in scratch]
        + [pltpu.SemaphoreType.DMA((wires,)), pltpu.SemaphoreType.DMA((wires,)), pltpu.SemaphoreType.DMA((16,))],
        compiler_params=pltpu.CompilerParams(
            vmem_limit_bytes=46 * 1024 * 1024, collective_id=0, has_side_effects=True
        ),
    )(*[pltpu.with_memory_space_constraint(a, pltpu.HBM) for a in args])
    big = [
        ((HALF, own * SEQ), BF16),
        ((HALF, own * SEQ), F32),
        (label_table.shape, F32),
        (time_table.shape, F32),
        ((6, HALF, D), F32),
        ((3, HALF, HALF), F32),
        ((HALF, HALF), F32),
        ((HALF, FFH), F32),
        ((HALF, FFH), F32),
    ]
    little = [
        ((own, D), F32),
        ((6, 1, HALF), F32),
        ((3, 1, HALF), F32),
        ((1, HALF), F32),
        ((1, FFH), F32),
        ((1, HALF), F32),
    ]
    (
        block_outs, input_grads, g_label, g_time, g_ada, g_qkv, g_proj, g_fc1, g_fc2,
        cond_grad, g_adab, g_qb, g_pb, g_b1, g_b2,
    ) = pl.pallas_call(
        last_kernel,
        out_shape=[jax.ShapeDtypeStruct(s, d) for s, d in big + little],
        in_specs=[vmem] * len(made),
        out_specs=[hbm] * len(big) + [vmem] * len(little),
        scratch_shapes=[pltpu.VMEM(s, d) for s, d in big[2:]] + [pltpu.SemaphoreType.DMA((len(big),))],
        compiler_params=pltpu.CompilerParams(vmem_limit_bytes=46 * 1024 * 1024),
    )(*made)
    return (
        block_outs.T[None],
        input_grads.T[None],
        cond_grad,
        g_label,
        g_time,
        jnp.transpose(g_ada, (2, 0, 1))[None],
        jnp.transpose(g_adab, (1, 0, 2)),
        jnp.transpose(g_qkv, (1, 0, 2))[None],
        jnp.transpose(g_qb, (1, 0, 2)),
        g_proj[None],
        g_pb,
        g_fc1[None],
        g_b1,
        g_fc2.T[None],
        g_b2,
    )


def solution(mesh):
    return jax.shard_map(
        on_device,
        mesh=mesh,
        in_specs=(
            P(("dp", "row"), "col"),
            P(("dp", "row")),
            P(("dp", "row")),
            P(("dp", "row"), "col"),
            P(),
            P(),
            P("section", None, None, "col"),
            P("section", None, "col"),
            P("section", "col", None, "row"),
            P("section", None, "row"),
            P("section", "row", "col"),
            P("section", "col"),
            P("section", "col", "row"),
            P("section", "row"),
            P("section", "row", "col"),
            P("section", "col"),
        ),
        out_specs=(
            P("section", ("dp", "row"), "col"),
            P("section", ("dp", "row"), "col"),
            P(("dp", "row"), None),
            P(),
            P(),
            P("section", None, None, "col"),
            P("section", None, "col"),
            P("section", "col", None, "row"),
            P("section", None, "row"),
            P("section", "row", "col"),
            P("section", "col"),
            P("section", "col", "row"),
            P("section", "row"),
            P("section", "row", "col"),
            P("section", "col"),
        ),
        check_vma=False,
    )
```

```python
import functools
import math

import jax
import jax.numpy as jnp
from jax import lax
from jax.experimental import pallas as pl
from jax.experimental.pallas import tpu as pltpu
from jax.sharding import PartitionSpec as P

D = 384
HALF = D // 2
HD = 64
FF = 1536
FFH = FF // 2
SEQ = 256
EPS = 1e-06
SCALE = 1.0 / math.sqrt(HD)
SOFT = SCALE * math.log2(math.e)
MESH = pl.DeviceIdType.MESH
F32 = jnp.float32
BF16 = jnp.bfloat16

ROWS_A, ROWS_B, ROWS_T = 4 * HALF, 5 * HALF, 6 * HALF
GROWS = ROWS_T + 16
GROUPS = (
    ((0, 96), (96, 96)),
    ((192, 96), (288, 96)),
    ((384, 96), (480, 96)),
    ((576, 96), (672, 96)),
    ((768, 64), (832, 64), (896, 64)),
    ((960, 64), (1024, 48), (1072, 48), (1120, 32), (1152, 16)),
)
CHUNKS = tuple(chunk for group in GROUPS for chunk in group)
LAGS = (3, 6)
PIECES = 6
RELAYED = 5
STRIP = HALF // 2
STRIPS = {i: ((0, STRIP),) if i < 4 else ((0, STRIP // 2), (STRIP // 2, STRIP // 2)) for i in range(RELAYED)}
PARTS = 4
PART = SEQ // PARTS


def dot(a, b):
    return jnp.dot(a, b, preferred_element_type=F32)


def dot_nt(a, b):
    return lax.dot_general(a, b, (((1,), (1,)), ((), ())), preferred_element_type=F32)


def dot_tn(a, b):
    return lax.dot_general(a, b, (((0,), (0,)), ((), ())), preferred_element_type=F32)


def norm_rows(v):
    mean_val = jnp.mean(v, axis=-1, keepdims=True)
    cen = v - mean_val
    inv = lax.rsqrt(jnp.mean(cen * cen, axis=-1, keepdims=True) + EPS)
    return cen * inv, inv


def norm_back(g, normed, inv):
    return inv * (
        g
        - jnp.mean(g, axis=-1, keepdims=True)
        - normed * jnp.mean(g * normed, axis=-1, keepdims=True)
    )


C0 = math.sqrt(2.0 / math.pi)
C1 = 0.044715 * C0


def gelu_and_slope(v):
    u = v * v
    p = 0.5 + 0.5 * jnp.tanh(v * (C0 + C1 * u))
    act = v * p
    return act, p + act * (1.0 - p) * (2.0 * C0 + (6.0 * C1) * u)


def col_sum(v):
    return jnp.sum(v.astype(F32), axis=0, keepdims=True)


def flipped(index, step):
    return index + step * (1 - 2 * lax.rem(index // step, 2))


def align(index, size):
    return pl.multiple_of(index * size, size)


class Wires:
    def __init__(self, send_sem, recv_sem):
        self.send_sem, self.recv_sem = send_sem, recv_sem
        self.number, self.started = {}, []

    def index(self, name):
        return self.number.setdefault(name, len(self.number))

    def copy(self, name, src, dst, where):
        k = self.index(name)
        return pltpu.make_async_remote_copy(
            src_ref=src,
            dst_ref=dst,
            send_sem=self.send_sem.at[k],
            recv_sem=self.recv_sem.at[k],
            device_id=where,
            device_id_type=MESH,
        )

    def send(self, name, src, dst, where):
        self.copy(name, src, dst, where).start()
        self.started.append((lambda: self.copy(name, src, dst, where), None))

    def send_if(self, cond, make):
        pl.when(cond)(lambda: make().start())
        self.started.append((make, cond))

    def arrived(self, name, dst, where):
        self.copy(name, dst, dst, where).wait_recv()

    def take(self):
        taken, self.started = self.started, []
        return taken

    def settle(self, started):
        for make, cond in started:

            def wait(make=make):
                make().wait_send()

            if cond is None:
                wait()
            else:
                pl.when(cond)(wait)


def main_kernel(
    bits, dp,
    lat, labels_in, times_in, cot, ltab_in, ttab_in, ada_in, adab_in, qkv_in, qb_in, proj_in, pb_in, fc1, b1_in, fc2, b2_in,
    res, block_out, input_grad, cond_grad, dm16, silu16, adab_sum, g3, ids,
    labels, times, adab, qkv, qb, proj, pb, b1, b2, ltab, ttab, ada, xr, cr, modbuf, mod, ball, sh, wa, wb, wp, w1, w2, xf, gof, x2, g2, obuf, gbuf,
    normed1, inv1, inv2, normed2, gh1, gh2, gm, gin, branch_a, branch_f, hidden1, hidden2, pqk, pv, prob, attended, act, slope,
    gf, gpre, gra, gatt, gqk, gv, outt, gint, gp, rc, t1, own1, rr, t2, zz, dmod, dm, pull, early, late, condb, biasg,
    send_sem, recv_sem, local_sem,
):
    r, c, z = lax.axis_index("row"), lax.axis_index("col"), lax.axis_index("dp")
    sec = lax.axis_index("section")
    h = lax.rem(z, 2)
    to_col, to_row, to_sec = {"col": 1 - c}, {"row": 1 - r}, {"section": 1 - sec}
    to_dp = [{"dp": flipped(z, 1 << j)} for j in range(bits)]
    middle_at = dp // 2
    left = jnp.where(z < middle_at, 1, 0)
    outer = jnp.logical_or(z == 0, z == dp - 1)
    inner = jnp.logical_or(z == middle_at - 1, z == middle_at)
    to_in = {"dp": z + 2 * left - 1}
    to_out = {"dp": jnp.where(outer, dp - 1 - z, z + 1 - 2 * left)}
    not_outer, not_inner = jnp.logical_not(outer), jnp.logical_not(inner)
    first, second = sec == 0, sec == 1

    barrier = pltpu.get_barrier_semaphore()
    me = 2 * z + r
    places = early.shape[0]
    others = [lax.rem(me + step, places) for step in range(1, places)]
    homes = [{"dp": other // 2, "row": lax.rem(other, 2)} for other in others]
    greeted = [to_col, to_sec, *homes]
    for where in greeted:
        pl.semaphore_signal(barrier, inc=1, device_id=where, device_id_type=MESH)

    def place(i, pr, pc, at, size):
        rows = pl.ds(pl.multiple_of(pc * HALF + at, 16), size)
        if i < 2:
            return (wa, wb)[i].at[pr, rows]
        return (w1 if i < 4 else w2).at[pr, rows, pl.ds((i % 2) * D, D)]

    own_lanes = pl.ds(align(c, SEQ), SEQ)
    their_lanes = pl.ds(align(1 - c, SEQ), SEQ)
    own_rows = pl.ds(align(c, HALF), HALF)
    local = []

    def bring(src, dst):
        copy = pltpu.make_async_copy(src, dst, local_sem.at[len(local)])
        copy.start()
        local.append(copy)

    for src, dst in (
        (qkv_in, qkv), (proj_in, proj), (qb_in, qb), (pb_in, pb), (b1_in, b1), (b2_in, b2),
        (labels_in, labels), (times_in, times), (adab_in, adab), (ltab_in, ltab), (ttab_in, ttab),
    ):
        bring(src, dst)
    bring(ada_in, ada)
    bring(lat.at[:, own_lanes], xr.at[c])
    bring(cot.at[:, own_lanes], cr.at[c])
    bring(fc1, w1.at[r, own_rows])
    bring(fc2, w2.at[r, own_rows])

    for copy in local[:6]:
        copy.wait()
    sh[0, :, :HALF] = qkv[0]
    sh[0, :, HALF:] = qkv[1]
    sh[1, :, :HALF] = qkv[2]
    sh[1, :, HALF:] = proj[...]
    own_bias = 2 * r + c
    ball[own_bias] = jnp.zeros((8, D), F32)
    ball[own_bias, 0:1, :HALF] = qb[0]
    ball[own_bias, 0:1, HALF:] = qb[1]
    ball[own_bias, 1:2, :HALF] = qb[2]
    ball[own_bias, 1:2, HALF:] = pb[...]
    ball[own_bias, 2:3, :] = b1[:, :D]
    ball[own_bias, 3:4, :] = b1[:, D:]
    ball[own_bias, 4:5, :HALF] = b2[...]

    pl.semaphore_wait(barrier, len(greeted))
    wires = Wires(send_sem, recv_sem)

    def source(i, at, size):
        rows = pl.ds(at, size)
        if i < 2:
            return sh.at[i, rows]
        return (fc1 if i < 4 else fc2).at[rows, pl.ds((i % 2) * D, D)]

    def strip(half, at):
        return pl.multiple_of(half * STRIP + at, 16)

    for i in range(RELAYED):
        for s, (at, size) in enumerate(STRIPS[i]):
            here = strip(h, at)
            wires.send(("y", i, s), source(i, here, size), place(i, r, c, here, size), to_row)
        if i == 0:
            wires.send("x", lat.at[:, their_lanes], xr.at[c], to_col)
            wires.send("bias col", ball.at[own_bias], ball.at[own_bias], to_col)
            for k in range(2):
                wires.send(("own", k), source(k, 0, HALF), place(k, r, c, 0, HALF), to_col)
            wires.send("bias row", ball.at[own_bias], ball.at[own_bias], to_row)
    for s in range(2):
        wires.send(("y", RELAYED, s), source(RELAYED, s * STRIP, STRIP), place(RELAYED, r, c, s * STRIP, STRIP), to_row)
    for k in range(2, PIECES):
        wires.send(("own", k), source(k, 0, HALF), place(k, r, c, 0, HALF), to_col)
    wires.send("cot", cot.at[:, their_lanes], cr.at[c], to_col)
    wa[r, own_rows] = sh[0]
    wb[r, own_rows] = sh[1]
    for copy in local[6:]:
        copy.wait()

    def hot(ids_ref, table_ref):
        wide = (2, table_ref.shape[0])
        wanted = jnp.where(lax.broadcasted_iota(jnp.int32, wide, 0) == 0, ids_ref[0], ids_ref[1])
        return dot(jnp.where(lax.broadcasted_iota(jnp.int32, wide, 1) == wanted, 1.0, 0.0).astype(BF16), table_ref[...])

    cond = hot(labels, ltab) + hot(times, ttab)
    condb[...] = cond
    silu_low = (cond / (1.0 + jnp.exp(-cond))).astype(BF16)
    modbuf[0:2] = jnp.zeros((2, 8, HALF), F32)
    for i in range(6):
        part = dot_nt(silu_low, ada[i]) + adab[i]
        for latent in range(2):
            modbuf[latent, i : i + 1, :] = part[latent : latent + 1, :]
    wires.send("mod", modbuf.at[1 - c], modbuf.at[2 + c], to_col)
    modbuf[2 + c] = modbuf[c]

    def y_step(i, s=0):
        if i < RELAYED:
            at, size = STRIPS[i][s]
            here = place(i, 1 - r, c, strip(h, at), size)
        else:
            here = place(i, 1 - r, c, s * STRIP, STRIP)
        wires.arrived(("y", i, s), here, to_row)
        if i < RELAYED:
            wires.copy(("z", i, s), here, here, to_dp[0]).start()
        wires.copy(("fy", i, s), here, here, to_col).start()

    def z_step(i, s=0):
        at, size = STRIPS[i][s]
        here = place(i, 1 - r, c, strip(1 - h, at), size)
        wires.arrived(("z", i, s), here, to_dp[0])
        wires.copy(("fz", i, s), here, here, to_col).start()

    def ready_own(i):
        wires.arrived(("own", i), place(i, r, 1 - c, 0, HALF), to_col)

    def ready_other(i):
        if i < RELAYED:
            for s, (at, size) in enumerate(STRIPS[i]):
                wires.arrived(("fy", i, s), place(i, 1 - r, 1 - c, strip(h, at), size), to_col)
                wires.arrived(("fz", i, s), place(i, 1 - r, 1 - c, strip(1 - h, at), size), to_col)
        else:
            for s in range(2):
                wires.arrived(("fy", i, s), place(i, 1 - r, 1 - c, s * STRIP, STRIP), to_col)

    def ids_of(ref):
        wanted = jnp.where(lax.broadcasted_iota(jnp.int32, (2, D), 0) == 0, ref[0], ref[1])
        return wanted.astype(F32)

    def share(name, table):
        for step, home in enumerate(homes):
            wires.copy((name, step), table.at[me], table.at[me], home).start()

    def shared(name, table, wait):
        for step in range(places - 1):
            other = lax.rem(me + places - 1 - step, places)
            copy = wires.copy((name, step), table.at[other], table.at[other], homes[step])
            copy.wait_recv() if wait else copy.wait_send()

    def spread_early():
        shared("s", early, True)
        rows = [early[i] for i in range(places)]
        silu16[...] = jnp.concatenate([v[0:2] for v in rows], axis=0).astype(BF16)
        for which in range(2):
            ids[which] = jnp.concatenate([v[2 + 2 * which : 4 + 2 * which] for v in rows], axis=0)

    early[me] = jnp.concatenate([silu_low.astype(F32), ids_of(labels), ids_of(times), jnp.zeros((2, D), F32)], axis=0)

    wires.arrived("x", xr.at[1 - c], to_col)
    wires.arrived("bias col", ball.at[2 * r + 1 - c], to_col)
    for k in range(2):
        ready_own(k)

    @pl.when(first)
    def _():
        xf[...] = jnp.concatenate([xr[0].astype(F32).T, xr[1].astype(F32).T], axis=1)

    wires.arrived("mod", modbuf.at[2 + 1 - c], to_col)
    for half in range(2):
        mod[:, half * HALF : (half + 1) * HALF] = modbuf[2 + half]
    wires.arrived("bias row", ball.at[2 * (1 - r) + c], to_row)

    @pl.when(second)
    def _():
        wires.arrived("cot", cr.at[1 - c], to_col)
        gof[...] = jnp.concatenate([cr[0].astype(F32).T, cr[1].astype(F32).T], axis=1)
        for kind, i, s in (
            (y_step, 0, 0), (y_step, 1, 0), (y_step, 2, 0), (z_step, 0, 0), (y_step, 3, 0), (z_step, 1, 0),
            (y_step, 4, 0), (y_step, 4, 1), (z_step, 2, 0), (z_step, 3, 0), (y_step, 5, 0), (z_step, 4, 0),
            (z_step, 4, 1), (y_step, 5, 1),
        ):
            kind(i, s)
        for i in range(PIECES):
            ready_other(i)
        share("s", early)
        spread_early()

    m = [mod[i : i + 1, :] for i in range(6)]

    def norm_one(part):
        rows = slice(part * PART, (part + 1) * PART)
        n1, inv1[rows, :] = norm_rows(xf[rows, :])
        normed1[rows, :] = n1
        hidden1[rows, :] = (n1 * (1.0 + m[1]) + m[0]).astype(BF16)

    def query_key(q):
        pqk[q] = (dot(hidden1[...], wa[q]) + ball[2 * q + c, 0:1, :]).astype(BF16)

    def value(q):
        pv[q] = (dot(hidden1[...], wb[q, :, :HALF]) + ball[2 * q + c, 1:2, :HALF]).astype(BF16)

    def parts_of(q, j):
        return pqk[q, :, j * HD : (j + 1) * HD], pqk[q, :, HALF + j * HD : HALF + (j + 1) * HD], pv[q, :, j * HD : (j + 1) * HD]

    def attend(q, j):
        query, key, val = parts_of(q, j)
        s = dot_nt(query, key)
        e = jnp.exp2((s - jnp.max(s, axis=-1, keepdims=True)) * SOFT)
        p = e * (1.0 / jnp.sum(e, axis=-1, keepdims=True))
        prob[3 * q + j] = p
        attended[q, :, j * HD : (j + 1) * HD] = dot(p.astype(BF16), val).astype(BF16)

    def whole_proj():
        for q in range(2):
            for half in range(2):
                rows = slice(half * HALF, (half + 1) * HALF)
                wp[q * HALF : (q + 1) * HALF, rows] = wb[q, rows, HALF:]

    def middle():
        ba = dot(attended[0], wp[:HALF]) + dot(attended[1], wp[HALF:])
        ba += jnp.concatenate([ball[2 * r, 1:2, HALF:], ball[2 * r + 1, 1:2, HALF:]], axis=1)
        branch_a[...] = ba
        mid = xf[...] + m[2] * ba
        n2, inv2[...] = norm_rows(mid)
        xf[...] = mid
        normed2[...] = n2
        hidden2[...] = (n2 * (1.0 + m[4]) + m[3]).astype(BF16)

    def up(q):
        bias = jnp.concatenate([ball[2 * q + c, 2:3, :], ball[2 * q + c, 3:4, :]], axis=1)
        a, sl = gelu_and_slope(dot(hidden2[...], w1[q]) + bias)
        act[q] = a.astype(BF16)
        slope[q] = sl

    def down_start(q):
        bias = jnp.concatenate([ball[2 * r, 4:5, :HALF], ball[2 * r + 1, 4:5, :HALF]], axis=1)
        branch_f[...] = dot_nt(act[q], w2[q]) + bias

    def down_end(q, part):
        rows = slice(part * 128, (part + 1) * 128)
        bf = branch_f[rows, :] + dot_nt(act[q, rows, :], w2[q])
        branch_f[rows, :] = bf
        obuf[rows, :] = (xf[rows, :] + m[5] * bf).astype(BF16)

    @pl.when(first)
    def _():
        for part in range(PARTS):
            norm_one(part)
        query_key(r)
        value(r)
        y_step(0)
        attend(r, 0)
        attend(r, 1)
        y_step(1)
        attend(r, 2)
        y_step(2)
        z_step(0)
        ready_other(0)
        query_key(1 - r)
        y_step(3)
        z_step(1)
        ready_other(1)
        value(1 - r)
        whole_proj()
        y_step(4, 0)
        attend(1 - r, 0)
        y_step(4, 1)
        attend(1 - r, 1)
        z_step(2)
        attend(1 - r, 2)
        middle()
        for k in range(2, PIECES):
            ready_own(k)
        up(r)
        z_step(3)
        y_step(5, 0)
        z_step(4, 0)
        ready_other(2)
        ready_other(3)
        up(1 - r)
        down_start(r)
        y_step(5, 1)
        z_step(4, 1)
        ready_other(4)
        ready_other(5)
        for part in range(2):
            down_end(1 - r, part)
            for sub in range(2):
                there = pl.ds((2 * part + sub) * PART, PART)
                wires.copy(("fwd", 2 * part + sub), obuf.at[there], x2.at[there], to_sec).start()

    @pl.when(second)
    def _():
        whole_proj()
        for k in range(2, PIECES):
            ready_own(k)
        for part in range(PARTS):
            rows = slice(part * PART, (part + 1) * PART)
            wires.arrived(("fwd", part), x2.at[pl.ds(part * PART, PART)], to_sec)
            xf[rows, :] = x2[rows, :].astype(F32)
            norm_one(part)
        for q in range(2):
            query_key(q)
            value(q)
        for head in range(6):
            attend(head // 3, head % 3)
        middle()
        for q in range(2):
            up(q)
        down_start(0)
        for part in range(2):
            down_end(1, part)

    their_feats = pl.ds(align(1 - c, HALF), HALF)

    def send_out():
        outt[...] = obuf[...].astype(F32).T.astype(BF16)
        wires.copy("out", outt.at[their_feats], block_out.at[:, own_lanes], to_col).start()
        block_out[:, own_lanes] = outt[own_rows, :]

    pl.when(first)(send_out)
    sent_early = wires.take()

    def settle_sent():
        wires.settle(sent_early)
        shared("s", early, False)
        for i in range(RELAYED):
            for s, (at, size) in enumerate(STRIPS[i]):
                near = place(i, 1 - r, c, strip(h, at), size)
                far = place(i, 1 - r, c, strip(1 - h, at), size)
                wires.copy(("z", i, s), near, near, to_dp[0]).wait_send()
                wires.copy(("fy", i, s), near, near, to_col).wait_send()
                wires.copy(("fz", i, s), far, far, to_col).wait_send()
        for s in range(2):
            near = place(RELAYED, 1 - r, c, s * STRIP, STRIP)
            wires.copy(("fy", RELAYED, s), near, near, to_col).wait_send()

    @pl.when(first)
    def _():
        share("s", early)
        spread_early()
        settle_sent()
        wires.arrived("cot", cr.at[1 - c], to_col)
        for part in range(PARTS):
            wires.arrived(("bwd", part), g2.at[pl.ds(part * PART, PART)], to_sec)
            rows = slice(part * PART, (part + 1) * PART)
            gof[rows, :] = g2[rows, :].astype(F32)

    def send_col(g):
        at = GROUPS[g][0][0]
        rows = pl.ds(at, GROUPS[g][-1][0] + GROUPS[g][-1][1] - at)
        wires.copy(("c0", g), gp.at[1 - r, 1 - c, rows], rc.at[1 - r, rows], to_col).start()
        wires.copy(("c1", g), gp.at[r, 1 - c, rows], rc.at[r, rows], to_col).start()

    def total(a, b):
        return (a.astype(F32) + b.astype(F32)).astype(BF16)

    def from_col(g):
        facing(g)
        settle(g)

    def facing(g):
        at = GROUPS[g][0][0]
        rows = pl.ds(at, GROUPS[g][-1][0] + GROUPS[g][-1][1] - at)
        wires.arrived(("c0", g), rc.at[1 - r, rows], to_col)
        for at, size in GROUPS[g]:
            chunk = pl.ds(at, size)
            t1[chunk, :] = total(gp[1 - r, c, chunk, :], rc[1 - r, chunk, :])
            wires.copy(("r", at), t1.at[chunk], rr.at[chunk], to_row).start()

    def settle(g):
        at = GROUPS[g][0][0]
        rows = pl.ds(at, GROUPS[g][-1][0] + GROUPS[g][-1][1] - at)
        wires.arrived(("c1", g), rc.at[r, rows], to_col)
        own1[rows, :] = total(gp[r, c, rows, :], rc[r, rows, :])

    zname = {0: "zi", 1: "zm"}

    roles = {
        name: [jnp.logical_and(which, kind) for kind in (not_inner, inner)]
        for name, which in (("outer", outer), ("rest", not_outer))
    }

    def send_in(k, cond, again=False):
        rows = pl.ds(*CHUNKS[k])
        for kind in range(2):
            say = roles[cond][kind]

            def make(kind=kind):
                return wires.copy((zname[kind], k), t2.at[rows], zz.at[kind, rows], to_in)

            if again:
                pl.when(say)(lambda make=make: make().start())
            else:
                wires.send_if(say, make)

    def from_row(k, again=False):
        rows = pl.ds(*CHUNKS[k])
        wires.arrived(("r", CHUNKS[k][0]), rr.at[rows], to_row)
        t2[rows, :] = total(own1[rows, :], rr[rows, :])
        send_in(k, "outer", again)

    def fold(k):
        rows = pl.ds(*CHUNKS[k])

        @pl.when(not_outer)
        def _():
            wires.arrived(("zi", k), zz.at[0, rows], to_out)
            t2[rows, :] = total(t2[rows, :], zz[0, rows, :])

        send_in(k, "rest")

    def send_back(k, cond):
        rows = pl.ds(*CHUNKS[k])
        wires.send_if(cond, lambda: wires.copy(("zo", k), res.at[rows], res.at[rows], to_out))

    def finish(k):
        rows = pl.ds(*CHUNKS[k])

        @pl.when(inner)
        def _():
            wires.arrived(("zm", k), zz.at[1, rows], to_in)
            res[rows, :] = total(t2[rows, :], zz[1, rows, :])

        send_back(k, jnp.logical_and(inner, not_outer))

    def last(k):
        rows = pl.ds(*CHUNKS[k])

        @pl.when(not_inner)
        def _():
            wires.arrived(("zo", k), res.at[rows], to_in)

        send_back(k, jnp.logical_and(not_inner, not_outer))

    def rows_of(half):
        return slice(half * HALF, (half + 1) * HALF)

    def send_part(g, which):
        q = r if which else 1 - r
        at = GROUPS[g][0][0]
        rows = pl.ds(at, GROUPS[g][-1][0] + GROUPS[g][-1][1] - at)
        wires.copy(("c" + str(which), g), gp.at[q, 1 - c, rows], rc.at[q, rows], to_col).start()

    def weight_down():
        back = gf[...].astype(F32).T.astype(BF16)
        for which in range(2):
            q = r if which else 1 - r
            for k in range(2):
                grad = dot(back, act[q, :, k * D : (k + 1) * D]).astype(BF16)
                for half in range(2):
                    gp[q, half, rows_of(k), :] = grad[rows_of(half), :]
                send_part(k, which)

    def weight_up():
        back = hidden2[...].astype(F32).T.astype(BF16)
        for k in range(2):
            for q in range(2):
                grad = dot(back, gpre[q, :, k * D : (k + 1) * D]).astype(BF16)
                for half in range(2):
                    gp[q, half, rows_of(2 + k), :] = grad[rows_of(half), :]
            send_col(2 + k)

    def weight_proj():
        for q in range(2):
            grad = dot_tn(attended[q], gra[...]).astype(BF16)
            for half in range(2):
                gp[q, half, ROWS_B:ROWS_T, HALF:] = grad[:, rows_of(half)]

    def sums_down():
        dmod[5:6, :] = col_sum(gof[...] * branch_f[...])
        biasg[0:1, :D] = col_sum(gf[...])
        for q in range(2):
            biasg[1:2, q * FFH : (q + 1) * FFH] = col_sum(gpre[q])

    def grad_down():
        for q in range(2):
            gpre[q] = (dot(gf[...], w2[q]) * slope[q]).astype(BF16)

    def grad_middle():
        grad_h2 = dot_nt(gpre[0], w1[0]) + dot_nt(gpre[1], w1[1])
        gh2[...] = grad_h2
        mid = gof[...] + norm_back(grad_h2 * (1.0 + m[4]), normed2[...], inv2[...])
        gm[...] = mid
        gra[...] = (mid * m[2]).astype(BF16)
        gatt[...] = dot_nt(gra[...], wp[...]).astype(BF16)

    def sums_middle():
        dmod[4:5, :] = col_sum(gh2[...] * normed2[...])
        dmod[3:4, :] = col_sum(gh2[...])
        dmod[2:3, :] = col_sum(gm[...] * branch_a[...])
        biasg[2:3, :D] = col_sum(gra[...])

    def attend_back(head):
        q, j = head // 3, head % 3
        query, key, val = parts_of(q, j)
        p = prob[head]
        g = gatt[:, head * HD : (head + 1) * HD]
        grad_prob = dot_nt(g, val)
        delta = jnp.sum(p * grad_prob, axis=-1, keepdims=True)
        gs = (p * (grad_prob - delta) * SCALE).astype(BF16)
        gqk[q, :, j * HD : (j + 1) * HD] = dot(gs, key).astype(BF16)
        gqk[q, :, HALF + j * HD : HALF + (j + 1) * HD] = dot_tn(gs, query).astype(BF16)
        gv[q, :, j * HD : (j + 1) * HD] = dot_tn(p.astype(BF16), g).astype(BF16)

    def grad_first():
        grad_h1 = dot_nt(gqk[0], wa[0]) + dot_nt(gqk[1], wa[1])
        gh1[...] = grad_h1 + dot_nt(gv[0], wb[0, :, :HALF]) + dot_nt(gv[1], wb[1, :, :HALF])

    def grad_input(part):
        rows = slice(part * PART, (part + 1) * PART)
        gin[rows, :] = gm[rows, :] + norm_back(gh1[rows, :] * (1.0 + m[1]), normed1[rows, :], inv1[rows, :])

    @pl.when(first)
    def _():
        gf[...] = (gof[...] * m[5]).astype(BF16)
        weight_down()
        facing(0)
        facing(1)
        grad_down()
        settle(0)
        settle(1)
        weight_up()
        sums_down()
        grad_middle()
        from_col(2)
        from_col(3)
        for head in range(6):
            attend_back(head)
        from_row(0)
        grad_first()
        weight_proj()
        from_row(1)

    @pl.when(second)
    def _():
        gf[...] = (gof[...] * m[5]).astype(BF16)
        grad_down()
        grad_middle()
        for head in range(6):
            attend_back(head)
        grad_first()
        for part in range(PARTS):
            rows = slice(part * PART, (part + 1) * PART)
            grad_input(part)
            gbuf[rows, :] = gin[rows, :].astype(BF16)
            there = pl.ds(part * PART, PART)
            wires.copy(("bwd", part), gbuf.at[there], g2.at[there], to_sec).start()
        settle_sent()
        weight_down()
        weight_up()
        sums_down()
        weight_proj()

    back = hidden1[...].astype(F32).T.astype(BF16)
    for q in range(2):
        grad = dot(back, gqk[q]).astype(BF16)
        for half in range(2):
            gp[q, half, ROWS_A:ROWS_B, :] = grad[rows_of(half), :]
    send_col(4)
    for q in range(2):
        grad = dot(back, gv[q]).astype(BF16)
        for half in range(2):
            gp[q, half, ROWS_B:ROWS_T, :HALF] = grad[rows_of(half), :]

    @pl.when(second)
    def _():
        from_col(0)
        from_col(1)

    sums_middle()
    zero = jnp.zeros((1, HALF), F32)
    for q in range(2):
        bqk, bv = col_sum(gqk[q]), col_sum(gv[q])
        for half in range(2):
            tail = [
                bqk,
                jnp.concatenate([bv, biasg[2:3, rows_of(half)]], axis=1),
                biasg[1:2, q * FFH : q * FFH + D],
                biasg[1:2, q * FFH + D : (q + 1) * FFH],
                jnp.concatenate([biasg[0:1, rows_of(half)], zero], axis=1),
                jnp.zeros((11, D), F32),
            ]
            gp[q, half, ROWS_T:GROWS, :] = jnp.concatenate(tail, axis=0).astype(BF16)
    send_col(5)

    @pl.when(second)
    def _():
        from_col(2)
        from_col(3)
        from_row(0, True)
        from_row(1, True)

    dmod[1:2, :] = col_sum(gh1[...] * normed1[...])
    dmod[0:1, :] = col_sum(gh1[...])
    for half in range(2):
        dm[2 + half, 0:6, :] = dmod[0:6, rows_of(half)]
        dm[2 + half, 6:8, :] = jnp.zeros((2, HALF), F32)
    wires.send("dm", dm.at[2 + 1 - c], dm.at[c], to_col)

    def send_input_grad():
        @pl.when(first)
        def _():
            for part in range(PARTS):
                grad_input(part)

        gint[...] = gin[...].T
        wires.send("gin", gint.at[their_feats], input_grad.at[:, own_lanes], to_col)
        input_grad[:, own_lanes] = gint[own_rows, :]

    pl.when(second)(send_out)

    def pull_part():
        wires.arrived("dm", dm.at[1 - c], to_col)
        dm[c] = dm[2 + c]
        part = jnp.zeros((2, D), F32)
        for i in range(6):
            low = jnp.concatenate([dm[0, i : i + 1, :], dm[1, i : i + 1, :]], axis=0).astype(BF16)
            part += dot(low, ada[i])
        pull[0] = jnp.concatenate([part, jnp.zeros((6, D), F32)], axis=0)
        wires.send("p0", pull.at[0], pull.at[1], to_col)

    def pull_section():
        wires.arrived("p0", pull.at[1], to_col)
        pull[2] = pull[0] + pull[1]
        wires.send("p1", pull.at[2], pull.at[3], to_sec)

    def fill_table():
        wires.arrived("p1", pull.at[3], to_sec)
        v = condb[...]
        sig = 1.0 / (1.0 + jnp.exp(-v))
        grad = (pull[2, 0:2, :] + pull[3, 0:2, :]) * (sig * (1.0 + v * (1.0 - sig)))
        cond_grad[...] = grad

        mods = jnp.concatenate([dm[0, 0:6, :], dm[1, 0:6, :]], axis=1)
        late[me] = jnp.concatenate([grad, mods], axis=0)
        share("t", late)

    def spread_late():
        shared("t", late, True)
        rows = [late[i] for i in range(places)]
        grads = jnp.concatenate([v[0:2] for v in rows], axis=0)
        high = grads.astype(BF16)
        rest = grads - high.astype(F32)
        mid = rest.astype(BF16)
        g3[...] = jnp.concatenate([high.astype(F32), mid.astype(F32), rest - mid.astype(F32)], axis=0).astype(BF16)
        summed = functools.reduce(lambda v, w: v + w, rows)
        for i in range(6):
            adab_sum[i] = summed[2 + i : 3 + i, :HALF] + summed[2 + i : 3 + i, HALF:]
            parts = []
            for v in rows:
                parts += [v[2 + i : 3 + i, :HALF], v[2 + i : 3 + i, HALF:]]
            dm16[i] = jnp.concatenate(parts, axis=0).astype(BF16)

    small = {2: pull_part, 5: pull_section, 9: fill_table}
    def settle_chunks():
        for g, group in enumerate(GROUPS):
            rows = pl.ds(group[0][0], group[-1][0] + group[-1][1] - group[0][0])
            wires.copy(("c0", g), gp.at[1 - r, 1 - c, rows], rc.at[1 - r, rows], to_col).wait_send()
            wires.copy(("c1", g), gp.at[r, 1 - c, rows], rc.at[r, rows], to_col).wait_send()
            for at, size in group:
                chunk = pl.ds(at, size)
                wires.copy(("r", at), t1.at[chunk], rr.at[chunk], to_row).wait_send()

    count = len(CHUNKS)
    for tick in range(count + LAGS[1]):
        if tick < 2:
            from_col(4 + tick)
        if tick == 4:
            send_input_grad()
        for lag, step in ((0, from_row), (LAGS[0], fold), (LAGS[1], finish)):
            if (2 if step is from_row else 0) <= tick - lag < count:
                step(tick - lag)
        if tick in small:
            small[tick]()
    spread_late()
    settle_chunks()
    wires.copy("out", outt.at[their_feats], block_out.at[:, own_lanes], to_col).wait_send()
    for name, src, dst, which in (("fwd", obuf, x2, first), ("bwd", gbuf, g2, second)):

        @pl.when(which)
        def _():
            for part in range(PARTS):
                there = pl.ds(part * PART, PART)
                wires.copy((name, part), src.at[there], dst.at[there], to_sec).wait_send()

    for k in range(count):
        last(k)
    wires.arrived("out", block_out.at[:, their_lanes], to_col)
    wires.arrived("gin", input_grad.at[:, their_lanes], to_col)
    shared("t", late, False)
    wires.settle(wires.take())


def last_kernel(
    res, block_in, grad_in, cond_in, dm16, silu16, adab_in, g3, ids,
    block_out, input_grad, label_out, time_out, ada_out, qkv_out, proj_out, fc1_out, fc2_out,
    cond_out, adab_out, qb_out, pb_out, b1_out, b2_out,
    g_label, g_time, g_ada, g_qkv, g_proj, g_fc1, g_fc2, g_qb, g_pb, g_b1, g_b2, sem,
):
    copies = []

    def move(src, dst):
        copy = pltpu.make_async_copy(src, dst, sem.at[len(copies)])
        copy.start()
        copies.append(copy)

    move(grad_in, input_grad)
    move(block_in, block_out)
    move(cond_in, cond_out)
    move(adab_in, adab_out)
    for k in range(2):
        g_fc2[:, k * D : (k + 1) * D] = res[k * HALF : (k + 1) * HALF, :].astype(F32)
    move(g_fc2, fc2_out)
    for k in range(2):
        g_fc1[:, k * D : (k + 1) * D] = res[(2 + k) * HALF : (3 + k) * HALF, :].astype(F32)
    move(g_fc1, fc1_out)
    for i in range(6):
        g_ada[i] = dot_tn(dm16[i], silu16[...])
    move(g_ada, ada_out)
    count = g3.shape[0] // 3
    for which, held, out in ((0, g_label, label_out), (1, g_time, time_out)):
        one = ids[which][:, :1]
        wide = (count, out.shape[0])
        hot = jnp.where(lax.broadcasted_iota(jnp.int32, wide, 1).astype(F32) == one, 1.0, 0.0).astype(BF16)
        held[...] = dot_tn(jnp.concatenate([hot, hot, hot], axis=0), g3[...])
        move(held, out)
    low = res[ROWS_A:ROWS_B, :].astype(F32)
    g_qkv[0] = low[:, :HALF]
    g_qkv[1] = low[:, HALF:]
    low = res[ROWS_B:ROWS_T, :].astype(F32)
    g_qkv[2] = low[:, :HALF]
    move(g_qkv, qkv_out)
    g_proj[...] = low[:, HALF:]
    move(g_proj, proj_out)
    tail = res[ROWS_T:GROWS, :].astype(F32)
    g_qb[0] = tail[0:1, :HALF]
    g_qb[1] = tail[0:1, HALF:]
    g_qb[2] = tail[1:2, :HALF]
    g_pb[...] = tail[1:2, HALF:]
    g_b1[:, :D] = tail[2:3, :]
    g_b1[:, D:] = tail[3:4, :]
    g_b2[...] = tail[4:5, :HALF]
    for held, out in ((g_qb, qb_out), (g_pb, pb_out), (g_b1, b1_out), (g_b2, b2_out)):
        move(held, out)
    for copy in copies:
        copy.wait()


def on_device(
    latents_in, labels, timesteps, out_grad, label_table, time_table, ada_w, ada_b,
    qkv_w, qkv_b, proj_w, proj_b, fc1_w, fc1_b, fc2_w, fc2_b,
):
    own = latents_in.shape[0] // SEQ
    dp = lax.axis_size("dp")
    places = dp * lax.axis_size("row")
    bits = dp.bit_length() - 1
    latents = places * own
    vmem, hbm = pl.BlockSpec(memory_space=pltpu.VMEM), pl.BlockSpec(memory_space=pltpu.HBM)
    args = (
        latents_in.T,
        labels,
        timesteps,
        out_grad.T,
        label_table,
        time_table,
        jnp.transpose(ada_w[0], (1, 2, 0)),
        jnp.transpose(ada_b, (1, 0, 2)),
        jnp.transpose(qkv_w[0], (1, 0, 2)),
        jnp.transpose(qkv_b, (1, 0, 2)),
        proj_w[0],
        proj_b,
        fc1_w[0],
        fc1_b,
        fc2_w[0].T,
        fc2_b,
    )
    outs = [
        ((GROWS, D), BF16),
        ((HALF, own * SEQ), BF16),
        ((HALF, own * SEQ), F32),
        ((own, D), F32),
        ((6, latents, HALF), BF16),
        ((latents, D), BF16),
        ((6, 1, HALF), F32),
        ((3 * latents, D), BF16),
        ((2, latents, D), F32),
    ]
    scratch = [
        ((6, 1, HALF), F32),
        ((3, HALF, HALF), BF16),
        ((3, 1, HALF), F32),
        ((HALF, HALF), BF16),
        ((1, HALF), F32),
        ((1, FFH), F32),
        ((1, HALF), F32),
        (label_table.shape, BF16),
        (time_table.shape, BF16),
        ((6, HALF, D), BF16),
        ((2, HALF, SEQ), BF16),
        ((2, HALF, SEQ), BF16),
        ((4, 8, HALF), F32),
        ((8, D), F32),
        ((4, 8, D), F32),
        ((2, HALF, D), BF16),
        ((2, D, D), BF16),
        ((2, D, D), BF16),
        ((D, D), BF16),
        ((2, D, FFH), BF16),
        ((2, D, FFH), BF16),
        ((SEQ, D), F32),
        ((SEQ, D), F32),
        ((SEQ, D), BF16),
        ((SEQ, D), BF16),
        ((SEQ, D), BF16),
        ((SEQ, D), BF16),
        ((SEQ, D), F32),
        ((SEQ, 1), F32),
        ((SEQ, 1), F32),
        ((SEQ, D), F32),
        ((SEQ, D), F32),
        ((SEQ, D), F32),
        ((SEQ, D), F32),
        ((SEQ, D), F32),
        ((SEQ, D), F32),
        ((SEQ, D), F32),
        ((SEQ, D), BF16),
        ((SEQ, D), BF16),
        ((2, SEQ, D), BF16),
        ((2, SEQ, HALF), BF16),
        ((6, SEQ, SEQ), F32),
        ((2, SEQ, HALF), BF16),
        ((2, SEQ, FFH), BF16),
        ((2, SEQ, FFH), F32),
        ((SEQ, D), BF16),
        ((2, SEQ, FFH), BF16),
        ((SEQ, D), BF16),
        ((SEQ, D), BF16),
        ((2, SEQ, D), BF16),
        ((2, SEQ, HALF), BF16),
        ((D, SEQ), BF16),
        ((D, SEQ), F32),
        ((2, 2, GROWS, D), BF16),
        ((2, GROWS, D), BF16),
        ((GROWS, D), BF16),
        ((GROWS, D), BF16),
        ((GROWS, D), BF16),
        ((GROWS, D), BF16),
        ((2, GROWS, D), BF16),
        ((8, D), F32),
        ((4, 8, HALF), F32),
        ((4, 8, D), F32),
        ((places, 8, D), F32),
        ((places, 8, D), F32),
        ((own, D), F32),
        ((8, FF), F32),
    ]
    wires = 64 + 2 * len(GROUPS) + 4 * len(CHUNKS) + 2 * places
    made = pl.pallas_call(
        functools.partial(main_kernel, bits, dp),
        out_shape=[jax.ShapeDtypeStruct(s, d) for s, d in outs],
        in_specs=[hbm] * len(args),
        out_specs=[vmem] * len(outs),
        scratch_shapes=[pltpu.SMEM((own,), jnp.int32)] * 2
        + [pltpu.VMEM(s, d) for s, d in scratch]
        + [pltpu.SemaphoreType.DMA((wires,)), pltpu.SemaphoreType.DMA((wires,)), pltpu.SemaphoreType.DMA((16,))],
        compiler_params=pltpu.CompilerParams(
            vmem_limit_bytes=46 * 1024 * 1024, collective_id=0, has_side_effects=True
        ),
    )(*[pltpu.with_memory_space_constraint(a, pltpu.HBM) for a in args])
    big = [
        ((HALF, own * SEQ), BF16),
        ((HALF, own * SEQ), F32),
        (label_table.shape, F32),
        (time_table.shape, F32),
        ((6, HALF, D), F32),
        ((3, HALF, HALF), F32),
        ((HALF, HALF), F32),
        ((HALF, FFH), F32),
        ((HALF, FFH), F32),
    ]
    little = [
        ((own, D), F32),
        ((6, 1, HALF), F32),
        ((3, 1, HALF), F32),
        ((1, HALF), F32),
        ((1, FFH), F32),
        ((1, HALF), F32),
    ]
    (
        block_outs, input_grads, g_label, g_time, g_ada, g_qkv, g_proj, g_fc1, g_fc2,
        cond_grad, g_adab, g_qb, g_pb, g_b1, g_b2,
    ) = pl.pallas_call(
        last_kernel,
        out_shape=[jax.ShapeDtypeStruct(s, d) for s, d in big + little],
        in_specs=[vmem] * len(made),
        out_specs=[hbm] * len(big + little),
        scratch_shapes=[pltpu.VMEM(s, d) for s, d in big[2:] + little[2:]]
        + [pltpu.SemaphoreType.DMA((len(big + little),))],
        compiler_params=pltpu.CompilerParams(vmem_limit_bytes=46 * 1024 * 1024),
    )(*made)
    return (
        block_outs.T[None],
        input_grads.T[None],
        cond_grad,
        g_label,
        g_time,
        jnp.transpose(g_ada, (2, 0, 1))[None],
        jnp.transpose(g_adab, (1, 0, 2)),
        jnp.transpose(g_qkv, (1, 0, 2))[None],
        jnp.transpose(g_qb, (1, 0, 2)),
        g_proj[None],
        g_pb,
        g_fc1[None],
        g_b1,
        g_fc2.T[None],
        g_b2,
    )


def solution(mesh):
    return jax.shard_map(
        on_device,
        mesh=mesh,
        in_specs=(
            P(("dp", "row"), "col"),
            P(("dp", "row")),
            P(("dp", "row")),
            P(("dp", "row"), "col"),
            P(),
            P(),
            P("section", None, None, "col"),
            P("section", None, "col"),
            P("section", "col", None, "row"),
            P("section", None, "row"),
            P("section", "row", "col"),
            P("section", "col"),
            P("section", "col", "row"),
            P("section", "row"),
            P("section", "row", "col"),
            P("section", "col"),
        ),
        out_specs=(
            P("section", ("dp", "row"), "col"),
            P("section", ("dp", "row"), "col"),
            P(("dp", "row"), None),
            P(),
            P(),
            P("section", None, None, "col"),
            P("section", None, "col"),
            P("section", "col", None, "row"),
            P("section", None, "row"),
            P("section", "row", "col"),
            P("section", "col"),
            P("section", "col", "row"),
            P("section", "row"),
            P("section", "row", "col"),
            P("section", "col"),
        ),
        check_vma=False,
    )
```

```python
import functools
import math

import jax
import jax.numpy as jnp
from jax import lax
from jax.experimental import pallas as pl
from jax.experimental.pallas import tpu as pltpu
from jax.sharding import PartitionSpec as P

D = 384
HALF = D // 2
HD = 64
FF = 1536
FFH = FF // 2
SEQ = 256
EPS = 1e-06
SCALE = 1.0 / math.sqrt(HD)
SOFT = SCALE * math.log2(math.e)
MESH = pl.DeviceIdType.MESH
F32 = jnp.float32
BF16 = jnp.bfloat16

ROWS_A, ROWS_B, ROWS_T = 4 * HALF, 5 * HALF, 6 * HALF
GROWS = ROWS_T + 16
GROUPS = (
    ((0, 96), (96, 96)),
    ((192, 96), (288, 96)),
    ((384, 96), (480, 96)),
    ((576, 96), (672, 96)),
    ((768, 64), (832, 64), (896, 64)),
    ((960, 64), (1024, 48), (1072, 48), (1120, 32), (1152, 16)),
)
CHUNKS = tuple(chunk for group in GROUPS for chunk in group)
LAGS = (3, 6)
PIECES = 6
RELAYED = 5
STRIP = HALF // 2
STRIPS = {i: ((0, STRIP),) if i < 4 else ((0, STRIP // 2), (STRIP // 2, STRIP // 2)) for i in range(RELAYED)}
PARTS = 4
PART = SEQ // PARTS


def dot(a, b):
    return jnp.dot(a, b, preferred_element_type=F32)


def dot_nt(a, b):
    return lax.dot_general(a, b, (((1,), (1,)), ((), ())), preferred_element_type=F32)


def dot_tn(a, b):
    return lax.dot_general(a, b, (((0,), (0,)), ((), ())), preferred_element_type=F32)


def norm_rows(v):
    mean_val = jnp.mean(v, axis=-1, keepdims=True)
    cen = v - mean_val
    inv = lax.rsqrt(jnp.mean(cen * cen, axis=-1, keepdims=True) + EPS)
    return cen * inv, inv


def norm_back(g, normed, inv):
    return inv * (
        g
        - jnp.mean(g, axis=-1, keepdims=True)
        - normed * jnp.mean(g * normed, axis=-1, keepdims=True)
    )


C0 = math.sqrt(2.0 / math.pi)
C1 = 0.044715 * C0


def gelu_and_slope(v):
    u = v * v
    p = 0.5 + 0.5 * jnp.tanh(v * (C0 + C1 * u))
    act = v * p
    return act, p + act * (1.0 - p) * (2.0 * C0 + (6.0 * C1) * u)


def col_sum(v):
    return jnp.sum(v.astype(F32), axis=0, keepdims=True)


def flipped(index, step):
    return index + step * (1 - 2 * lax.rem(index // step, 2))


def align(index, size):
    return pl.multiple_of(index * size, size)


class Wires:
    def __init__(self, send_sem, recv_sem):
        self.send_sem, self.recv_sem = send_sem, recv_sem
        self.number, self.started = {}, []

    def index(self, name):
        return self.number.setdefault(name, len(self.number))

    def copy(self, name, src, dst, where):
        k = self.index(name)
        return pltpu.make_async_remote_copy(
            src_ref=src,
            dst_ref=dst,
            send_sem=self.send_sem.at[k],
            recv_sem=self.recv_sem.at[k],
            device_id=where,
            device_id_type=MESH,
        )

    def send(self, name, src, dst, where):
        self.copy(name, src, dst, where).start()
        self.started.append((lambda: self.copy(name, src, dst, where), None))

    def send_if(self, cond, make):
        pl.when(cond)(lambda: make().start())
        self.started.append((make, cond))

    def arrived(self, name, dst, where):
        self.copy(name, dst, dst, where).wait_recv()

    def take(self):
        taken, self.started = self.started, []
        return taken

    def settle(self, started):
        for make, cond in started:

            def wait(make=make):
                make().wait_send()

            if cond is None:
                wait()
            else:
                pl.when(cond)(wait)


def main_kernel(
    bits, dp,
    lat, labels_in, times_in, cot, ltab_in, ttab_in, ada_in, adab_in, qkv_in, qb_in, proj_in, pb_in, fc1, b1_in, fc2, b2_in,
    res, block_out, input_grad, cond_grad, dm16, silu16, adab_sum, g3, ids,
    labels, times, adab, qkv, qb, proj, pb, b1, b2, ltab, ttab, ada, xr, cr, modbuf, mod, ball, sh, wa, wb, wp, w1, w2, xf, gof, x2, g2, obuf, gbuf,
    normed1, inv1, inv2, normed2, gh1, gh2, gm, gin, branch_a, branch_f, hidden1, hidden2, pqk, pv, prob, attended, act, slope,
    gf, gft, gpre, gra, gatt, gqk, gv, outt, gint, gp, rc, t1, own1, rr, t2, zz, dmod, dm, pull, early, late, condb, biasg,
    send_sem, recv_sem, local_sem,
):
    r, c, z = lax.axis_index("row"), lax.axis_index("col"), lax.axis_index("dp")
    sec = lax.axis_index("section")
    h = lax.rem(z, 2)
    to_col, to_row, to_sec = {"col": 1 - c}, {"row": 1 - r}, {"section": 1 - sec}
    to_dp = [{"dp": flipped(z, 1 << j)} for j in range(bits)]
    middle_at = dp // 2
    left = jnp.where(z < middle_at, 1, 0)
    outer = jnp.logical_or(z == 0, z == dp - 1)
    inner = jnp.logical_or(z == middle_at - 1, z == middle_at)
    to_in = {"dp": z + 2 * left - 1}
    to_out = {"dp": jnp.where(outer, dp - 1 - z, z + 1 - 2 * left)}
    not_outer, not_inner = jnp.logical_not(outer), jnp.logical_not(inner)
    first, second = sec == 0, sec == 1

    barrier = pltpu.get_barrier_semaphore()
    me = 2 * z + r
    places = early.shape[0]
    others = [lax.rem(me + step, places) for step in range(1, places)]
    homes = [{"dp": other // 2, "row": lax.rem(other, 2)} for other in others]
    greeted = [to_col, to_sec, *homes]
    for where in greeted:
        pl.semaphore_signal(barrier, inc=1, device_id=where, device_id_type=MESH)

    def place(i, pr, pc, at, size):
        rows = pl.ds(pl.multiple_of(pc * HALF + at, 16), size)
        if i < 2:
            return (wa, wb)[i].at[pr, rows]
        return (w1 if i < 4 else w2).at[pr, rows, pl.ds((i % 2) * D, D)]

    own_lanes = pl.ds(align(c, SEQ), SEQ)
    their_lanes = pl.ds(align(1 - c, SEQ), SEQ)
    own_rows = pl.ds(align(c, HALF), HALF)
    local = []

    def bring(src, dst):
        copy = pltpu.make_async_copy(src, dst, local_sem.at[len(local)])
        copy.start()
        local.append(copy)

    for src, dst in (
        (qkv_in, qkv), (proj_in, proj), (qb_in, qb), (pb_in, pb), (b1_in, b1), (b2_in, b2),
        (labels_in, labels), (times_in, times), (adab_in, adab), (ltab_in, ltab), (ttab_in, ttab),
    ):
        bring(src, dst)
    bring(ada_in, ada)
    bring(lat.at[:, own_lanes], xr.at[c])
    bring(cot.at[:, own_lanes], cr.at[c])
    bring(fc1, w1.at[r, own_rows])
    bring(fc2, w2.at[r, own_rows])

    for copy in local[:6]:
        copy.wait()
    sh[0, :, :HALF] = qkv[0]
    sh[0, :, HALF:] = qkv[1]
    sh[1, :, :HALF] = qkv[2]
    sh[1, :, HALF:] = proj[...]
    own_bias = 2 * r + c
    ball[own_bias] = jnp.zeros((8, D), F32)
    ball[own_bias, 0:1, :HALF] = qb[0]
    ball[own_bias, 0:1, HALF:] = qb[1]
    ball[own_bias, 1:2, :HALF] = qb[2]
    ball[own_bias, 1:2, HALF:] = pb[...]
    ball[own_bias, 2:3, :] = b1[:, :D]
    ball[own_bias, 3:4, :] = b1[:, D:]
    ball[own_bias, 4:5, :HALF] = b2[...]

    pl.semaphore_wait(barrier, len(greeted))
    wires = Wires(send_sem, recv_sem)

    def source(i, at, size):
        rows = pl.ds(at, size)
        if i < 2:
            return sh.at[i, rows]
        return (fc1 if i < 4 else fc2).at[rows, pl.ds((i % 2) * D, D)]

    def strip(half, at):
        return pl.multiple_of(half * STRIP + at, 16)

    for i in range(RELAYED):
        for s, (at, size) in enumerate(STRIPS[i]):
            here = strip(h, at)
            wires.send(("y", i, s), source(i, here, size), place(i, r, c, here, size), to_row)
        if i == 0:
            wires.send("x", lat.at[:, their_lanes], xr.at[c], to_col)
            wires.send("bias col", ball.at[own_bias], ball.at[own_bias], to_col)
            for k in range(2):
                wires.send(("own", k), source(k, 0, HALF), place(k, r, c, 0, HALF), to_col)
            wires.send("bias row", ball.at[own_bias], ball.at[own_bias], to_row)
    for s in range(2):
        wires.send(("y", RELAYED, s), source(RELAYED, s * STRIP, STRIP), place(RELAYED, r, c, s * STRIP, STRIP), to_row)
    for k in range(2, PIECES):
        wires.send(("own", k), source(k, 0, HALF), place(k, r, c, 0, HALF), to_col)
    wires.send("cot", cot.at[:, their_lanes], cr.at[c], to_col)
    wa[r, own_rows] = sh[0]
    wb[r, own_rows] = sh[1]
    for copy in local[6:]:
        copy.wait()

    def hot(ids_ref, table_ref):
        wide = (2, table_ref.shape[0])
        wanted = jnp.where(lax.broadcasted_iota(jnp.int32, wide, 0) == 0, ids_ref[0], ids_ref[1])
        return dot(jnp.where(lax.broadcasted_iota(jnp.int32, wide, 1) == wanted, 1.0, 0.0).astype(BF16), table_ref[...])

    cond = hot(labels, ltab) + hot(times, ttab)
    condb[...] = cond
    silu_low = (cond / (1.0 + jnp.exp(-cond))).astype(BF16)
    modbuf[0:2] = jnp.zeros((2, 8, HALF), F32)
    for i in range(6):
        part = dot_nt(silu_low, ada[i]) + adab[i]
        for latent in range(2):
            modbuf[latent, i : i + 1, :] = part[latent : latent + 1, :]
    wires.send("mod", modbuf.at[1 - c], modbuf.at[2 + c], to_col)
    modbuf[2 + c] = modbuf[c]

    def y_step(i, s=0):
        if i < RELAYED:
            at, size = STRIPS[i][s]
            here = place(i, 1 - r, c, strip(h, at), size)
        else:
            here = place(i, 1 - r, c, s * STRIP, STRIP)
        wires.arrived(("y", i, s), here, to_row)
        if i < RELAYED:
            wires.copy(("z", i, s), here, here, to_dp[0]).start()
        wires.copy(("fy", i, s), here, here, to_col).start()

    def z_step(i, s=0):
        at, size = STRIPS[i][s]
        here = place(i, 1 - r, c, strip(1 - h, at), size)
        wires.arrived(("z", i, s), here, to_dp[0])
        wires.copy(("fz", i, s), here, here, to_col).start()

    def ready_own(i):
        wires.arrived(("own", i), place(i, r, 1 - c, 0, HALF), to_col)

    def ready_other(i):
        if i < RELAYED:
            for s, (at, size) in enumerate(STRIPS[i]):
                wires.arrived(("fy", i, s), place(i, 1 - r, 1 - c, strip(h, at), size), to_col)
                wires.arrived(("fz", i, s), place(i, 1 - r, 1 - c, strip(1 - h, at), size), to_col)
        else:
            for s in range(2):
                wires.arrived(("fy", i, s), place(i, 1 - r, 1 - c, s * STRIP, STRIP), to_col)

    def ids_of(ref):
        wanted = jnp.where(lax.broadcasted_iota(jnp.int32, (2, D), 0) == 0, ref[0], ref[1])
        return wanted.astype(F32)

    def share(name, table):
        for step, home in enumerate(homes):
            wires.copy((name, step), table.at[me], table.at[me], home).start()

    def shared(name, table, wait):
        for step in range(places - 1):
            other = lax.rem(me + places - 1 - step, places)
            copy = wires.copy((name, step), table.at[other], table.at[other], homes[step])
            copy.wait_recv() if wait else copy.wait_send()

    def spread_early():
        shared("s", early, True)
        rows = [early[i] for i in range(places)]
        silu16[...] = jnp.concatenate([v[0:2] for v in rows], axis=0).astype(BF16)
        for which in range(2):
            ids[which] = jnp.concatenate([v[2 + 2 * which : 4 + 2 * which] for v in rows], axis=0)

    early[me] = jnp.concatenate([silu_low.astype(F32), ids_of(labels), ids_of(times), jnp.zeros((2, D), F32)], axis=0)

    wires.arrived("x", xr.at[1 - c], to_col)
    wires.arrived("bias col", ball.at[2 * r + 1 - c], to_col)
    for k in range(2):
        ready_own(k)

    @pl.when(first)
    def _():
        xf[...] = jnp.concatenate([xr[0].astype(F32).T, xr[1].astype(F32).T], axis=1)

    wires.arrived("mod", modbuf.at[2 + 1 - c], to_col)
    for half in range(2):
        mod[:, half * HALF : (half + 1) * HALF] = modbuf[2 + half]
    wires.arrived("bias row", ball.at[2 * (1 - r) + c], to_row)

    @pl.when(second)
    def _():
        wires.arrived("cot", cr.at[1 - c], to_col)
        gof[...] = jnp.concatenate([cr[0].astype(F32).T, cr[1].astype(F32).T], axis=1)
        for kind, i, s in (
            (y_step, 0, 0), (y_step, 1, 0), (y_step, 2, 0), (z_step, 0, 0), (y_step, 3, 0), (z_step, 1, 0),
            (y_step, 4, 0), (y_step, 4, 1), (z_step, 2, 0), (z_step, 3, 0), (y_step, 5, 0), (z_step, 4, 0),
            (z_step, 4, 1), (y_step, 5, 1),
        ):
            kind(i, s)
        for i in range(PIECES):
            ready_other(i)
        share("s", early)
        spread_early()

    m = [mod[i : i + 1, :] for i in range(6)]

    def norm_one(part):
        rows = slice(part * PART, (part + 1) * PART)
        n1, inv1[rows, :] = norm_rows(xf[rows, :])
        normed1[rows, :] = n1
        hidden1[rows, :] = (n1 * (1.0 + m[1]) + m[0]).astype(BF16)

    def query_key(q, rows=slice(None)):
        pqk[q, rows, :] = (dot(hidden1[rows, :], wa[q]) + ball[2 * q + c, 0:1, :]).astype(BF16)

    def value(q, rows=slice(None)):
        pv[q, rows, :] = (dot(hidden1[rows, :], wb[q, :, :HALF]) + ball[2 * q + c, 1:2, :HALF]).astype(BF16)

    def parts_of(q, j):
        return pqk[q, :, j * HD : (j + 1) * HD], pqk[q, :, HALF + j * HD : HALF + (j + 1) * HD], pv[q, :, j * HD : (j + 1) * HD]

    def attend(q, j):
        query, key, val = parts_of(q, j)
        s = dot_nt(query, key)
        e = jnp.exp2((s - jnp.max(s, axis=-1, keepdims=True)) * SOFT)
        p = e * (1.0 / jnp.sum(e, axis=-1, keepdims=True))
        prob[3 * q + j] = p
        attended[q, :, j * HD : (j + 1) * HD] = dot(p.astype(BF16), val).astype(BF16)

    def whole_proj():
        for q in range(2):
            for half in range(2):
                rows = slice(half * HALF, (half + 1) * HALF)
                wp[q * HALF : (q + 1) * HALF, rows] = wb[q, rows, HALF:]

    def middle():
        ba = dot(attended[0], wp[:HALF]) + dot(attended[1], wp[HALF:])
        ba += jnp.concatenate([ball[2 * r, 1:2, HALF:], ball[2 * r + 1, 1:2, HALF:]], axis=1)
        branch_a[...] = ba
        mid = xf[...] + m[2] * ba
        n2, inv2[...] = norm_rows(mid)
        xf[...] = mid
        normed2[...] = n2
        hidden2[...] = (n2 * (1.0 + m[4]) + m[3]).astype(BF16)

    def up(q):
        bias = jnp.concatenate([ball[2 * q + c, 2:3, :], ball[2 * q + c, 3:4, :]], axis=1)
        a, sl = gelu_and_slope(dot(hidden2[...], w1[q]) + bias)
        act[q] = a.astype(BF16)
        slope[q] = sl

    def down_start(q):
        bias = jnp.concatenate([ball[2 * r, 4:5, :HALF], ball[2 * r + 1, 4:5, :HALF]], axis=1)
        branch_f[...] = dot_nt(act[q], w2[q]) + bias

    def down_end(q, part):
        rows = slice(part * 128, (part + 1) * 128)
        bf = branch_f[rows, :] + dot_nt(act[q, rows, :], w2[q])
        branch_f[rows, :] = bf
        obuf[rows, :] = (xf[rows, :] + m[5] * bf).astype(BF16)

    @pl.when(first)
    def _():
        for part in range(PARTS):
            norm_one(part)
        query_key(r)
        value(r)
        y_step(0)
        attend(r, 0)
        attend(r, 1)
        y_step(1)
        attend(r, 2)
        y_step(2)
        z_step(0)
        ready_other(0)
        query_key(1 - r)
        y_step(3)
        z_step(1)
        ready_other(1)
        value(1 - r)
        whole_proj()
        y_step(4, 0)
        attend(1 - r, 0)
        y_step(4, 1)
        attend(1 - r, 1)
        z_step(2)
        attend(1 - r, 2)
        middle()
        for k in range(2, PIECES):
            ready_own(k)
        up(r)
        z_step(3)
        y_step(5, 0)
        z_step(4, 0)
        ready_other(2)
        ready_other(3)
        up(1 - r)
        down_start(r)
        y_step(5, 1)
        z_step(4, 1)
        ready_other(4)
        ready_other(5)
        for part in range(2):
            down_end(1 - r, part)
            for sub in range(2):
                there = pl.ds((2 * part + sub) * PART, PART)
                wires.copy(("fwd", 2 * part + sub), obuf.at[there], x2.at[there], to_sec).start()

    @pl.when(second)
    def _():
        whole_proj()
        for k in range(2, PIECES):
            ready_own(k)
        for part in range(PARTS):
            rows = slice(part * PART, (part + 1) * PART)
            wires.arrived(("fwd", part), x2.at[pl.ds(part * PART, PART)], to_sec)
            xf[rows, :] = x2[rows, :].astype(F32)
            norm_one(part)
            if part % 2 == 1:
                side = slice((part // 2) * 128, (part // 2 + 1) * 128)
                for q in range(2):
                    query_key(q, side)
                    value(q, side)
        for head in range(6):
            attend(head // 3, head % 3)
        middle()
        for q in range(2):
            up(q)
        down_start(0)
        for part in range(2):
            down_end(1, part)

    their_feats = pl.ds(align(1 - c, HALF), HALF)

    def send_out():
        outt[...] = obuf[...].astype(F32).T.astype(BF16)
        wires.copy("out", outt.at[their_feats], block_out.at[:, own_lanes], to_col).start()
        block_out[:, own_lanes] = outt[own_rows, :]

    pl.when(first)(send_out)
    sent_early = wires.take()

    def settle_sent():
        wires.settle(sent_early)
        shared("s", early, False)
        for i in range(RELAYED):
            for s, (at, size) in enumerate(STRIPS[i]):
                near = place(i, 1 - r, c, strip(h, at), size)
                far = place(i, 1 - r, c, strip(1 - h, at), size)
                wires.copy(("z", i, s), near, near, to_dp[0]).wait_send()
                wires.copy(("fy", i, s), near, near, to_col).wait_send()
                wires.copy(("fz", i, s), far, far, to_col).wait_send()
        for s in range(2):
            near = place(RELAYED, 1 - r, c, s * STRIP, STRIP)
            wires.copy(("fy", RELAYED, s), near, near, to_col).wait_send()
    def turn_down(side):
        rows = slice(side * 128, (side + 1) * 128)
        gft[:, rows] = gf[rows, :].astype(F32).T.astype(BF16)


    @pl.when(first)
    def _():
        share("s", early)
        spread_early()
        settle_sent()
        wires.arrived("cot", cr.at[1 - c], to_col)
        for part in range(PARTS):
            wires.arrived(("bwd", part), g2.at[pl.ds(part * PART, PART)], to_sec)
            rows = slice(part * PART, (part + 1) * PART)
            gof[rows, :] = g2[rows, :].astype(F32)
            gf[rows, :] = (gof[rows, :] * m[5]).astype(BF16)
            if part % 2 == 1:
                turn_down(part // 2)

    def send_col(g):
        at = GROUPS[g][0][0]
        rows = pl.ds(at, GROUPS[g][-1][0] + GROUPS[g][-1][1] - at)
        wires.copy(("c0", g), gp.at[1 - r, 1 - c, rows], rc.at[1 - r, rows], to_col).start()
        wires.copy(("c1", g), gp.at[r, 1 - c, rows], rc.at[r, rows], to_col).start()

    def total(a, b):
        return (a.astype(F32) + b.astype(F32)).astype(BF16)

    def from_col(g):
        facing(g)
        settle(g)

    def facing(g):
        at = GROUPS[g][0][0]
        rows = pl.ds(at, GROUPS[g][-1][0] + GROUPS[g][-1][1] - at)
        wires.arrived(("c0", g), rc.at[1 - r, rows], to_col)
        for at, size in GROUPS[g]:
            chunk = pl.ds(at, size)
            t1[chunk, :] = total(gp[1 - r, c, chunk, :], rc[1 - r, chunk, :])
            wires.copy(("r", at), t1.at[chunk], rr.at[chunk], to_row).start()

    def settle(g):
        at = GROUPS[g][0][0]
        rows = pl.ds(at, GROUPS[g][-1][0] + GROUPS[g][-1][1] - at)
        wires.arrived(("c1", g), rc.at[r, rows], to_col)
        own1[rows, :] = total(gp[r, c, rows, :], rc[r, rows, :])

    zname = {0: "zi", 1: "zm"}

    roles = {
        name: [jnp.logical_and(which, kind) for kind in (not_inner, inner)]
        for name, which in (("outer", outer), ("rest", not_outer))
    }

    def send_in(k, cond, again=False):
        rows = pl.ds(*CHUNKS[k])
        for kind in range(2):
            say = roles[cond][kind]

            def make(kind=kind):
                return wires.copy((zname[kind], k), t2.at[rows], zz.at[kind, rows], to_in)

            if again:
                pl.when(say)(lambda make=make: make().start())
            else:
                wires.send_if(say, make)

    def from_row(k, again=False):
        rows = pl.ds(*CHUNKS[k])
        wires.arrived(("r", CHUNKS[k][0]), rr.at[rows], to_row)
        t2[rows, :] = total(own1[rows, :], rr[rows, :])
        send_in(k, "outer", again)

    def fold(k):
        rows = pl.ds(*CHUNKS[k])

        @pl.when(not_outer)
        def _():
            wires.arrived(("zi", k), zz.at[0, rows], to_out)
            t2[rows, :] = total(t2[rows, :], zz[0, rows, :])

        send_in(k, "rest")

    def send_back(k, cond):
        rows = pl.ds(*CHUNKS[k])
        wires.send_if(cond, lambda: wires.copy(("zo", k), res.at[rows], res.at[rows], to_out))

    def finish(k):
        rows = pl.ds(*CHUNKS[k])

        @pl.when(inner)
        def _():
            wires.arrived(("zm", k), zz.at[1, rows], to_in)
            res[rows, :] = total(t2[rows, :], zz[1, rows, :])

        send_back(k, jnp.logical_and(inner, not_outer))

    def last(k):
        rows = pl.ds(*CHUNKS[k])

        @pl.when(not_inner)
        def _():
            wires.arrived(("zo", k), res.at[rows], to_in)

        send_back(k, jnp.logical_and(not_inner, not_outer))

    def rows_of(half):
        return slice(half * HALF, (half + 1) * HALF)

    def send_part(g, which):
        q = r if which else 1 - r
        at = GROUPS[g][0][0]
        rows = pl.ds(at, GROUPS[g][-1][0] + GROUPS[g][-1][1] - at)
        wires.copy(("c" + str(which), g), gp.at[q, 1 - c, rows], rc.at[q, rows], to_col).start()

    def weight_down():
        back = gft[...]
        for which in range(2):
            q = r if which else 1 - r
            for k in range(2):
                grad = dot(back, act[q, :, k * D : (k + 1) * D]).astype(BF16)
                for half in range(2):
                    gp[q, half, rows_of(k), :] = grad[rows_of(half), :]
                send_part(k, which)

    def weight_up():
        back = hidden2[...].astype(F32).T.astype(BF16)
        for k in range(2):
            for q in range(2):
                grad = dot(back, gpre[q, :, k * D : (k + 1) * D]).astype(BF16)
                for half in range(2):
                    gp[q, half, rows_of(2 + k), :] = grad[rows_of(half), :]
            send_col(2 + k)

    def weight_proj():
        for q in range(2):
            grad = dot_tn(attended[q], gra[...]).astype(BF16)
            for half in range(2):
                gp[q, half, ROWS_B:ROWS_T, HALF:] = grad[:, rows_of(half)]

    def sums_down():
        dmod[5:6, :] = col_sum(gof[...] * branch_f[...])
        biasg[0:1, :D] = col_sum(gf[...])
        for q in range(2):
            biasg[1:2, q * FFH : (q + 1) * FFH] = col_sum(gpre[q])

    def grad_down():
        for q in range(2):
            gpre[q] = (dot(gf[...], w2[q]) * slope[q]).astype(BF16)

    def grad_middle():
        grad_h2 = dot_nt(gpre[0], w1[0]) + dot_nt(gpre[1], w1[1])
        gh2[...] = grad_h2
        mid = gof[...] + norm_back(grad_h2 * (1.0 + m[4]), normed2[...], inv2[...])
        gm[...] = mid
        gra[...] = (mid * m[2]).astype(BF16)
        gatt[...] = dot_nt(gra[...], wp[...]).astype(BF16)

    def sums_middle():
        dmod[4:5, :] = col_sum(gh2[...] * normed2[...])
        dmod[3:4, :] = col_sum(gh2[...])
        dmod[2:3, :] = col_sum(gm[...] * branch_a[...])
        biasg[2:3, :D] = col_sum(gra[...])

    def attend_back(head):
        q, j = head // 3, head % 3
        query, key, val = parts_of(q, j)
        p = prob[head]
        g = gatt[:, head * HD : (head + 1) * HD]
        grad_prob = dot_nt(g, val)
        delta = jnp.sum(p * grad_prob, axis=-1, keepdims=True)
        gs = (p * (grad_prob - delta) * SCALE).astype(BF16)
        gqk[q, :, j * HD : (j + 1) * HD] = dot(gs, key).astype(BF16)
        gqk[q, :, HALF + j * HD : HALF + (j + 1) * HD] = dot_tn(gs, query).astype(BF16)
        gv[q, :, j * HD : (j + 1) * HD] = dot_tn(p.astype(BF16), g).astype(BF16)

    def grad_first():
        grad_h1 = dot_nt(gqk[0], wa[0]) + dot_nt(gqk[1], wa[1])
        gh1[...] = grad_h1 + dot_nt(gv[0], wb[0, :, :HALF]) + dot_nt(gv[1], wb[1, :, :HALF])

    def grad_input(part):
        rows = slice(part * PART, (part + 1) * PART)
        gin[rows, :] = gm[rows, :] + norm_back(gh1[rows, :] * (1.0 + m[1]), normed1[rows, :], inv1[rows, :])

    @pl.when(first)
    def _():
        weight_down()
        facing(0)
        facing(1)
        grad_down()
        settle(0)
        settle(1)
        weight_up()
        sums_down()
        grad_middle()
        from_col(2)
        from_col(3)
        for head in range(6):
            attend_back(head)
        from_row(0)
        grad_first()
        weight_proj()
        from_row(1)

    @pl.when(second)
    def _():
        gf[...] = (gof[...] * m[5]).astype(BF16)
        grad_down()
        grad_middle()
        for head in range(6):
            attend_back(head)
        grad_first()
        for part in range(PARTS):
            rows = slice(part * PART, (part + 1) * PART)
            grad_input(part)
            gbuf[rows, :] = gin[rows, :].astype(BF16)
            there = pl.ds(part * PART, PART)
            wires.copy(("bwd", part), gbuf.at[there], g2.at[there], to_sec).start()
        settle_sent()
        for side in range(2):
            turn_down(side)
        weight_down()
        weight_up()
        sums_down()
        weight_proj()

    back = hidden1[...].astype(F32).T.astype(BF16)
    for q in range(2):
        grad = dot(back, gqk[q]).astype(BF16)
        for half in range(2):
            gp[q, half, ROWS_A:ROWS_B, :] = grad[rows_of(half), :]
    send_col(4)
    for q in range(2):
        grad = dot(back, gv[q]).astype(BF16)
        for half in range(2):
            gp[q, half, ROWS_B:ROWS_T, :HALF] = grad[rows_of(half), :]

    @pl.when(second)
    def _():
        from_col(0)
        from_col(1)

    sums_middle()
    zero = jnp.zeros((1, HALF), F32)
    for q in range(2):
        bqk, bv = col_sum(gqk[q]), col_sum(gv[q])
        for half in range(2):
            tail = [
                bqk,
                jnp.concatenate([bv, biasg[2:3, rows_of(half)]], axis=1),
                biasg[1:2, q * FFH : q * FFH + D],
                biasg[1:2, q * FFH + D : (q + 1) * FFH],
                jnp.concatenate([biasg[0:1, rows_of(half)], zero], axis=1),
                jnp.zeros((11, D), F32),
            ]
            gp[q, half, ROWS_T:GROWS, :] = jnp.concatenate(tail, axis=0).astype(BF16)
    send_col(5)

    @pl.when(second)
    def _():
        from_col(2)
        from_col(3)
        from_row(0, True)
        from_row(1, True)

    dmod[1:2, :] = col_sum(gh1[...] * normed1[...])
    dmod[0:1, :] = col_sum(gh1[...])
    for half in range(2):
        dm[2 + half, 0:6, :] = dmod[0:6, rows_of(half)]
        dm[2 + half, 6:8, :] = jnp.zeros((2, HALF), F32)
    wires.send("dm", dm.at[2 + 1 - c], dm.at[c], to_col)

    def send_input_grad():
        @pl.when(first)
        def _():
            for part in range(PARTS):
                grad_input(part)

        gint[...] = gin[...].T
        wires.send("gin", gint.at[their_feats], input_grad.at[:, own_lanes], to_col)
        input_grad[:, own_lanes] = gint[own_rows, :]

    pl.when(second)(send_out)

    def pull_part():
        wires.arrived("dm", dm.at[1 - c], to_col)
        dm[c] = dm[2 + c]
        part = jnp.zeros((2, D), F32)
        for i in range(6):
            low = jnp.concatenate([dm[0, i : i + 1, :], dm[1, i : i + 1, :]], axis=0).astype(BF16)
            part += dot(low, ada[i])
        pull[0] = jnp.concatenate([part, jnp.zeros((6, D), F32)], axis=0)
        wires.send("p0", pull.at[0], pull.at[1], to_col)

    def pull_section():
        wires.arrived("p0", pull.at[1], to_col)
        pull[2] = pull[0] + pull[1]
        wires.send("p1", pull.at[2], pull.at[3], to_sec)

    def fill_table():
        wires.arrived("p1", pull.at[3], to_sec)
        v = condb[...]
        sig = 1.0 / (1.0 + jnp.exp(-v))
        grad = (pull[2, 0:2, :] + pull[3, 0:2, :]) * (sig * (1.0 + v * (1.0 - sig)))
        cond_grad[...] = grad

        mods = jnp.concatenate([dm[0, 0:6, :], dm[1, 0:6, :]], axis=1)
        late[me] = jnp.concatenate([grad, mods], axis=0)
        share("t", late)

    def spread_late():
        shared("t", late, True)
        rows = [late[i] for i in range(places)]
        grads = jnp.concatenate([v[0:2] for v in rows], axis=0)
        high = grads.astype(BF16)
        rest = grads - high.astype(F32)
        mid = rest.astype(BF16)
        g3[...] = jnp.concatenate([high.astype(F32), mid.astype(F32), rest - mid.astype(F32)], axis=0).astype(BF16)
        summed = functools.reduce(lambda v, w: v + w, rows)
        for i in range(6):
            adab_sum[i] = summed[2 + i : 3 + i, :HALF] + summed[2 + i : 3 + i, HALF:]
            parts = []
            for v in rows:
                parts += [v[2 + i : 3 + i, :HALF], v[2 + i : 3 + i, HALF:]]
            dm16[i] = jnp.concatenate(parts, axis=0).astype(BF16)

    small = {2: pull_part, 5: pull_section, 9: fill_table}
    def settle_chunks():
        for g, group in enumerate(GROUPS):
            rows = pl.ds(group[0][0], group[-1][0] + group[-1][1] - group[0][0])
            wires.copy(("c0", g), gp.at[1 - r, 1 - c, rows], rc.at[1 - r, rows], to_col).wait_send()
            wires.copy(("c1", g), gp.at[r, 1 - c, rows], rc.at[r, rows], to_col).wait_send()
            for at, size in group:
                chunk = pl.ds(at, size)
                wires.copy(("r", at), t1.at[chunk], rr.at[chunk], to_row).wait_send()

    count = len(CHUNKS)
    for tick in range(count + LAGS[1]):
        if tick < 2:
            from_col(4 + tick)
        if tick == 4:
            send_input_grad()
        for lag, step in ((0, from_row), (LAGS[0], fold), (LAGS[1], finish)):
            if (2 if step is from_row else 0) <= tick - lag < count:
                step(tick - lag)
        if tick in small:
            small[tick]()
    spread_late()
    settle_chunks()
    wires.copy("out", outt.at[their_feats], block_out.at[:, own_lanes], to_col).wait_send()
    for name, src, dst, which in (("fwd", obuf, x2, first), ("bwd", gbuf, g2, second)):

        @pl.when(which)
        def _():
            for part in range(PARTS):
                there = pl.ds(part * PART, PART)
                wires.copy((name, part), src.at[there], dst.at[there], to_sec).wait_send()

    for k in range(count):
        last(k)
    wires.arrived("out", block_out.at[:, their_lanes], to_col)
    wires.arrived("gin", input_grad.at[:, their_lanes], to_col)
    shared("t", late, False)
    wires.settle(wires.take())


def last_kernel(
    res, block_in, grad_in, cond_in, dm16, silu16, adab_in, g3, ids,
    block_out, input_grad, label_out, time_out, ada_out, qkv_out, proj_out, fc1_out, fc2_out,
    cond_out, adab_out, qb_out, pb_out, b1_out, b2_out,
    g_label, g_time, g_ada, g_qkv, g_proj, g_fc1, g_fc2, g_qb, g_pb, g_b1, g_b2, sem,
):
    copies = []

    def move(src, dst):
        copy = pltpu.make_async_copy(src, dst, sem.at[len(copies)])
        copy.start()
        copies.append(copy)

    move(grad_in, input_grad)
    move(block_in, block_out)
    move(cond_in, cond_out)
    move(adab_in, adab_out)
    for k in range(2):
        g_fc2[:, k * D : (k + 1) * D] = res[k * HALF : (k + 1) * HALF, :].astype(F32)
    move(g_fc2, fc2_out)
    for k in range(2):
        g_fc1[:, k * D : (k + 1) * D] = res[(2 + k) * HALF : (3 + k) * HALF, :].astype(F32)
    move(g_fc1, fc1_out)
    for i in range(6):
        g_ada[i] = dot_tn(dm16[i], silu16[...])
    move(g_ada, ada_out)
    count = g3.shape[0] // 3
    for which, held, out in ((0, g_label, label_out), (1, g_time, time_out)):
        one = ids[which][:, :1]
        wide = (count, out.shape[0])
        hot = jnp.where(lax.broadcasted_iota(jnp.int32, wide, 1).astype(F32) == one, 1.0, 0.0).astype(BF16)
        held[...] = dot_tn(jnp.concatenate([hot, hot, hot], axis=0), g3[...])
        move(held, out)
    low = res[ROWS_A:ROWS_B, :].astype(F32)
    g_qkv[0] = low[:, :HALF]
    g_qkv[1] = low[:, HALF:]
    low = res[ROWS_B:ROWS_T, :].astype(F32)
    g_qkv[2] = low[:, :HALF]
    move(g_qkv, qkv_out)
    g_proj[...] = low[:, HALF:]
    move(g_proj, proj_out)
    tail = res[ROWS_T:GROWS, :].astype(F32)
    g_qb[0] = tail[0:1, :HALF]
    g_qb[1] = tail[0:1, HALF:]
    g_qb[2] = tail[1:2, :HALF]
    g_pb[...] = tail[1:2, HALF:]
    g_b1[:, :D] = tail[2:3, :]
    g_b1[:, D:] = tail[3:4, :]
    g_b2[...] = tail[4:5, :HALF]
    for held, out in ((g_qb, qb_out), (g_pb, pb_out), (g_b1, b1_out), (g_b2, b2_out)):
        move(held, out)
    for copy in copies:
        copy.wait()


def on_device(
    latents_in, labels, timesteps, out_grad, label_table, time_table, ada_w, ada_b,
    qkv_w, qkv_b, proj_w, proj_b, fc1_w, fc1_b, fc2_w, fc2_b,
):
    own = latents_in.shape[0] // SEQ
    dp = lax.axis_size("dp")
    places = dp * lax.axis_size("row")
    bits = dp.bit_length() - 1
    latents = places * own
    vmem, hbm = pl.BlockSpec(memory_space=pltpu.VMEM), pl.BlockSpec(memory_space=pltpu.HBM)
    args = (
        latents_in.T,
        labels,
        timesteps,
        out_grad.T,
        label_table,
        time_table,
        jnp.transpose(ada_w[0], (1, 2, 0)),
        jnp.transpose(ada_b, (1, 0, 2)),
        jnp.transpose(qkv_w[0], (1, 0, 2)),
        jnp.transpose(qkv_b, (1, 0, 2)),
        proj_w[0],
        proj_b,
        fc1_w[0],
        fc1_b,
        fc2_w[0].T,
        fc2_b,
    )
    outs = [
        ((GROWS, D), BF16),
        ((HALF, own * SEQ), BF16),
        ((HALF, own * SEQ), F32),
        ((own, D), F32),
        ((6, latents, HALF), BF16),
        ((latents, D), BF16),
        ((6, 1, HALF), F32),
        ((3 * latents, D), BF16),
        ((2, latents, D), F32),
    ]
    scratch = [
        ((6, 1, HALF), F32),
        ((3, HALF, HALF), BF16),
        ((3, 1, HALF), F32),
        ((HALF, HALF), BF16),
        ((1, HALF), F32),
        ((1, FFH), F32),
        ((1, HALF), F32),
        (label_table.shape, BF16),
        (time_table.shape, BF16),
        ((6, HALF, D), BF16),
        ((2, HALF, SEQ), BF16),
        ((2, HALF, SEQ), BF16),
        ((4, 8, HALF), F32),
        ((8, D), F32),
        ((4, 8, D), F32),
        ((2, HALF, D), BF16),
        ((2, D, D), BF16),
        ((2, D, D), BF16),
        ((D, D), BF16),
        ((2, D, FFH), BF16),
        ((2, D, FFH), BF16),
        ((SEQ, D), F32),
        ((SEQ, D), F32),
        ((SEQ, D), BF16),
        ((SEQ, D), BF16),
        ((SEQ, D), BF16),
        ((SEQ, D), BF16),
        ((SEQ, D), F32),
        ((SEQ, 1), F32),
        ((SEQ, 1), F32),
        ((SEQ, D), F32),
        ((SEQ, D), F32),
        ((SEQ, D), F32),
        ((SEQ, D), F32),
        ((SEQ, D), F32),
        ((SEQ, D), F32),
        ((SEQ, D), F32),
        ((SEQ, D), BF16),
        ((SEQ, D), BF16),
        ((2, SEQ, D), BF16),
        ((2, SEQ, HALF), BF16),
        ((6, SEQ, SEQ), F32),
        ((2, SEQ, HALF), BF16),
        ((2, SEQ, FFH), BF16),
        ((2, SEQ, FFH), F32),
        ((SEQ, D), BF16),
        ((D, SEQ), BF16),
        ((2, SEQ, FFH), BF16),
        ((SEQ, D), BF16),
        ((SEQ, D), BF16),
        ((2, SEQ, D), BF16),
        ((2, SEQ, HALF), BF16),
        ((D, SEQ), BF16),
        ((D, SEQ), F32),
        ((2, 2, GROWS, D), BF16),
        ((2, GROWS, D), BF16),
        ((GROWS, D), BF16),
        ((GROWS, D), BF16),
        ((GROWS, D), BF16),
        ((GROWS, D), BF16),
        ((2, GROWS, D), BF16),
        ((8, D), F32),
        ((4, 8, HALF), F32),
        ((4, 8, D), F32),
        ((places, 8, D), F32),
        ((places, 8, D), F32),
        ((own, D), F32),
        ((8, FF), F32),
    ]
    wires = 64 + 2 * len(GROUPS) + 4 * len(CHUNKS) + 2 * places
    made = pl.pallas_call(
        functools.partial(main_kernel, bits, dp),
        out_shape=[jax.ShapeDtypeStruct(s, d) for s, d in outs],
        in_specs=[hbm] * len(args),
        out_specs=[vmem] * len(outs),
        scratch_shapes=[pltpu.SMEM((own,), jnp.int32)] * 2
        + [pltpu.VMEM(s, d) for s, d in scratch]
        + [pltpu.SemaphoreType.DMA((wires,)), pltpu.SemaphoreType.DMA((wires,)), pltpu.SemaphoreType.DMA((16,))],
        compiler_params=pltpu.CompilerParams(
            vmem_limit_bytes=46 * 1024 * 1024, collective_id=0, has_side_effects=True
        ),
    )(*[pltpu.with_memory_space_constraint(a, pltpu.HBM) for a in args])
    big = [
        ((HALF, own * SEQ), BF16),
        ((HALF, own * SEQ), F32),
        (label_table.shape, F32),
        (time_table.shape, F32),
        ((6, HALF, D), F32),
        ((3, HALF, HALF), F32),
        ((HALF, HALF), F32),
        ((HALF, FFH), F32),
        ((HALF, FFH), F32),
    ]
    little = [
        ((own, D), F32),
        ((6, 1, HALF), F32),
        ((3, 1, HALF), F32),
        ((1, HALF), F32),
        ((1, FFH), F32),
        ((1, HALF), F32),
    ]
    (
        block_outs, input_grads, g_label, g_time, g_ada, g_qkv, g_proj, g_fc1, g_fc2,
        cond_grad, g_adab, g_qb, g_pb, g_b1, g_b2,
    ) = pl.pallas_call(
        last_kernel,
        out_shape=[jax.ShapeDtypeStruct(s, d) for s, d in big + little],
        in_specs=[vmem] * len(made),
        out_specs=[hbm] * len(big + little),
        scratch_shapes=[pltpu.VMEM(s, d) for s, d in big[2:] + little[2:]]
        + [pltpu.SemaphoreType.DMA((len(big + little),))],
        compiler_params=pltpu.CompilerParams(vmem_limit_bytes=46 * 1024 * 1024),
    )(*made)
    return (
        block_outs.T[None],
        input_grads.T[None],
        cond_grad,
        g_label,
        g_time,
        jnp.transpose(g_ada, (2, 0, 1))[None],
        jnp.transpose(g_adab, (1, 0, 2)),
        jnp.transpose(g_qkv, (1, 0, 2))[None],
        jnp.transpose(g_qb, (1, 0, 2)),
        g_proj[None],
        g_pb,
        g_fc1[None],
        g_b1,
        g_fc2.T[None],
        g_b2,
    )


def solution(mesh):
    return jax.shard_map(
        on_device,
        mesh=mesh,
        in_specs=(
            P(("dp", "row"), "col"),
            P(("dp", "row")),
            P(("dp", "row")),
            P(("dp", "row"), "col"),
            P(),
            P(),
            P("section", None, None, "col"),
            P("section", None, "col"),
            P("section", "col", None, "row"),
            P("section", None, "row"),
            P("section", "row", "col"),
            P("section", "col"),
            P("section", "col", "row"),
            P("section", "row"),
            P("section", "row", "col"),
            P("section", "col"),
        ),
        out_specs=(
            P("section", ("dp", "row"), "col"),
            P("section", ("dp", "row"), "col"),
            P(("dp", "row"), None),
            P(),
            P(),
            P("section", None, None, "col"),
            P("section", None, "col"),
            P("section", "col", None, "row"),
            P("section", None, "row"),
            P("section", "row", "col"),
            P("section", "col"),
            P("section", "col", "row"),
            P("section", "row"),
            P("section", "row", "col"),
            P("section", "col"),
        ),
        check_vma=False,
    )
```
